128 devices in a mesh: prow: 16 (over y, z), pcol: 8 (over x, core).
Axes of the slice: x: 4, y: 4, z: 4, core: 2. Of those that a mesh axis runs over, the one named last changes fastest.
Arguments:
- front: float32 [8, 16, 16, 8, 128, 128], P(None, 'prow', None, 'pcol'), may hold values from -6 to 6, as said below
- child_blocks: float32 [16384, 128, 128], P(('prow', 'pcol')), may hold values from -3 to 3
- owners: int32 [16384, 1], P(('prow', 'pcol')), may hold values from 0 to 127; in each aligned block of 128 rows (0 to 127, 128 to 255, ...) at most 2 rows name the same one
- slots: int32 [16384], P(('prow', 'pcol')), may hold values from 1 to 127
- pattern: int32 [2, 128], replicated, may hold values 0 or 1
Outputs:
- factored: float32 [8, 16, 16, 8, 128, 128], P(None, 'prow', None, 'pcol')
The draws below stay inside these ranges and needn't reach their ends.
Inputs may be any that keep to these rules, and one draw needn't show every extreme that they name: `front`: in the leading 2 * 256 rows and columns, off-diagonal entries lie within 2 / 512 in magnitude and diagonal entries within 3 to 5. `owners`: among the 128 child blocks of one device no owner is named more than 2 times; some owner is named exactly 2 times. `slots`: slot 0 never occurs.
All inputs are finite; a program needn't handle non-finite values.
Results may differ from the reference program's by a relative error of at most 0.0001.
Values sent between devices are 32-bit elements; how exact they have to be, the bound alone decides.
A program may use at most 192 MiB of HBM per device.

```python
import math
import jax
import jax.numpy as jnp
import numpy as np
from jax import lax

TILE = 128
PANEL = 256
CAP = 2
BR = 8
PROWS = 16
PCOLS = 8
NB = 128
BC = 16
CHILDREN = 128
CHILD_ALL = 16384
DEVICES = 128


def draw_front(key, part):
    key_off, key_diag, key_rest = jax.random.split(key, 3)
    shape = (BR, PROWS, BC, PCOLS, TILE, TILE)
    row_block = lax.broadcasted_iota(jnp.int32, shape, 0) * PROWS + lax.broadcasted_iota(jnp.int32, shape, 1)
    col_block = lax.broadcasted_iota(jnp.int32, shape, 2) * PCOLS + lax.broadcasted_iota(jnp.int32, shape, 3)
    glob_row = row_block * TILE + lax.broadcasted_iota(jnp.int32, shape, 4)
    glob_col = col_block * TILE + lax.broadcasted_iota(jnp.int32, shape, 5)
    lead = 2 * PANEL
    leading = (glob_row < lead) & (glob_col < lead)
    off_part = jax.random.uniform(key_off, shape, jnp.float32, -1.0, 1.0) * (2.0 / lead)
    diag_part = jax.random.uniform(key_diag, shape, jnp.float32, 3.0, 5.0)
    rest = jnp.clip(jax.random.normal(key_rest, shape, jnp.float32), -5.5, 5.5)
    rest = rest * jnp.where(glob_col < lead, 0.5, 1.0)
    inner = jnp.where(glob_row == glob_col, diag_part, off_part)
    return jnp.where(leading, inner, rest).astype(jnp.float32)


def with_ends(values, key, low, largest):
    index_at = [jax.random.randint(jax.random.fold_in(key, axis), (), 0, length) for axis, length in enumerate(values.shape)]
    main_axis = values.shape.index(max(values.shape))
    neighbour = index_at[:main_axis] + [(index_at[main_axis] + 1) % values.shape[main_axis]] + index_at[main_axis + 1:]
    return values.at[tuple(index_at)].set(low).at[tuple(neighbour)].set(largest)


def block_levels(stream_key, dims, shards, low, largest):
    loudness = 1.0
    for dim, parts in shards:
        steps = jax.random.uniform(jax.random.fold_in(jax.random.fold_in(stream_key, 6), dim), (parts,), jnp.float32, low / len(shards), largest / len(shards))
        loudness = loudness * jnp.repeat(jnp.exp(steps), dims[dim] // parts).reshape((-1,) + (1,) * (len(dims) - 1 - dim))
    return loudness


def assign_block(stream_key, own, number, rows, amount, top, bound, slope):
    ranking = jax.random.permutation(stream_key, amount)
    heavy_load, ordinary = shares(amount, rows * top, bound, slope, True), shares(amount, rows * top, bound, slope, False)
    places = jnp.arange(amount)

    def named(tallies, offset_by):
        used = int((tallies > 0).sum())
        fixed = max(1, used // 4)
        passed = fixed + (places - fixed + offset_by * (used - fixed)) % max(1, amount - fixed)
        return jnp.zeros((amount,), jnp.int32).at[ranking[jnp.where(places < fixed, places, passed)]].set(jnp.asarray(tallies, jnp.int32))

    tallies = jnp.where(number % 4 == 0, named(heavy_load, number // 4), named(ordinary, number - number // 4 - 1))
    mixed = jax.random.permutation(jax.random.fold_in(own, 3), amount)
    donor, taker = mixed[0:amount // 2 * 2:2], mixed[1:amount // 2 * 2:2]
    slack = jnp.minimum(tallies[donor] - 1, bound - tallies[taker]) // 2
    slack = jnp.where((donor == ranking[0]) | (taker == ranking[0]) | (tallies[taker] == 0), 0, jnp.maximum(slack, 0))
    passed = jax.random.randint(jax.random.fold_in(own, 4), (amount // 2,), 0, 1 << 20) % (slack + 1)
    tallies = tallies.at[donor].add(-passed).at[taker].add(passed)
    items = jnp.searchsorted(jnp.cumsum(tallies), jnp.arange(rows * top), side="right").astype(jnp.int32)
    grid = items.reshape(top, rows).T
    grid = grid[jax.random.permutation(jax.random.fold_in(own, 1), rows)]
    offset_by = jax.random.randint(jax.random.fold_in(own, 2), (rows, 1), 0, top)
    return jnp.take_along_axis(grid, (jnp.arange(top)[None, :] + offset_by) % top, axis=1)


def shares(number_of, total, limit, skew, full):
    weights = [(1 << 20) // math.isqrt(rank ** skew) + 1 for rank in range(1, number_of + 1)]
    largest = limit if full else min(limit, max(-(-total // number_of), total * weights[0] // sum(weights)))
    least = 1 if total - largest >= number_of - 1 else 0
    holding, surplus = [largest] + [least] * (number_of - 1), total - largest - least * (number_of - 1)
    while surplus > 0:
        movable = [i for i in range(1, number_of) if holding[i] < largest] or [i for i in range(1, number_of) if holding[i] < limit]
        mass, budget = sum([weights[i] for i in movable]), surplus
        for i in movable:
            addition = min(limit - holding[i], max(1, budget * weights[i] // mass), surplus)
            holding[i] = holding[i] + addition
            surplus = surplus - addition
    return np.array(holding)


def normal_values(stream_key, extent, deviation, bound, cuts=(), held_as=jnp.bfloat16):
    values = jax.random.normal(stream_key, extent, jnp.float32) * deviation
    if len(cuts) > 0:
        values = block_levels(stream_key, extent, cuts, -0.22, 0.18) * values
    return jnp.clip(values, min=-bound, max=bound).astype(held_as)


def setup_inputs(seed: int = 0) -> dict:
    arg_keys = jax.random.split(jax.random.key(seed), 6)
    front = draw_front(jax.random.fold_in(arg_keys[5], 71), 0)
    child_blocks = normal_values(arg_keys[1], (CHILD_ALL, TILE, TILE), 0.5, 3.0, ((0, 128),), jnp.float32)
    owners_keys = jax.random.split(jax.random.fold_in(arg_keys[2], 1), CHILD_ALL // CHILDREN)
    owners_turns = jax.random.permutation(jax.random.fold_in(arg_keys[2], 3), CHILD_ALL // CHILDREN)
    owners = jax.vmap(lambda own, number: assign_block(jax.random.fold_in(arg_keys[2], 2), own, number, CHILDREN, DEVICES, 1, CAP, 2))(owners_keys, owners_turns).reshape((CHILD_ALL, 1))
    slots = with_ends(jax.random.randint(arg_keys[3], (CHILD_ALL,), 1, BR * BC), jax.random.fold_in(arg_keys[3], 1), 1, (BR * BC) - 1).astype(jnp.int32)
    pattern = with_ends((jax.random.randint(arg_keys[4], (2, NB), 0, 2) < 1).astype(jnp.int32), jax.random.fold_in(arg_keys[4], 1), 0, 1)
    return dict(front=front, child_blocks=child_blocks, owners=owners, slots=slots, pattern=pattern)


def to_matrix(blocks):
    shape = blocks.shape
    moved = jnp.transpose(blocks, (0, 1, 4, 2, 3, 5))
    return moved.reshape(shape[0] * shape[1] * shape[4], shape[2] * shape[3] * shape[5])

def to_blocks(matrix):
    grouped = matrix.reshape(BR, PROWS, TILE, BC, PCOLS, TILE)
    return jnp.transpose(grouped, (0, 1, 3, 4, 2, 5))

def symmetric_lower(square):
    return jnp.tril(square) + jnp.tril(square, -1).T

def reference(front, child_blocks, owners, slots, pattern):
    owner_ids = owners[:, 0]
    row_owner = owner_ids // PCOLS
    col_owner = owner_ids % PCOLS
    local_row = slots // BC
    local_col = slots % BC
    flat_index = ((local_row * PROWS + row_owner) * BC + local_col) * PCOLS + col_owner
    assembled = front.reshape(-1, TILE, TILE).at[flat_index].add(child_blocks)
    matrix = to_matrix(assembled.reshape(front.shape))
    block_row = jnp.arange(NB * TILE, dtype=jnp.int32) // TILE
    patterns = (pattern[0], jnp.maximum(pattern[0], pattern[1]))
    factors = []
    for panel_idx in range(2):
        start = panel_idx * PANEL
        stop = start + PANEL
        column = matrix[:, start:stop]
        factor = jnp.linalg.cholesky(symmetric_lower(column[start:stop]))
        solved = jax.scipy.linalg.solve_triangular(factor, column.T, lower=True).T
        solved = solved.at[start:stop].set(factor)
        own_rows = (block_row >= 2 * panel_idx) & (block_row < 2 * panel_idx + 2)
        chosen = patterns[panel_idx][block_row].astype(jnp.float32)
        keep_rows = jnp.where(own_rows, 1.0, jnp.where(block_row < 2 * panel_idx, 0.0, chosen))
        lower_rows = solved * keep_rows[:, None]
        tail = lower_rows[stop:]
        matrix = matrix.at[stop:, stop:].add(-jnp.dot(tail, tail.T, precision=lax.Precision.HIGHEST))
        factors.append(lower_rows)
    lead = 2 * PANEL
    result = matrix.at[:, :lead].set(jnp.concatenate(factors, axis=1))
    result = result.at[:lead, lead:].set(0.0)
    return to_blocks(result)
```

```python
import jax
import jax.numpy as jnp
from jax import lax
from jax.experimental import pallas as pl
from jax.experimental.pallas import tpu as pltpu
from jax.sharding import PartitionSpec as P

T = 128
MESH = pl.DeviceIdType.MESH
ANY = pl.ANY
VLIM = 60000 * 1024
HI = lax.Precision.HIGHEST


def spec(space):
    return pl.BlockSpec(memory_space=space)


def pack_kernel(owners, child, send, buf, cnt, isem, osem):
    for g in range(8):
        pltpu.make_async_copy(child.at[pl.ds(g * 16, 16)], buf.at[pl.ds(g * 16, 16)], isem.at[g]).start()

    def zero(i, _):
        cnt[i] = 0
        return 0

    lax.fori_loop(0, 128, zero, 0)
    for g in range(8):
        pltpu.make_async_copy(child.at[pl.ds(g * 16, 16)], buf.at[pl.ds(g * 16, 16)], isem.at[g]).wait()

        def put(i, _):
            o = owners[i]
            k = cnt[o]
            cnt[o] = k + 1
            pltpu.make_async_copy(buf.at[i], send.at[o * 2 + k], osem.at[i]).start()
            return 0

        lax.fori_loop(g * 16, g * 16 + 16, put, 0)

    def fin(i, _):
        pltpu.make_async_copy(buf.at[i], send.at[0], osem.at[i]).wait()
        return 0

    lax.fori_loop(0, 128, fin, 0)


def pack(owners, child):
    return pl.pallas_call(
        pack_kernel,
        out_shape=jax.ShapeDtypeStruct((256, T, T), jnp.float32),
        in_specs=[spec(pltpu.SMEM), spec(ANY)],
        out_specs=spec(ANY),
        scratch_shapes=[
            pltpu.VMEM((128, T, T), jnp.float32),
            pltpu.SMEM((128,), jnp.int32),
            pltpu.SemaphoreType.DMA((8,)),
            pltpu.SemaphoreType.DMA((128,)),
        ],
        compiler_params=pltpu.CompilerParams(vmem_limit_bytes=VLIM),
        cost_estimate=pl.CostEstimate(flops=0, bytes_accessed=2 << 23, transcendentals=0),
        name="pack",
    )(owners, child)


def assemble_kernel(slots, recv, front, out, acc, buf, fsem, rsem, osem):
    for g in range(8):
        pltpu.make_async_copy(front.at[pl.ds(g * 16, 16)], acc.at[pl.ds(g * 16, 16)], fsem.at[g]).start()

    def get(i, _):
        @pl.when(slots[i] != 0)
        def _():
            pltpu.make_async_copy(recv.at[i], buf.at[i], rsem.at[i]).start()

        return 0

    lax.fori_loop(0, 256, get, 0)
    for g in range(8):
        pltpu.make_async_copy(front.at[pl.ds(g * 16, 16)], acc.at[pl.ds(g * 16, 16)], fsem.at[g]).wait()

    def add(i, _):
        s = slots[i]

        @pl.when(s != 0)
        def _():
            pltpu.make_async_copy(recv.at[i], buf.at[i], rsem.at[i]).wait()
            acc[s] = acc[s] + buf[i]

        return 0

    lax.fori_loop(0, 256, add, 0)
    for g in range(8):
        pltpu.make_async_copy(acc.at[pl.ds(g * 16, 16)], out.at[pl.ds(g * 16, 16)], osem.at[g]).start()
    for g in range(8):
        pltpu.make_async_copy(acc.at[pl.ds(g * 16, 16)], out.at[pl.ds(g * 16, 16)], osem.at[g]).wait()


def assemble(slots, recv, front):
    return pl.pallas_call(
        assemble_kernel,
        out_shape=jax.ShapeDtypeStruct((128, T, T), jnp.float32),
        in_specs=[spec(pltpu.SMEM), spec(ANY), spec(ANY)],
        out_specs=spec(ANY),
        scratch_shapes=[
            pltpu.VMEM((128, T, T), jnp.float32),
            pltpu.VMEM((256, T, T), jnp.float32),
            pltpu.SemaphoreType.DMA((8,)),
            pltpu.SemaphoreType.DMA((256,)),
            pltpu.SemaphoreType.DMA((8,)),
        ],
        compiler_params=pltpu.CompilerParams(vmem_limit_bytes=VLIM),
        cost_estimate=pl.CostEstimate(flops=0, bytes_accessed=4 << 23, transcendentals=0),
        name="assemble",
    )(slots, recv, front)


def dot(a, b, ta=0, tb=0):
    dims = (((0 if ta else 1,), (1 if tb else 0,)), ((), ()))
    return lax.dot_general(a, b, dims, precision=HI, preferred_element_type=jnp.float32)


def split(x):
    hi = x.astype(jnp.bfloat16)
    lo = (x - hi.astype(jnp.float32)).astype(jnp.bfloat16)
    return hi, lo


def eliminate(a_ref, b_ref, u_ref, w_ref):
    lane = lax.broadcasted_iota(jnp.int32, (T, T), 1)
    sub = lax.broadcasted_iota(jnp.int32, (T, T), 0)
    lane1 = lax.broadcasted_iota(jnp.int32, (1, T), 1)
    sub1 = lax.broadcasted_iota(jnp.int32, (T, 1), 0)
    b_ref[...] = (lane == sub).astype(jnp.float32)

    def step(k, _):
        row = a_ref[pl.ds(k, 1), :]
        brow = b_ref[pl.ds(k, 1), :]
        mat = a_ref[...]
        d = jnp.sum(jnp.where(lane1 == k, row, 0.0), axis=1, keepdims=True)
        col = jnp.sum(jnp.where(lane == k, mat, 0.0), axis=1, keepdims=True)
        rs = 1.0 / jnp.sqrt(d)
        m = jnp.where(sub1 > k, col * (1.0 / d), 0.0)
        u_ref[pl.ds(k, 1), :] = jnp.where(lane1 >= k, row * rs, 0.0)
        w_ref[pl.ds(k, 1), :] = brow * rs
        a_ref[...] = mat - m * row
        b_ref[...] = b_ref[...] - m * brow
        return 0

    lax.fori_loop(0, T, step, 0)
    return u_ref[...].T, w_ref[...]


def sym_lower(x):
    lane = lax.broadcasted_iota(jnp.int32, (T, T), 1)
    sub = lax.broadcasted_iota(jnp.int32, (T, T), 0)
    return jnp.where(sub >= lane, x, x.T)


def factor256(g00, g10, g11, a_ref, b_ref, u_ref, w_ref):
    a_ref[...] = sym_lower(g00)
    l00, w00 = eliminate(a_ref, b_ref, u_ref, w_ref)
    l10 = dot(g10, w00, tb=1)
    a_ref[...] = sym_lower(g11 - dot(l10, l10, tb=1))
    l11, w11 = eliminate(a_ref, b_ref, u_ref, w_ref)
    w10 = -dot(w11, dot(l10, w00))
    zero = jnp.zeros((T, T), jnp.float32)
    low = jnp.concatenate([jnp.concatenate([l00, zero], 1), jnp.concatenate([l10, l11], 1)], 0)
    inv = jnp.concatenate([jnp.concatenate([w00, zero], 1), jnp.concatenate([w10, w11], 1)], 0)
    return low, inv


def lead_factor(pat, blk, q_ref, thi, tlo, phi, plo, a_ref, b_ref, u_ref, w_ref):
    low0, inv0 = factor256(blk(0, 0), blk(1, 0), blk(1, 1), a_ref, b_ref, u_ref, w_ref)
    rect = jnp.concatenate(
        [jnp.concatenate([blk(2, 0), blk(2, 1)], 1), jnp.concatenate([blk(3, 0), blk(3, 1)], 1)], 0
    )
    s = dot(rect, inv0, tb=1)
    e2 = pat[0, 2].astype(jnp.float32)
    e3 = pat[0, 3].astype(jnp.float32)
    s = jnp.concatenate([s[:T] * e2, s[T:] * e3], 0)
    ss = dot(s, s, tb=1)
    low1, inv1 = factor256(
        blk(2, 2) - ss[:T, :T], blk(3, 2) - ss[T:, :T], blk(3, 3) - ss[T:, T:], a_ref, b_ref, u_ref, w_ref
    )
    zero = jnp.zeros((256, 256), jnp.float32)
    q_ref[0:256, 0:256] = low0
    q_ref[0:256, 256:512] = zero
    q_ref[256:512, 0:256] = s
    q_ref[256:512, 256:512] = low1
    t01 = -dot(inv0, dot(s, inv1, ta=1, tb=1), ta=1)
    t = jnp.concatenate(
        [jnp.concatenate([inv0.T, t01], 1), jnp.concatenate([zero, inv1.T], 1)], 0
    )
    p = dot(t, t, tb=1)
    hi, lo = split(t)
    thi[...] = hi
    tlo[...] = lo
    hi, lo = split(p)
    phi[...] = hi
    plo[...] = lo


LOWER = [(i, j) for i in range(4) for j in range(i + 1)]


def factor_kernel(pat, lead, q_ref, thi, tlo, phi, plo, a_ref, b_ref, u_ref, w_ref):
    def blk(i, j):
        return lead[LOWER.index((i, j))]

    lead_factor(pat, blk, q_ref, thi, tlo, phi, plo, a_ref, b_ref, u_ref, w_ref)


def factor(pattern, lead):
    vm = spec(pltpu.VMEM)
    bf = jax.ShapeDtypeStruct((512, 512), jnp.bfloat16)
    return pl.pallas_call(
        factor_kernel,
        out_shape=(jax.ShapeDtypeStruct((512, 512), jnp.float32), bf, bf, bf, bf),
        in_specs=[spec(pltpu.SMEM), vm],
        out_specs=(vm,) * 5,
        scratch_shapes=[pltpu.VMEM((T, T), jnp.float32)] * 4,
        compiler_params=pltpu.CompilerParams(vmem_limit_bytes=VLIM),
        cost_estimate=pl.CostEstimate(flops=1 << 31, bytes_accessed=1 << 24, transcendentals=0),
        name="factor",
    )(pattern, lead)


def panel_kernel(asm, rows, cols, lsem, ssem_sc, rsem_sc, s1s, s1r, s2s, s2r, fs, fr, rs_s, rs_r, pt_s, pt_r):
    r = lax.axis_index("prow")
    c = lax.axis_index("pcol")
    y, z, x, k = r // 4, r % 4, c // 2, c % 2
    tc = r % 8
    half = r // 8
    selfhit = (c < 4) & (tc == c)
    bar = pltpu.get_barrier_semaphore()

    def sig(rr, cc):
        pl.semaphore_signal(bar, inc=1, device_id=(rr, cc), device_id_type=MESH)

    def zn(d):
        return y * 4 + (z + d) % 4

    def yn(d):
        return ((y + d) % 4) * 4 + z

    def xn(d):
        return ((x + d) % 4) * 2 + k

    for q in range(16):
        @pl.when((c < 4) & jnp.logical_not((tc == c) & (r == q)))
        def _():
            sig(q, tc)
    for h in range(2):
        for cc in range(4):
            @pl.when(jnp.logical_not((r == c + 8 * h) & (c == cc)))
            def _():
                sig(c + 8 * h, cc)
    for d in (1, 2, 3):
        sig(zn(d), c)
        sig(yn(d), c)
    sig(r, xn(1))
    sig(r, xn(3))
    sig(r, x * 2 + 1 - k)
    n_sc = jnp.where(c < 4, 16, 0) + 8 - jnp.where(selfhit, 2, 0)
    pl.semaphore_wait(bar, n_sc + 9)

    def rcopy(src, dst, ss, rs, dev):
        return pltpu.make_async_remote_copy(
            src_ref=src, dst_ref=dst, send_sem=ss, recv_sem=rs, device_id=dev, device_id_type=MESH
        )

    def sc_dst(h, q, cc):
        return cols.at[h, pl.ds(q * 64, 64), pl.ds(cc * T, T)]

    def sc_copy(q):
        src = asm.at[q // 2, 0, pl.ds((q % 2) * 64, 64), :]
        return src, sc_dst(half, q, c), rsem_sc.at[half * 4 + c]

    own = asm.at[:, 0]

    def rowcol(cc):
        return rows.at[:, :, pl.ds(pl.multiple_of(cc * T, T), T)]

    @pl.when(c < 4)
    def _():
        for q in range(16):
            src, dst, rsem = sc_copy(q)
            hit = (tc == c) & (r == q)

            @pl.when(hit)
            def _():
                pltpu.make_async_copy(src, dst, rsem).start()

            @pl.when(jnp.logical_not(hit))
            def _():
                rcopy(src, dst, ssem_sc.at[q], rsem, (q, tc)).start()

        pltpu.make_async_copy(own, rowcol(c), lsem).start()

    for e in range(2):
        @pl.when(x == e)
        def _():
            rcopy(own, rowcol(c), rs_s.at[0], rs_r.at[e], (r, xn(1))).start()
            rcopy(own, rowcol(c), rs_s.at[1], rs_r.at[e], (r, xn(3))).start()

    def slab(h, q):
        return cols.at[h, pl.ds(q * 64, 64), :]

    for h in range(2):
        nb = zn if h == 0 else yn
        for cc in range(4):
            piece = sc_dst(h, r, cc)
            pltpu.make_async_copy(piece, piece, rsem_sc.at[h * 4 + cc]).wait()
        for d in (1, 3, 2):
            rcopy(slab(h, r), slab(h, r), s1s.at[h, d], s1r.at[h, d], (nb(d), c)).start()

    part = (r, x * 2 + 1 - k)
    for e in range(2):
        item = rowcol(2 * e + k)

        @pl.when(x != e)
        def _():
            rcopy(item, item, rs_s.at[2], rs_r.at[e], part).wait_recv()

        @pl.when(x == 3 - e)
        def _():
            rcopy(item, item, rs_s.at[2], rs_r.at[e], (r, (2 + e) * 2 + k)).start()

        @pl.when(x == e)
        def _():
            pltpu.make_async_copy(own, rowcol(c), lsem).wait()

        rcopy(item, item, pt_s.at[e], pt_r.at[e], part).start()

    def line(h, p, j):
        if h == 0:
            return slab(0, ((y + p) % 4) * 4 + j)
        return slab(1, j * 4 + (z + p) % 4)

    for h in range(2):
        nb1 = zn if h == 0 else yn
        nb2 = yn if h == 0 else zn
        for d in (1, 3, 2):
            got = slab(h, nb1(-d))
            rcopy(got, got, s1s.at[h, d], s1r.at[h, d], part).wait_recv()
        for j in range(4):
            jp, jm = j, (j + 2) % 4
            for dirn, jj in ((0, jp), (1, jm)):
                sl = line(h, 0, jj)
                dev = (nb2(1 if dirn == 0 else 3), c)
                rcopy(sl, sl, s2s.at[h, dirn, jj], s2r.at[h, dirn, jj], dev).start()
    for i in range(2):
        for h in range(2):
            nb2 = yn if h == 0 else zn
            sl = line(h, 3, i)
            rcopy(sl, sl, s2s.at[h, 0, i], s2r.at[h, 0, i], part).wait_recv()
            rcopy(sl, sl, fs.at[h, 0, i], fr.at[h, 0, i], (nb2(1), c)).start()
            sl = line(h, 1, 2 + i)
            rcopy(sl, sl, s2s.at[h, 1, 2 + i], s2r.at[h, 1, 2 + i], part).wait_recv()
            rcopy(sl, sl, fs.at[h, 1, i], fr.at[h, 1, i], (nb2(3), c)).start()
    for h in range(2):
        for i in range(2):
            sl = line(h, 3, 2 + i)
            rcopy(sl, sl, s2s.at[h, 0, 2 + i], s2r.at[h, 0, 2 + i], part).wait_recv()
            sl = line(h, 1, i)
            rcopy(sl, sl, s2s.at[h, 1, i], s2r.at[h, 1, i], part).wait_recv()
            sl = line(h, 2, i)
            rcopy(sl, sl, fs.at[h, 0, i], fr.at[h, 0, i], part).wait_recv()
            sl = line(h, 2, 2 + i)
            rcopy(sl, sl, fs.at[h, 1, i], fr.at[h, 1, i], part).wait_recv()
    for e in range(2):
        item = rowcol(2 * e + 1 - k)
        rcopy(item, item, pt_s.at[e], pt_r.at[e], part).wait_recv()
    sl = slab(0, r)
    for h in range(2):
        for d in (1, 2, 3):
            rcopy(sl, sl, s1s.at[h, d], s1r.at[h, d], part).wait_send()
        for dirn in range(2):
            for j in range(4):
                rcopy(sl, sl, s2s.at[h, dirn, j], s2r.at[h, dirn, j], part).wait_send()
            for i in range(2):
                rcopy(sl, sl, fs.at[h, dirn, i], fr.at[h, dirn, i], part).wait_send()
    item = rowcol(k)
    for e in range(2):
        rcopy(item, item, pt_s.at[e], pt_r.at[e], part).wait_send()

    @pl.when(x < 2)
    def _():
        rcopy(item, item, rs_s.at[0], rs_r.at[0], part).wait_send()
        rcopy(item, item, rs_s.at[1], rs_r.at[0], part).wait_send()

    @pl.when(x >= 2)
    def _():
        rcopy(item, item, rs_s.at[2], rs_r.at[0], part).wait_send()

    @pl.when(c < 4)
    def _():
        for q in range(16):
            @pl.when(jnp.logical_not((tc == c) & (r == q)))
            def _():
                src, dst, rsem = sc_copy(q)
                rcopy(src, dst, ssem_sc.at[q], rsem, part).wait_send()


def panel(asm):
    dma = pltpu.SemaphoreType.DMA
    return pl.pallas_call(
        panel_kernel,
        out_shape=(
            jax.ShapeDtypeStruct((8, T, 512), jnp.float32),
            jax.ShapeDtypeStruct((2, 1024, 512), jnp.float32),
        ),
        in_specs=[spec(ANY)],
        out_specs=(spec(ANY), spec(ANY)),
        scratch_shapes=[
            dma(()),
            dma((16,)),
            dma((8,)),
            dma((2, 4)),
            dma((2, 4)),
            dma((2, 2, 4)),
            dma((2, 2, 4)),
            dma((2, 2, 2)),
            dma((2, 2, 2)),
            dma((3,)),
            dma((2,)),
            dma((2,)),
            dma((2,)),
        ],
        compiler_params=pltpu.CompilerParams(collective_id=1, has_side_effects=True, vmem_limit_bytes=VLIM),
        cost_estimate=pl.CostEstimate(flops=0, bytes_accessed=1 << 26, transcendentals=0),
        name="panel",
    )(asm)


def schur_kernel(pat, rows, cols, acc, phi, plo, thi, tlo, q_ref, out, yext, cext, qbuf):
    r = lax.axis_index("prow")
    c = lax.axis_index("pcol")
    s = pl.program_id(0)
    f32 = jnp.float32

    def masks(i):
        e0 = pat[0, i].astype(f32)
        e1 = jnp.maximum(pat[0, i], pat[1, i]).astype(f32)
        return e0, e1

    def mm(a, b):
        return jnp.dot(a, b, preferred_element_type=f32)

    def masked(x, e):
        return jnp.concatenate([x[:, :256] * e[0], x[:, 256:] * e[1]], axis=1)

    @pl.when(s == 0)
    def _():
        off = pl.multiple_of(jnp.minimum(c, 3) * T, T)

        def row(a, _):
            hi, lo = split(masked(rows[a], masks(a * 16 + r)))
            y = mm(hi, phi[...]) + mm(lo, phi[...]) + mm(hi, plo[...])
            yh, yl = split(y)
            at = pl.ds(pl.multiple_of(a * T, T), T)
            yext[at, 0:512] = yh
            yext[at, 512:1024] = yh
            yext[at, 1024:1536] = yl

            @pl.when(c < 4)
            def _():
                th = thi[:, pl.ds(off, T)]
                qbuf[a] = mm(hi, th) + mm(lo, th) + mm(hi, tlo[:, pl.ds(off, T)])

            return 0

        lax.fori_loop(0, 8, row, 0)

        @pl.when((c < 4) & (r < 4))
        def _():
            qbuf[0] = q_ref[pl.ds(pl.multiple_of(jnp.minimum(r, 3) * T, T), T), pl.ds(off, T)]

    for h in range(2):
        hi, lo = split(masked(cols[h], masks(s * 16 + h * 8 + c)))
        cext[h * T : (h + 1) * T, 0:512] = hi
        cext[h * T : (h + 1) * T, 512:1024] = lo
        cext[h * T : (h + 1) * T, 1024:1536] = hi
    ce = cext[...]

    def body(a, _):
        at = pl.ds(pl.multiple_of(a * T, T), T)
        upd = lax.dot_general(yext[at, :], ce, (((1,), (1,)), ((), ())), preferred_element_type=f32)
        keep = jnp.where((a * 16 + r) < 4, 0.0, 1.0)
        for h in range(2):
            m = acc[a, 0, h, 0]
            val = m - upd[:, h * T : (h + 1) * T]
            out[a, 0, h, 0] = jnp.where(keep > 0.0, val, 0.0)
        return 0

    lax.fori_loop(0, 8, body, 0)

    @pl.when((s == 0) & (c < 4))
    def _():
        for a in range(8):
            out[a, 0, 0, 0] = qbuf[a]


def schur(pattern, rows, cols, acc, phi, plo, thi, tlo, qlead):
    full = lambda *shape: pl.BlockSpec(shape, lambda s: (0,) * len(shape))
    blk = pl.BlockSpec((8, 1, 2, 1, T, T), lambda s: (0, 0, s, 0, 0, 0))
    return pl.pallas_call(
        schur_kernel,
        grid=(8,),
        out_shape=jax.ShapeDtypeStruct((8, 1, 16, 1, T, T), jnp.float32),
        in_specs=[
            spec(pltpu.SMEM),
            full(8, T, 512),
            pl.BlockSpec((2, T, 512), lambda s: (0, s, 0)),
            blk,
            full(512, 512),
            full(512, 512),
            full(512, 512),
            full(512, 512),
            full(512, 512),
        ],
        out_specs=blk,
        scratch_shapes=[
            pltpu.VMEM((1024, 1536), jnp.bfloat16),
            pltpu.VMEM((256, 1536), jnp.bfloat16),
            pltpu.VMEM((8, T, T), jnp.float32),
        ],
        compiler_params=pltpu.CompilerParams(vmem_limit_bytes=VLIM),
        cost_estimate=pl.CostEstimate(flops=7 << 30, bytes_accessed=6 << 22, transcendentals=0),
        name="schur",
    )(pattern, rows, cols, acc, phi, plo, thi, tlo, qlead)


def local(front, child_blocks, owners, slots, pattern):
    r = lax.axis_index("prow")
    c = lax.axis_index("pcol")
    me = r * 8 + c
    owner = owners[:, 0]
    meta_all = lax.all_gather(owner * 128 + slots, ("prow", "pcol"), tiled=False)
    ri = jnp.array([i for i, _ in LOWER], jnp.int32)
    ci = jnp.array([j for _, j in LOWER], jnp.int32)
    pick = (ri == r) & (ci == c)
    lead = lax.psum(
        jnp.where(pick[:, None, None], front[0, 0, 0, 0][None], 0.0), ("prow", "pcol")
    )
    send = pack(owner, child_blocks)
    got = lax.all_to_all(
        send.reshape(128, 2, T, T), ("prow", "pcol"), split_axis=0, concat_axis=0, tiled=True
    ).reshape(256, T, T)
    qlead, thi, tlo, phi, plo = factor(pattern, lead)
    mine = (meta_all // 128) == me
    idx = lax.broadcasted_iota(jnp.int32, (128, 128), 1)
    first = jnp.min(jnp.where(mine, idx, 128), axis=1)
    last = jnp.max(jnp.where(mine, idx, -1), axis=1)
    sl = meta_all % 128
    s0 = jnp.sum(jnp.where(mine & (idx == first[:, None]), sl, 0), axis=1)
    s1 = jnp.sum(jnp.where(mine & (idx == last[:, None]) & (idx > first[:, None]), sl, 0), axis=1)
    got_slots = jnp.stack([s0, s1], axis=1).reshape(256)
    asm = assemble(got_slots, got, front.reshape(128, T, T))
    rows, cols = panel(asm.reshape(8, 16, T, T))
    return schur(
        pattern, rows, cols, asm.reshape(8, 1, 16, 1, T, T), phi, plo, thi, tlo, qlead
    )


def solution(mesh):
    placed = (
        P(None, "prow", None, "pcol", None, None),
        P(("prow", "pcol"), None, None),
        P(("prow", "pcol"), None),
        P(("prow", "pcol")),
        P(),
    )
    return jax.shard_map(
        local,
        mesh=mesh,
        in_specs=placed,
        out_specs=P(None, "prow", None, "pcol", None, None),
        check_vma=False,
    )
```

```python
import jax
import jax.numpy as jnp
from jax import lax
from jax.experimental import pallas as pl
from jax.experimental.pallas import tpu as pltpu
from jax.sharding import PartitionSpec as P

T = 128
MESH = pl.DeviceIdType.MESH
ANY = pl.ANY
VLIM = 60000 * 1024
HI = lax.Precision.HIGHEST


def spec(space):
    return pl.BlockSpec(memory_space=space)


def pack_kernel(owners, owners_v, slots_v, child, send, meta, buf, cnt, isem, osem):
    for g in range(8):
        pltpu.make_async_copy(child.at[pl.ds(g * 16, 16)], buf.at[pl.ds(g * 16, 16)], isem.at[g]).start()
    meta[...] = owners_v[...] * 128 + slots_v[...]

    def zero(i, _):
        cnt[i] = 0
        return 0

    lax.fori_loop(0, 128, zero, 0)
    for g in range(8):
        pltpu.make_async_copy(child.at[pl.ds(g * 16, 16)], buf.at[pl.ds(g * 16, 16)], isem.at[g]).wait()

        def put(i, _):
            o = owners[i]
            k = cnt[o]
            cnt[o] = k + 1
            pltpu.make_async_copy(buf.at[i], send.at[o, k], osem.at[i]).start()
            return 0

        lax.fori_loop(g * 16, g * 16 + 16, put, 0)

    def fin(i, _):
        pltpu.make_async_copy(buf.at[i], send.at[0, 0], osem.at[i]).wait()
        return 0

    lax.fori_loop(0, 128, fin, 0)


def pack(owners, slots, child):
    return pl.pallas_call(
        pack_kernel,
        out_shape=(
            jax.ShapeDtypeStruct((128, 2, T, T), jnp.float32),
            jax.ShapeDtypeStruct((1, 128), jnp.int32),
        ),
        in_specs=[spec(pltpu.SMEM), spec(pltpu.VMEM), spec(pltpu.VMEM), spec(ANY)],
        out_specs=(spec(ANY), spec(pltpu.VMEM)),
        scratch_shapes=[
            pltpu.VMEM((128, T, T), jnp.float32),
            pltpu.SMEM((128,), jnp.int32),
            pltpu.SemaphoreType.DMA((8,)),
            pltpu.SemaphoreType.DMA((128,)),
        ],
        compiler_params=pltpu.CompilerParams(vmem_limit_bytes=VLIM),
        cost_estimate=pl.CostEstimate(flops=0, bytes_accessed=2 << 23, transcendentals=0),
        name="pack",
    )(owners, owners.reshape(1, 128), slots.reshape(1, 128), child)


def assemble_kernel(slots, recv, front, out, acc, buf, fsem, rsem, osem):
    for g in range(8):
        pltpu.make_async_copy(front.at[pl.ds(g * 16, 16)], acc.at[pl.ds(g * 16, 16)], fsem.at[g]).start()

    def get(i, _):
        @pl.when(slots[i % 2, i // 2] != 0)
        def _():
            pltpu.make_async_copy(recv.at[i // 2, i % 2], buf.at[i], rsem.at[i]).start()

        return 0

    lax.fori_loop(0, 256, get, 0)
    for g in range(8):
        pltpu.make_async_copy(front.at[pl.ds(g * 16, 16)], acc.at[pl.ds(g * 16, 16)], fsem.at[g]).wait()

    def add(i, _):
        s = slots[i % 2, i // 2]

        @pl.when(s != 0)
        def _():
            pltpu.make_async_copy(recv.at[i // 2, i % 2], buf.at[i], rsem.at[i]).wait()
            acc[s] = acc[s] + buf[i]

        return 0

    lax.fori_loop(0, 256, add, 0)
    for g in range(8):
        pltpu.make_async_copy(acc.at[pl.ds(g * 16, 16)], out.at[pl.ds(g * 16, 16)], osem.at[g]).start()
    for g in range(8):
        pltpu.make_async_copy(acc.at[pl.ds(g * 16, 16)], out.at[pl.ds(g * 16, 16)], osem.at[g]).wait()


def assemble(slots, recv, front):
    return pl.pallas_call(
        assemble_kernel,
        out_shape=jax.ShapeDtypeStruct((128, T, T), jnp.float32),
        in_specs=[spec(pltpu.SMEM), spec(ANY), spec(ANY)],
        out_specs=spec(ANY),
        scratch_shapes=[
            pltpu.VMEM((128, T, T), jnp.float32),
            pltpu.VMEM((256, T, T), jnp.float32),
            pltpu.SemaphoreType.DMA((8,)),
            pltpu.SemaphoreType.DMA((256,)),
            pltpu.SemaphoreType.DMA((8,)),
        ],
        compiler_params=pltpu.CompilerParams(vmem_limit_bytes=VLIM),
        cost_estimate=pl.CostEstimate(flops=0, bytes_accessed=4 << 23, transcendentals=0),
        name="assemble",
    )(slots, recv, front)


def dot(a, b, ta=0, tb=0):
    dims = (((0 if ta else 1,), (1 if tb else 0,)), ((), ()))
    return lax.dot_general(a, b, dims, precision=HI, preferred_element_type=jnp.float32)


def split(x):
    hi = x.astype(jnp.bfloat16)
    lo = (x - hi.astype(jnp.float32)).astype(jnp.bfloat16)
    return hi, lo


def eliminate(a_ref, b_ref, u_ref, w_ref):
    lane = lax.broadcasted_iota(jnp.int32, (T, T), 1)
    sub = lax.broadcasted_iota(jnp.int32, (T, T), 0)
    lane1 = lax.broadcasted_iota(jnp.int32, (1, T), 1)
    sub1 = lax.broadcasted_iota(jnp.int32, (T, 1), 0)
    b_ref[...] = (lane == sub).astype(jnp.float32)

    def step(k, _):
        row = a_ref[pl.ds(k, 1), :]
        brow = b_ref[pl.ds(k, 1), :]
        mat = a_ref[...]
        d = jnp.sum(jnp.where(lane1 == k, row, 0.0), axis=1, keepdims=True)
        col = jnp.sum(jnp.where(lane == k, mat, 0.0), axis=1, keepdims=True)
        rs = 1.0 / jnp.sqrt(d)
        m = jnp.where(sub1 > k, col * (1.0 / d), 0.0)
        u_ref[pl.ds(k, 1), :] = jnp.where(lane1 >= k, row * rs, 0.0)
        w_ref[pl.ds(k, 1), :] = brow * rs
        a_ref[...] = mat - m * row
        b_ref[...] = b_ref[...] - m * brow
        return 0

    lax.fori_loop(0, T, step, 0)
    return u_ref[...].T, w_ref[...]


def sym_lower(x):
    lane = lax.broadcasted_iota(jnp.int32, (T, T), 1)
    sub = lax.broadcasted_iota(jnp.int32, (T, T), 0)
    return jnp.where(sub >= lane, x, x.T)


def factor256(g00, g10, g11, a_ref, b_ref, u_ref, w_ref, hook):
    a_ref[...] = sym_lower(g00)
    l00, w00 = eliminate(a_ref, b_ref, u_ref, w_ref)
    hook()
    l10 = dot(g10, w00, tb=1)
    a_ref[...] = sym_lower(g11 - dot(l10, l10, tb=1))
    l11, w11 = eliminate(a_ref, b_ref, u_ref, w_ref)
    hook()
    w10 = -dot(w11, dot(l10, w00))
    zero = jnp.zeros((T, T), jnp.float32)
    low = jnp.concatenate([jnp.concatenate([l00, zero], 1), jnp.concatenate([l10, l11], 1)], 0)
    inv = jnp.concatenate([jnp.concatenate([w00, zero], 1), jnp.concatenate([w10, w11], 1)], 0)
    return low, inv


def lead_factor(pat, blk, q_ref, thi, tlo, phi, plo, a_ref, b_ref, u_ref, w_ref, hook):
    low0, inv0 = factor256(blk(0, 0), blk(1, 0), blk(1, 1), a_ref, b_ref, u_ref, w_ref, hook)
    rect = jnp.concatenate(
        [jnp.concatenate([blk(2, 0), blk(2, 1)], 1), jnp.concatenate([blk(3, 0), blk(3, 1)], 1)], 0
    )
    s = dot(rect, inv0, tb=1)
    e2 = pat[0, 2].astype(jnp.float32)
    e3 = pat[0, 3].astype(jnp.float32)
    s = jnp.concatenate([s[:T] * e2, s[T:] * e3], 0)
    ss = dot(s, s, tb=1)
    low1, inv1 = factor256(
        blk(2, 2) - ss[:T, :T], blk(3, 2) - ss[T:, :T], blk(3, 3) - ss[T:, T:], a_ref, b_ref, u_ref, w_ref, hook
    )
    zero = jnp.zeros((256, 256), jnp.float32)
    q_ref[0:256, 0:256] = low0
    q_ref[0:256, 256:512] = zero
    q_ref[256:512, 0:256] = s
    q_ref[256:512, 256:512] = low1
    t01 = -dot(inv0, dot(s, inv1, ta=1, tb=1), ta=1)
    t = jnp.concatenate(
        [jnp.concatenate([inv0.T, t01], 1), jnp.concatenate([zero, inv1.T], 1)], 0
    )
    p = dot(t, t, tb=1)
    hi, lo = split(t)
    thi[...] = hi
    tlo[...] = lo
    hi, lo = split(p)
    phi[...] = hi
    plo[...] = lo


LAG = 3
STEP = 8
NBATCH = 16


def exchange_kernel(
    pat, meta, send, front, recv, relay, slots, q_ref, thi, tlo, phi, plo,
    lead, meta_all, a_ref, b_ref, u_ref, w_ref,
    lsem, msem, mssem, ss, rs, rss, rrs, fss, frs, l0, l1s, l1r, l2s, l2r, l4s, l4r, l5s, l5r,
):
    r = lax.axis_index("prow")
    c = lax.axis_index("pcol")
    y, z, x, k = r // 4, r % 4, c // 2, c % 2
    me = r * 8 + c
    part = (r, x * 2 + 1 - k)
    bar = pltpu.get_barrier_semaphore()

    def rcopy(src, dst, s_sem, r_sem, dev):
        return pltpu.make_async_remote_copy(
            src_ref=src, dst_ref=dst, send_sem=s_sem, recv_sem=r_sem, device_id=dev, device_id_type=MESH
        )

    def steps(t):
        return (t // 2) % 4, t // 32, (t // 8) % 4

    def target(t):
        dx, dy, dz = steps(t)
        return ((y + dy) % 4) * 4 + (z + dz) % 4, ((x + dx) % 4) * 2 + (k + t) % 2

    def two(d):
        return jnp.where(d == 2, 1, 0)

    def is_tie(t):
        dx, dy, dz = steps(t)
        return (two(dx) + two(dy) + two(dz)) > 0

    def sig(i, _):
        pl.semaphore_signal(bar, inc=1, device_id=target(i), device_id_type=MESH)
        return 0

    lax.fori_loop(1, 128, sig, 0)
    pl.semaphore_wait(bar, 127)

    def issue(b):
        def one(i, _):
            t = (i * 37) % 128
            dr, dc = target(t)
            d = dr * 8 + dc
            dx, dy, dz = steps(t)
            tie = is_tie(t)

            @pl.when(tie)
            def _():
                ir = ((y + 3 * two(dy)) % 4) * 4 + (z + 3 * two(dz)) % 4
                ic = ((x + 3 * two(dx)) % 4) * 2 + k
                rcopy(send.at[d, 1], relay.at[t], rss.at[t], rrs.at[t], (ir, ic)).start()
                rcopy(send.at[d, 0], recv.at[me, 0], ss.at[t], rs.at[t], (dr, dc)).start()

            @pl.when(jnp.logical_not(tie))
            def _():
                rcopy(send.at[d], recv.at[me], ss.at[t], rs.at[t], (dr, dc)).start()

            return 0

        lax.fori_loop(max(b * STEP, 1), b * STEP + STEP, one, 0)

    def forward(b):
        def one(i, _):
            t = (i * 37) % 128

            @pl.when(is_tie(t))
            def _():
                dx, dy, dz = steps(t)
                sy, sz, sx = (y + two(dy)) % 4, (z + two(dz)) % 4, (x + two(dx)) % 4
                src = (sy * 4 + sz) * 8 + sx * 2 + k
                dr = ((sy + dy) % 4) * 4 + (sz + dz) % 4
                dc = ((sx + dx) % 4) * 2 + (k + t) % 2
                rcopy(send.at[0, 1], relay.at[t], rss.at[t], rrs.at[t], part).wait_recv()
                rcopy(relay.at[t], recv.at[src, 1], fss.at[t], frs.at[t], (dr, dc)).start()

            return 0

        lax.fori_loop(max(b * STEP, 1), b * STEP + STEP, one, 0)

    state = [0]

    def go(n=1):
        for _ in range(n):
            b = state[0]
            state[0] = b + 1
            if b < NBATCH:
                issue(b)
            if LAG <= b < NBATCH + LAG:
                forward(b - LAG)

    def cset(j):
        return lead.at[j, pl.ds(j, 4 - j)]

    for j in range(4):
        @pl.when((y == 0) & (c == j) & (z >= j))
        def _():
            cp = pltpu.make_async_copy(front.at[0], lead.at[j, z], l0)
            cp.start()
            cp.wait()
            for d in (1, 2, 3):
                rcopy(lead.at[j, z], lead.at[j, z], l1s.at[d], l1r.at[z], ((z + d) % 4, c)).start()

    pltpu.make_async_copy(send.at[me], recv.at[me], lsem).start()
    mrow = meta_all.at[pl.ds(me, 1), :]
    pltpu.make_async_copy(meta, mrow, msem).start()

    def tell(i, _):
        rcopy(meta, mrow, mssem.at[i], msem, target(i)).start()
        return 0

    lax.fori_loop(1, 128, tell, 0)
    go()
    for j in range(4):
        e = j // 2

        @pl.when((y == 0) & (c == j))
        def _():
            for i in range(j, 4):
                @pl.when(z != i)
                def _():
                    rcopy(lead.at[j, i], lead.at[j, i], l1s.at[0], l1r.at[i], part).wait_recv()

            rcopy(cset(j), cset(j), l2s.at[0], l2r.at[e], (r, ((x + 1) % 4) * 2 + k)).start()
            rcopy(cset(j), cset(j), l2s.at[1], l2r.at[e], (r, ((x + 3) % 4) * 2 + k)).start()

    go()
    for j in range(4):
        e = j // 2

        @pl.when((y == 0) & (k == j % 2) & ((x == (e + 1) % 4) | (x == (e + 3) % 4)))
        def _():
            rcopy(cset(j), cset(j), l2s.at[2], l2r.at[e], part).wait_recv()

        @pl.when((y == 0) & (k == j % 2) & (x == 3 - e))
        def _():
            rcopy(cset(j), cset(j), l2s.at[2], l2r.at[e], (r, (2 + e) * 2 + k)).start()

    go()
    for j in range(4):
        e = j // 2

        @pl.when((y == 0) & (k == j % 2) & (x == 2 + e))
        def _():
            rcopy(cset(j), cset(j), l2s.at[2], l2r.at[e], part).wait_recv()

        @pl.when((y == 0) & (k == j % 2))
        def _():
            for d in (1, 3, 2):
                rcopy(cset(j), cset(j), l4s.at[e, d], l4r.at[e], (d * 4 + z, c)).start()

    go()
    for j in range(4):
        e = j // 2

        @pl.when((y != 0) & (k == j % 2))
        def _():
            rcopy(cset(j), cset(j), l4s.at[e, 0], l4r.at[e], part).wait_recv()

        @pl.when(k == j % 2)
        def _():
            rcopy(cset(j), cset(j), l5s.at[e], l5r.at[e], part).start()

    go()
    pltpu.make_async_copy(meta_all, meta_all, msem).wait()
    mt = meta_all[...].astype(jnp.float32).T
    own = jnp.floor(mt * (1.0 / 128.0))
    sl = mt - own * 128.0
    idx = lax.broadcasted_iota(jnp.int32, (128, 128), 0).astype(jnp.float32)
    mine = own == me.astype(jnp.float32)
    first = jnp.min(jnp.where(mine, idx, 999.0), axis=0, keepdims=True)
    last = jnp.max(jnp.where(mine, idx, -1.0), axis=0, keepdims=True)
    s0 = jnp.sum(jnp.where(mine & (idx == first), sl, 0.0), axis=0, keepdims=True)
    s1 = jnp.sum(jnp.where(mine & (idx == last) & (idx > first), sl, 0.0), axis=0, keepdims=True)
    slots[0:1, :] = s0.astype(jnp.int32)
    slots[1:2, :] = s1.astype(jnp.int32)
    for j in range(4):
        e = j // 2

        @pl.when(k != j % 2)
        def _():
            rcopy(cset(j), cset(j), l5s.at[e], l5r.at[e], part).wait_recv()

    go()
    lead_factor(
        pat, lambda i, j: lead[j, i], q_ref, thi, tlo, phi, plo, a_ref, b_ref, u_ref, w_ref, lambda: go(2)
    )
    while state[0] < NBATCH + LAG:
        go()
    pltpu.make_async_copy(send.at[me], recv.at[me], lsem).wait()

    def drain(t, _):
        tie = is_tie(t)

        @pl.when(tie)
        def _():
            cp = rcopy(send.at[0, 0], recv.at[0, 0], ss.at[t], rs.at[t], part)
            cp.wait_send()
            cp.wait_recv()
            rcopy(send.at[0, 0], relay.at[0], rss.at[t], rrs.at[t], part).wait_send()
            cp = rcopy(relay.at[0], recv.at[0, 1], fss.at[t], frs.at[t], part)
            cp.wait_send()
            cp.wait_recv()

        @pl.when(jnp.logical_not(tie))
        def _():
            cp = rcopy(send.at[0], recv.at[0], ss.at[t], rs.at[t], part)
            cp.wait_send()
            cp.wait_recv()

        rcopy(meta, mrow, mssem.at[t], msem, part).wait_send()
        return 0

    lax.fori_loop(1, 128, drain, 0)
    for j in range(4):
        e = j // 2

        @pl.when((y == 0) & (c == j))
        def _():
            @pl.when(z >= j)
            def _():
                for d in (1, 2, 3):
                    rcopy(lead.at[j, 0], lead.at[j, 0], l1s.at[d], l1r.at[0], part).wait_send()

            rcopy(cset(j), cset(j), l2s.at[0], l2r.at[e], part).wait_send()
            rcopy(cset(j), cset(j), l2s.at[1], l2r.at[e], part).wait_send()

        @pl.when((y == 0) & (k == j % 2) & (x == 3 - e))
        def _():
            rcopy(cset(j), cset(j), l2s.at[2], l2r.at[e], part).wait_send()

        @pl.when((y == 0) & (k == j % 2))
        def _():
            for d in (1, 3, 2):
                rcopy(cset(j), cset(j), l4s.at[e, d], l4r.at[e], part).wait_send()

        @pl.when(k == j % 2)
        def _():
            rcopy(cset(j), cset(j), l5s.at[e], l5r.at[e], part).wait_send()


def exchange(pattern, meta, send, front):
    vm = spec(pltpu.VMEM)
    dma = pltpu.SemaphoreType.DMA
    bf = jax.ShapeDtypeStruct((512, 512), jnp.bfloat16)
    return pl.pallas_call(
        exchange_kernel,
        out_shape=(
            jax.ShapeDtypeStruct((128, 2, T, T), jnp.float32),
            jax.ShapeDtypeStruct((128, T, T), jnp.float32),
            jax.ShapeDtypeStruct((8, 128), jnp.int32),
            jax.ShapeDtypeStruct((512, 512), jnp.float32),
            bf, bf, bf, bf,
        ),
        in_specs=[spec(pltpu.SMEM), vm, spec(ANY), spec(ANY)],
        out_specs=(spec(ANY), spec(ANY), vm, vm, vm, vm, vm, vm),
        scratch_shapes=[pltpu.VMEM((4, 4, T, T), jnp.float32), pltpu.VMEM((128, 128), jnp.int32)]
        + [pltpu.VMEM((T, T), jnp.float32)] * 4
        + [dma(()), dma(())]
        + [dma((128,))] * 7
        + [dma(()), dma((4,)), dma((4,)), dma((3,)), dma((2,)), dma((2, 4)), dma((2,)), dma((2,)), dma((2,))],
        compiler_params=pltpu.CompilerParams(collective_id=0, has_side_effects=True, vmem_limit_bytes=VLIM),
        name="exchange",
    )(pattern, meta, send, front)


def panel_kernel(asm, rows, cols, lsem, ssem_sc, rsem_sc, s1s, s1r, s2s, s2r, fs, fr, rs_s, rs_r, pt_s, pt_r):
    r = lax.axis_index("prow")
    c = lax.axis_index("pcol")
    y, z, x, k = r // 4, r % 4, c // 2, c % 2
    tc = r % 8
    half = r // 8
    selfhit = (c < 4) & (tc == c)
    bar = pltpu.get_barrier_semaphore()

    def sig(rr, cc):
        pl.semaphore_signal(bar, inc=1, device_id=(rr, cc), device_id_type=MESH)

    def zn(d):
        return y * 4 + (z + d) % 4

    def yn(d):
        return ((y + d) % 4) * 4 + z

    def xn(d):
        return ((x + d) % 4) * 2 + k

    for q in range(16):
        @pl.when((c < 4) & jnp.logical_not((tc == c) & (r == q)))
        def _():
            sig(q, tc)
    for h in range(2):
        for cc in range(4):
            @pl.when(jnp.logical_not((r == c + 8 * h) & (c == cc)))
            def _():
                sig(c + 8 * h, cc)
    for d in (1, 2, 3):
        sig(zn(d), c)
        sig(yn(d), c)
    sig(r, xn(1))
    sig(r, xn(3))
    sig(r, x * 2 + 1 - k)
    n_sc = jnp.where(c < 4, 16, 0) + 8 - jnp.where(selfhit, 2, 0)
    pl.semaphore_wait(bar, n_sc + 9)

    def rcopy(src, dst, ss, rs, dev):
        return pltpu.make_async_remote_copy(
            src_ref=src, dst_ref=dst, send_sem=ss, recv_sem=rs, device_id=dev, device_id_type=MESH
        )

    def sc_dst(h, q, cc):
        return cols.at[h, pl.ds(q * 64, 64), pl.ds(cc * T, T)]

    def sc_copy(q):
        src = asm.at[q // 2, 0, pl.ds((q % 2) * 64, 64), :]
        return src, sc_dst(half, q, c), rsem_sc.at[half * 4 + c]

    own = asm.at[:, 0]

    def rowcol(cc):
        return rows.at[:, :, pl.ds(pl.multiple_of(cc * T, T), T)]

    @pl.when(c < 4)
    def _():
        for q in range(16):
            src, dst, rsem = sc_copy(q)
            hit = (tc == c) & (r == q)

            @pl.when(hit)
            def _():
                pltpu.make_async_copy(src, dst, rsem).start()

            @pl.when(jnp.logical_not(hit))
            def _():
                rcopy(src, dst, ssem_sc.at[q], rsem, (q, tc)).start()

        pltpu.make_async_copy(own, rowcol(c), lsem).start()

    for e in range(2):
        @pl.when(x == e)
        def _():
            rcopy(own, rowcol(c), rs_s.at[0], rs_r.at[e], (r, xn(1))).start()
            rcopy(own, rowcol(c), rs_s.at[1], rs_r.at[e], (r, xn(3))).start()

    def slab(h, q):
        return cols.at[h, pl.ds(q * 64, 64), :]

    for h in range(2):
        nb = zn if h == 0 else yn
        for cc in range(4):
            piece = sc_dst(h, r, cc)
            pltpu.make_async_copy(piece, piece, rsem_sc.at[h * 4 + cc]).wait()
        for d in (1, 3, 2):
            rcopy(slab(h, r), slab(h, r), s1s.at[h, d], s1r.at[h, d], (nb(d), c)).start()

    part = (r, x * 2 + 1 - k)
    for e in range(2):
        item = rowcol(2 * e + k)

        @pl.when((x == (e + 1) % 4) | (x == (e + 3) % 4))
        def _():
            rcopy(item, item, rs_s.at[2], rs_r.at[e], part).wait_recv()

        @pl.when(x == 3 - e)
        def _():
            rcopy(item, item, rs_s.at[2], rs_r.at[e], (r, (2 + e) * 2 + k)).start()

        @pl.when(x == e)
        def _():
            pltpu.make_async_copy(own, rowcol(c), lsem).wait()

        @pl.when(x != 2 + e)
        def _():
            rcopy(item, item, pt_s.at[e], pt_r.at[e], part).start()

    def line(h, p, j):
        if h == 0:
            return slab(0, ((y + p) % 4) * 4 + j)
        return slab(1, j * 4 + (z + p) % 4)

    for h in range(2):
        nb1 = zn if h == 0 else yn
        nb2 = yn if h == 0 else zn
        for d in (1, 3, 2):
            got = slab(h, nb1(-d))
            rcopy(got, got, s1s.at[h, d], s1r.at[h, d], part).wait_recv()
        for j in range(4):
            jp, jm = j, (j + 2) % 4
            for dirn, jj in ((0, jp), (1, jm)):
                sl = line(h, 0, jj)
                dev = (nb2(1 if dirn == 0 else 3), c)
                rcopy(sl, sl, s2s.at[h, dirn, jj], s2r.at[h, dirn, jj], dev).start()
    for i in range(2):
        for h in range(2):
            nb2 = yn if h == 0 else zn
            sl = line(h, 3, i)
            rcopy(sl, sl, s2s.at[h, 0, i], s2r.at[h, 0, i], part).wait_recv()
            rcopy(sl, sl, fs.at[h, 0, i], fr.at[h, 0, i], (nb2(1), c)).start()
            sl = line(h, 1, 2 + i)
            rcopy(sl, sl, s2s.at[h, 1, 2 + i], s2r.at[h, 1, 2 + i], part).wait_recv()
            rcopy(sl, sl, fs.at[h, 1, i], fr.at[h, 1, i], (nb2(3), c)).start()
    for e in range(2):
        item = rowcol(2 * e + k)

        @pl.when(x == 2 + e)
        def _():
            rcopy(item, item, rs_s.at[2], rs_r.at[e], part).wait_recv()
            rcopy(item, item, pt_s.at[e], pt_r.at[e], part).start()

    for h in range(2):
        for i in range(2):
            sl = line(h, 3, 2 + i)
            rcopy(sl, sl, s2s.at[h, 0, 2 + i], s2r.at[h, 0, 2 + i], part).wait_recv()
            sl = line(h, 1, i)
            rcopy(sl, sl, s2s.at[h, 1, i], s2r.at[h, 1, i], part).wait_recv()
            sl = line(h, 2, i)
            rcopy(sl, sl, fs.at[h, 0, i], fr.at[h, 0, i], part).wait_recv()
            sl = line(h, 2, 2 + i)
            rcopy(sl, sl, fs.at[h, 1, i], fr.at[h, 1, i], part).wait_recv()
    for e in range(2):
        item = rowcol(2 * e + 1 - k)
        rcopy(item, item, pt_s.at[e], pt_r.at[e], part).wait_recv()
    sl = slab(0, r)
    for h in range(2):
        for d in (1, 2, 3):
            rcopy(sl, sl, s1s.at[h, d], s1r.at[h, d], part).wait_send()
        for dirn in range(2):
            for j in range(4):
                rcopy(sl, sl, s2s.at[h, dirn, j], s2r.at[h, dirn, j], part).wait_send()
            for i in range(2):
                rcopy(sl, sl, fs.at[h, dirn, i], fr.at[h, dirn, i], part).wait_send()
    item = rowcol(k)
    for e in range(2):
        rcopy(item, item, pt_s.at[e], pt_r.at[e], part).wait_send()

    @pl.when(x < 2)
    def _():
        rcopy(item, item, rs_s.at[0], rs_r.at[0], part).wait_send()
        rcopy(item, item, rs_s.at[1], rs_r.at[0], part).wait_send()

    @pl.when(x >= 2)
    def _():
        rcopy(item, item, rs_s.at[2], rs_r.at[0], part).wait_send()

    @pl.when(c < 4)
    def _():
        for q in range(16):
            @pl.when(jnp.logical_not((tc == c) & (r == q)))
            def _():
                src, dst, rsem = sc_copy(q)
                rcopy(src, dst, ssem_sc.at[q], rsem, part).wait_send()


def panel(asm):
    dma = pltpu.SemaphoreType.DMA
    return pl.pallas_call(
        panel_kernel,
        out_shape=(
            jax.ShapeDtypeStruct((8, T, 512), jnp.float32),
            jax.ShapeDtypeStruct((2, 1024, 512), jnp.float32),
        ),
        in_specs=[spec(ANY)],
        out_specs=(spec(ANY), spec(ANY)),
        scratch_shapes=[
            dma(()),
            dma((16,)),
            dma((8,)),
            dma((2, 4)),
            dma((2, 4)),
            dma((2, 2, 4)),
            dma((2, 2, 4)),
            dma((2, 2, 2)),
            dma((2, 2, 2)),
            dma((3,)),
            dma((2,)),
            dma((2,)),
            dma((2,)),
        ],
        compiler_params=pltpu.CompilerParams(collective_id=1, has_side_effects=True, vmem_limit_bytes=VLIM),
        cost_estimate=pl.CostEstimate(flops=0, bytes_accessed=1 << 26, transcendentals=0),
        name="panel",
    )(asm)


def schur_kernel(pat, rows, cols, acc, phi, plo, thi, tlo, q_ref, out, yext, cext, xh, xl, qbuf):
    r = lax.axis_index("prow")
    c = lax.axis_index("pcol")
    s = pl.program_id(0)
    f32 = jnp.float32

    def masks(i):
        e0 = pat[0, i].astype(f32)
        e1 = jnp.maximum(pat[0, i], pat[1, i]).astype(f32)
        return e0, e1

    def mm(a, b):
        return jnp.dot(a, b, preferred_element_type=f32)

    def masked(x, e):
        return jnp.concatenate([x[:, :256] * e[0], x[:, 256:] * e[1]], axis=1)

    @pl.when(s == 0)
    def _():
        off = pl.multiple_of(jnp.minimum(c, 3) * T, T)
        for a in range(8):
            hi, lo = split(masked(rows[a], masks(a * 16 + r)))
            xh[a * T : (a + 1) * T, :] = hi
            xl[a * T : (a + 1) * T, :] = lo
        y = mm(xh[...], phi[...]) + mm(xl[...], phi[...]) + mm(xh[...], plo[...])
        yh, yl = split(y)
        yext[:, 0:512] = yh
        yext[:, 512:1024] = yh
        yext[:, 1024:1536] = yl

        @pl.when(c < 4)
        def _():
            th = thi[:, pl.ds(off, T)]
            qbuf[...] = mm(xh[...], th) + mm(xl[...], th) + mm(xh[...], tlo[:, pl.ds(off, T)])

        @pl.when((c < 4) & (r < 4))
        def _():
            qbuf[0:T, :] = q_ref[pl.ds(pl.multiple_of(jnp.minimum(r, 3) * T, T), T), pl.ds(off, T)]

    for h in range(2):
        hi, lo = split(masked(cols[h], masks(s * 16 + h * 8 + c)))
        cext[h * T : (h + 1) * T, 0:512] = hi
        cext[h * T : (h + 1) * T, 512:1024] = lo
        cext[h * T : (h + 1) * T, 1024:1536] = hi
    upd = lax.dot_general(yext[...], cext[...], (((1,), (1,)), ((), ())), preferred_element_type=f32)
    for a in range(8):
        for h in range(2):
            val = acc[a, 0, h, 0] - upd[a * T : (a + 1) * T, h * T : (h + 1) * T]
            if a == 0:
                val = jnp.where(r < 4, 0.0, val)
            out[a, 0, h, 0] = val

    @pl.when((s == 0) & (c < 4))
    def _():
        for a in range(8):
            out[a, 0, 0, 0] = qbuf[a * T : (a + 1) * T, :]


def schur(pattern, rows, cols, acc, phi, plo, thi, tlo, qlead):
    full = lambda *shape: pl.BlockSpec(shape, lambda s: (0,) * len(shape))
    blk = pl.BlockSpec((8, 1, 2, 1, T, T), lambda s: (0, 0, s, 0, 0, 0))
    return pl.pallas_call(
        schur_kernel,
        grid=(8,),
        out_shape=jax.ShapeDtypeStruct((8, 1, 16, 1, T, T), jnp.float32),
        in_specs=[
            spec(pltpu.SMEM),
            full(8, T, 512),
            pl.BlockSpec((2, T, 512), lambda s: (0, s, 0)),
            blk,
            full(512, 512),
            full(512, 512),
            full(512, 512),
            full(512, 512),
            full(512, 512),
        ],
        out_specs=blk,
        scratch_shapes=[
            pltpu.VMEM((1024, 1536), jnp.bfloat16),
            pltpu.VMEM((256, 1536), jnp.bfloat16),
            pltpu.VMEM((1024, 512), jnp.bfloat16),
            pltpu.VMEM((1024, 512), jnp.bfloat16),
            pltpu.VMEM((1024, T), jnp.float32),
        ],
        compiler_params=pltpu.CompilerParams(vmem_limit_bytes=VLIM),
        cost_estimate=pl.CostEstimate(flops=7 << 30, bytes_accessed=6 << 22, transcendentals=0),
        name="schur",
    )(pattern, rows, cols, acc, phi, plo, thi, tlo, qlead)


def local(front, child_blocks, owners, slots, pattern):
    send, meta = pack(owners[:, 0], slots, child_blocks)
    blocks = front.reshape(128, T, T)
    recv, _, got, qlead, thi, tlo, phi, plo = exchange(pattern, meta, send, blocks)
    asm = assemble(got, recv, blocks)
    rows, cols = panel(asm.reshape(8, 16, T, T))
    return schur(
        pattern, rows, cols, asm.reshape(8, 1, 16, 1, T, T), phi, plo, thi, tlo, qlead
    )


def solution(mesh):
    placed = (
        P(None, "prow", None, "pcol", None, None),
        P(("prow", "pcol"), None, None),
        P(("prow", "pcol"), None),
        P(("prow", "pcol")),
        P(),
    )
    return jax.shard_map(
        local,
        mesh=mesh,
        in_specs=placed,
        out_specs=P(None, "prow", None, "pcol", None, None),
        check_vma=False,
    )
```

```python
import jax
import jax.numpy as jnp
from jax import lax
from jax.experimental import pallas as pl
from jax.experimental.pallas import tpu as pltpu
from jax.sharding import PartitionSpec as P

T = 128
MESH = pl.DeviceIdType.MESH
ANY = pl.ANY
VLIM = 60000 * 1024
HI = lax.Precision.HIGHEST


def spec(space):
    return pl.BlockSpec(memory_space=space)


def pack_kernel(owners, owners_v, slots_v, child, send, meta, buf, cnt, isem, osem):
    for g in range(8):
        pltpu.make_async_copy(child.at[pl.ds(g * 16, 16)], buf.at[pl.ds(g * 16, 16)], isem.at[g]).start()
    meta[...] = owners_v[...] * 128 + slots_v[...]

    def zero(i, _):
        cnt[i] = 0
        return 0

    lax.fori_loop(0, 128, zero, 0)
    for g in range(8):
        pltpu.make_async_copy(child.at[pl.ds(g * 16, 16)], buf.at[pl.ds(g * 16, 16)], isem.at[g]).wait()

        def put(i, _):
            o = owners[i]
            k = cnt[o]
            cnt[o] = k + 1
            dst = send.at[o >> 5, (o >> 3) & 3, o & 7, pl.ds(pl.multiple_of(k * T, T), T)]
            pltpu.make_async_copy(buf.at[i], dst, osem.at[i]).start()
            return 0

        lax.fori_loop(g * 16, g * 16 + 16, put, 0)

    def fin(i, _):
        pltpu.make_async_copy(buf.at[i], send.at[0, 0, 0, pl.ds(0, T)], osem.at[i]).wait()
        return 0

    lax.fori_loop(0, 128, fin, 0)


def pack(owners, slots, child):
    return pl.pallas_call(
        pack_kernel,
        out_shape=(
            jax.ShapeDtypeStruct((4, 4, 8, 256, T), jnp.float32),
            jax.ShapeDtypeStruct((1, 128), jnp.int32),
        ),
        in_specs=[spec(pltpu.SMEM), spec(pltpu.VMEM), spec(pltpu.VMEM), spec(ANY)],
        out_specs=(spec(ANY), spec(pltpu.VMEM)),
        scratch_shapes=[
            pltpu.VMEM((128, T, T), jnp.float32),
            pltpu.SMEM((128,), jnp.int32),
            pltpu.SemaphoreType.DMA((8,)),
            pltpu.SemaphoreType.DMA((128,)),
        ],
        compiler_params=pltpu.CompilerParams(vmem_limit_bytes=VLIM),
        cost_estimate=pl.CostEstimate(flops=0, bytes_accessed=2 << 23, transcendentals=0),
        name="pack",
    )(owners, owners.reshape(1, 128), slots.reshape(1, 128), child)


def assemble_kernel(slots, pa, pb, pc, front, out, acc, buf, fsem, rsem, osem):
    def copies(i, h):
        y, z, c = i >> 6, (i >> 4) & 3, (i >> 1) & 7
        a, b, d = pa.at[z, y, c], pb.at[c, z, y], pc.at[y, c, z]
        if h == 0:
            return (
                pltpu.make_async_copy(a, buf.at[i, pl.ds(0, 88)], rsem.at[i, 0]),
                pltpu.make_async_copy(b.at[pl.ds(0, 40)], buf.at[i, pl.ds(88, 40)], rsem.at[i, 1]),
            )
        return (
            pltpu.make_async_copy(b.at[pl.ds(40, 48)], buf.at[i, pl.ds(0, 48)], rsem.at[i, 0]),
            pltpu.make_async_copy(d, buf.at[i, pl.ds(48, 80)], rsem.at[i, 1]),
        )

    def get(n, _):
        for h in range(2):
            i = 2 * n + h

            @pl.when(slots[h, n] != 0)
            def _():
                for cp in copies(i, h):
                    cp.start()

        return 0

    lax.fori_loop(0, 128, get, 0)
    for g in range(8):
        pltpu.make_async_copy(front.at[pl.ds(g * 16, 16)], acc.at[pl.ds(g * 16, 16)], fsem.at[g]).start()
    for g in range(8):
        pltpu.make_async_copy(front.at[pl.ds(g * 16, 16)], acc.at[pl.ds(g * 16, 16)], fsem.at[g]).wait()

    def add(n, _):
        for h in range(2):
            i = 2 * n + h
            s = slots[h, n]

            @pl.when(s != 0)
            def _():
                for cp in copies(i, h):
                    cp.wait()
                acc[s] = acc[s] + buf[i]

        return 0

    lax.fori_loop(0, 128, add, 0)
    for g in range(8):
        pltpu.make_async_copy(acc.at[pl.ds(g * 16, 16)], out.at[pl.ds(g * 16, 16)], osem.at[g]).start()
    for g in range(8):
        pltpu.make_async_copy(acc.at[pl.ds(g * 16, 16)], out.at[pl.ds(g * 16, 16)], osem.at[g]).wait()


def assemble(slots, pa, pb, pc, front):
    return pl.pallas_call(
        assemble_kernel,
        out_shape=jax.ShapeDtypeStruct((128, T, T), jnp.float32),
        in_specs=[spec(pltpu.SMEM)] + [spec(ANY)] * 4,
        out_specs=spec(ANY),
        scratch_shapes=[
            pltpu.VMEM((128, T, T), jnp.float32),
            pltpu.VMEM((256, T, T), jnp.float32),
            pltpu.SemaphoreType.DMA((8,)),
            pltpu.SemaphoreType.DMA((256, 2)),
            pltpu.SemaphoreType.DMA((8,)),
        ],
        compiler_params=pltpu.CompilerParams(vmem_limit_bytes=VLIM),
        cost_estimate=pl.CostEstimate(flops=0, bytes_accessed=4 << 23, transcendentals=0),
        name="assemble",
    )(slots, pa, pb, pc, front)


def dot(a, b, ta=0, tb=0):
    dims = (((0 if ta else 1,), (1 if tb else 0,)), ((), ()))
    return lax.dot_general(a, b, dims, precision=HI, preferred_element_type=jnp.float32)


def split(x):
    hi = x.astype(jnp.bfloat16)
    lo = (x - hi.astype(jnp.float32)).astype(jnp.bfloat16)
    return hi, lo


def eliminate(a_ref, b_ref, u_ref, w_ref):
    lane = lax.broadcasted_iota(jnp.int32, (T, T), 1)
    sub = lax.broadcasted_iota(jnp.int32, (T, T), 0)
    lane1 = lax.broadcasted_iota(jnp.int32, (1, T), 1)
    sub1 = lax.broadcasted_iota(jnp.int32, (T, 1), 0)
    b_ref[...] = (lane == sub).astype(jnp.float32)

    def step(k, _):
        row = a_ref[pl.ds(k, 1), :]
        brow = b_ref[pl.ds(k, 1), :]
        mat = a_ref[...]
        d = jnp.sum(jnp.where(lane1 == k, row, 0.0), axis=1, keepdims=True)
        col = jnp.sum(jnp.where(lane == k, mat, 0.0), axis=1, keepdims=True)
        rs = 1.0 / jnp.sqrt(d)
        m = jnp.where(sub1 > k, col * (1.0 / d), 0.0)
        u_ref[pl.ds(k, 1), :] = jnp.where(lane1 >= k, row * rs, 0.0)
        w_ref[pl.ds(k, 1), :] = brow * rs
        a_ref[...] = mat - m * row
        b_ref[...] = b_ref[...] - m * brow
        return 0

    lax.fori_loop(0, T, step, 0)
    return u_ref[...].T, w_ref[...]


def sym_lower(x):
    lane = lax.broadcasted_iota(jnp.int32, (T, T), 1)
    sub = lax.broadcasted_iota(jnp.int32, (T, T), 0)
    return jnp.where(sub >= lane, x, x.T)


def factor256(g00, g10, g11, a_ref, b_ref, u_ref, w_ref, hook):
    a_ref[...] = sym_lower(g00)
    l00, w00 = eliminate(a_ref, b_ref, u_ref, w_ref)
    hook()
    l10 = dot(g10, w00, tb=1)
    a_ref[...] = sym_lower(g11 - dot(l10, l10, tb=1))
    l11, w11 = eliminate(a_ref, b_ref, u_ref, w_ref)
    hook()
    w10 = -dot(w11, dot(l10, w00))
    zero = jnp.zeros((T, T), jnp.float32)
    low = jnp.concatenate([jnp.concatenate([l00, zero], 1), jnp.concatenate([l10, l11], 1)], 0)
    inv = jnp.concatenate([jnp.concatenate([w00, zero], 1), jnp.concatenate([w10, w11], 1)], 0)
    return low, inv


def lead_factor(pat, blk, q_ref, thi, tlo, phi, plo, a_ref, b_ref, u_ref, w_ref, hook):
    low0, inv0 = factor256(blk(0, 0), blk(1, 0), blk(1, 1), a_ref, b_ref, u_ref, w_ref, hook)
    rect = jnp.concatenate(
        [jnp.concatenate([blk(2, 0), blk(2, 1)], 1), jnp.concatenate([blk(3, 0), blk(3, 1)], 1)], 0
    )
    s = dot(rect, inv0, tb=1)
    e2 = pat[0, 2].astype(jnp.float32)
    e3 = pat[0, 3].astype(jnp.float32)
    s = jnp.concatenate([s[:T] * e2, s[T:] * e3], 0)
    ss = dot(s, s, tb=1)
    low1, inv1 = factor256(
        blk(2, 2) - ss[:T, :T], blk(3, 2) - ss[T:, :T], blk(3, 3) - ss[T:, T:], a_ref, b_ref, u_ref, w_ref, hook
    )
    zero = jnp.zeros((256, 256), jnp.float32)
    q_ref[0:256, 0:256] = low0
    q_ref[0:256, 256:512] = zero
    q_ref[256:512, 0:256] = s
    q_ref[256:512, 256:512] = low1
    t01 = -dot(inv0, dot(s, inv1, ta=1, tb=1), ta=1)
    t = jnp.concatenate(
        [jnp.concatenate([inv0.T, t01], 1), jnp.concatenate([zero, inv1.T], 1)], 0
    )
    p = dot(t, t, tb=1)
    hi, lo = split(t)
    thi[...] = hi
    tlo[...] = lo
    hi, lo = split(p)
    phi[...] = hi
    plo[...] = lo


PARTS = (("c", "y", "z"), ("y", "z", "c"), ("z", "c", "y"))
NEAR = {"c": (2, 3, 6, 7, 1), "y": (1, 3), "z": (1, 3)}
FAR = {"c": (4, 5), "y": (2,), "z": (2,)}
SIZE = {"c": 8, "y": 4, "z": 4}
ROWS = (88, 88, 80)


def exchange_kernel(
    pat, meta, send, front, oa, ob, oc, slots, q_ref, thi, tlo, phi, plo,
    ba1, bb1, bc1, ba2, bb2, bc2,
    lead, meta_all, a_ref, b_ref, u_ref, w_ref,
    msem, mssem, f1s, f1r, f2s, f2r, f3s, f3r, l0, l1s, l1r, l2s, l2r, l4s, l4r, l5s, l5r,
):
    r = lax.axis_index("prow")
    c = lax.axis_index("pcol")
    y, z, x, k = r // 4, r % 4, c // 2, c % 2
    me = r * 8 + c
    part = (r, x * 2 + 1 - k)
    b1, b2, b3 = (ba1, bb1, bc1), (ba2, bb2, bc2), (oa, ob, oc)
    own = {"y": y, "z": z, "c": c}
    bar = pltpu.get_barrier_semaphore()

    def rcopy(src, dst, s_sem, r_sem, dev):
        return pltpu.make_async_remote_copy(
            src_ref=src, dst_ref=dst, send_sem=s_sem, recv_sem=r_sem, device_id=dev, device_id_type=MESH
        )

    def other(t):
        return ((y + t // 32) % 4) * 4 + (z + (t // 8) % 4) % 4, ((x + (t // 2) % 4) % 4) * 2 + (k + t) % 2

    def sig(i, _):
        pl.semaphore_signal(bar, inc=1, device_id=other(i), device_id_type=MESH)
        return 0

    lax.fori_loop(1, 128, sig, 0)
    pl.semaphore_wait(bar, 127)

    def plus(ax, o):
        if ax == "c":
            return ((x + o // 2) % 4) * 2 + (k + o) % 2
        return (own[ax] + o) % 4

    def minus(ax, o):
        if ax == "c":
            return ((x + 4 - o // 2) % 4) * 2 + (k + o) % 2
        return (own[ax] + 4 - o) % 4

    def dev(ax, v):
        return {"c": (r, v), "y": (v * 4 + z, c), "z": (y * 4 + v, c)}[ax]

    def src1(n, v):
        return (
            lambda: send.at[:, :, v, pl.ds(0, 88)],
            lambda: send.at[v, :, :, pl.ds(88, 88)],
            lambda: send.at[:, v, :, pl.ds(176, 80)],
        )[n]()

    def src2(n, i, v):
        return b1[n].at[i, :, v] if n == 2 else b1[n].at[i, v]

    def src3(n, j, v):
        return b2[n].at[j, :, v]

    def first(n):
        p = PARTS[n][0]
        for o in NEAR[p] + FAR[p]:
            v = plus(p, o)
            rcopy(src1(n, v), b1[n].at[own[p]], f1s.at[n, o], f1r.at[n, own[p]], dev(p, v)).start()

    def first_own(n):
        p = PARTS[n][0]
        pltpu.make_async_copy(src1(n, own[p]), b1[n].at[own[p]], f1r.at[n, own[p]]).start()

    def second(n, i):
        q = PARTS[n][1]
        piece = b1[n].at[i]
        pltpu.make_async_copy(piece, piece, f1r.at[n, i]).wait()
        for o in NEAR[q] + FAR[q]:
            v = plus(q, o)
            rcopy(src2(n, i, v), b2[n].at[own[q], i], f2s.at[n, i, o], f2r.at[n, own[q], i], dev(q, v)).start()
        pltpu.make_async_copy(src2(n, i, own[q]), b2[n].at[own[q], i], f2r.at[n, own[q], i]).start()

    def third(n, j):
        p, q, u = PARTS[n]
        for i in range(SIZE[p]):
            piece = b2[n].at[j, i]
            pltpu.make_async_copy(piece, piece, f2r.at[n, j, i]).wait()
        for o in NEAR[u] + FAR[u]:
            v = plus(u, o)
            rcopy(src3(n, j, v), b3[n].at[own[u], j], f3s.at[n, j, o], f3r.at[n, own[u], j], dev(u, v)).start()
        pltpu.make_async_copy(src3(n, j, own[u]), b3[n].at[own[u], j], f3r.at[n, own[u], j]).start()

    def cset(j):
        return lead.at[j, pl.ds(j, 4 - j)]

    for j in range(4):
        @pl.when((y == 0) & (c == j) & (z >= j))
        def _():
            cp = pltpu.make_async_copy(front.at[0], lead.at[j, z], l0)
            cp.start()
            cp.wait()
            for d in (1, 2, 3):
                rcopy(lead.at[j, z], lead.at[j, z], l1s.at[d], l1r.at[z], ((z + d) % 4, c)).start()

    mrow = meta_all.at[pl.ds(me, 1), :]
    pltpu.make_async_copy(meta, mrow, msem).start()

    def tell(i, _):
        rcopy(meta, mrow, mssem.at[i], msem, other(i)).start()
        return 0

    lax.fori_loop(1, 128, tell, 0)
    first(2)

    @pl.when(y != 0)
    def _():
        first(0)
        first(1)

    for n in range(3):
        first_own(n)
    for j in range(4):
        e = j // 2

        @pl.when((y == 0) & (c == j))
        def _():
            for i in range(j, 4):
                @pl.when(z != i)
                def _():
                    rcopy(lead.at[j, i], lead.at[j, i], l1s.at[0], l1r.at[i], part).wait_recv()

            rcopy(cset(j), cset(j), l2s.at[0], l2r.at[e], (r, ((x + 1) % 4) * 2 + k)).start()
            rcopy(cset(j), cset(j), l2s.at[1], l2r.at[e], (r, ((x + 3) % 4) * 2 + k)).start()

    for j in range(4):
        e = j // 2

        @pl.when((y == 0) & (k == j % 2) & ((x == (e + 1) % 4) | (x == (e + 3) % 4)))
        def _():
            rcopy(cset(j), cset(j), l2s.at[2], l2r.at[e], part).wait_recv()

        @pl.when((y == 0) & (k == j % 2) & (x == 3 - e))
        def _():
            rcopy(cset(j), cset(j), l2s.at[2], l2r.at[e], (r, (2 + e) * 2 + k)).start()

    @pl.when(y == 0)
    def _():
        first(0)

    for j in range(4):
        e = j // 2

        @pl.when((y == 0) & (k == j % 2) & (x == 2 + e))
        def _():
            rcopy(cset(j), cset(j), l2s.at[2], l2r.at[e], part).wait_recv()

        @pl.when((y == 0) & (k == j % 2))
        def _():
            for d in (1, 3, 2):
                rcopy(cset(j), cset(j), l4s.at[e, d], l4r.at[e], (d * 4 + z, c)).start()

    @pl.when(y == 0)
    def _():
        first(1)

    for n in range(3):
        second(n, own[PARTS[n][0]])
    for j in range(4):
        e = j // 2

        @pl.when((y != 0) & (k == j % 2))
        def _():
            rcopy(cset(j), cset(j), l4s.at[e, 0], l4r.at[e], part).wait_recv()

        @pl.when(k == j % 2)
        def _():
            rcopy(cset(j), cset(j), l5s.at[e], l5r.at[e], part).start()

    pltpu.make_async_copy(meta_all, meta_all, msem).wait()
    mt = meta_all[...].astype(jnp.float32).T
    whose = jnp.floor(mt * (1.0 / 128.0))
    sl = mt - whose * 128.0
    idx = lax.broadcasted_iota(jnp.int32, (128, 128), 0).astype(jnp.float32)
    mine = whose == me.astype(jnp.float32)
    low = jnp.min(jnp.where(mine, idx, 999.0), axis=0, keepdims=True)
    high = jnp.max(jnp.where(mine, idx, -1.0), axis=0, keepdims=True)
    s0 = jnp.sum(jnp.where(mine & (idx == low), sl, 0.0), axis=0, keepdims=True)
    s1 = jnp.sum(jnp.where(mine & (idx == high) & (idx > low), sl, 0.0), axis=0, keepdims=True)
    slots[0:1, :] = s0.astype(jnp.int32)
    slots[1:2, :] = s1.astype(jnp.int32)
    for j in range(4):
        e = j // 2

        @pl.when(k != j % 2)
        def _():
            rcopy(cset(j), cset(j), l5s.at[e], l5r.at[e], part).wait_recv()

    def go2(offsets):
        for n in range(3):
            p = PARTS[n][0]
            for o in offsets[p]:
                second(n, minus(p, o))

    def go3(offsets):
        for n in range(3):
            q = PARTS[n][1]
            for o in offsets[q]:
                third(n, minus(q, o))

    work = [
        lambda: go2(NEAR),
        lambda: go2(FAR),
        lambda: go3({"c": (0,), "y": (0,), "z": (0,)}),
        lambda: go3({"c": (2, 3, 1), "y": (1,), "z": (1,)}),
        lambda: go3({"c": (6, 7), "y": (3,), "z": (3,)}),
        lambda: go3(FAR),
    ]

    def hook():
        if work:
            work.pop(0)()

    lead_factor(
        pat, lambda i, j: lead[j, i], q_ref, thi, tlo, phi, plo, a_ref, b_ref, u_ref, w_ref, hook
    )
    while work:
        hook()
    for n in range(3):
        p, q, u = PARTS[n]

        def arrived(j, _):
            for v in range(SIZE[u]):
                piece = b3[n].at[v, j]
                pltpu.make_async_copy(piece, piece, f3r.at[n, v, j]).wait()
            for o in NEAR[u] + FAR[u]:
                rcopy(src3(n, 0, 0), b3[n].at[0, 0], f3s.at[n, j, o], f3r.at[n, 0, 0], part).wait_send()
            return 0

        lax.fori_loop(0, SIZE[q], arrived, 0)
        for o in NEAR[p] + FAR[p]:
            rcopy(src1(n, 0), b1[n].at[0], f1s.at[n, o], f1r.at[n, 0], part).wait_send()

        def sent(i, _):
            for o in NEAR[q] + FAR[q]:
                rcopy(src2(n, 0, 0), b2[n].at[0, 0], f2s.at[n, i, o], f2r.at[n, 0, 0], part).wait_send()
            return 0

        lax.fori_loop(0, SIZE[p], sent, 0)

    def told(t, _):
        rcopy(meta, mrow, mssem.at[t], msem, part).wait_send()
        return 0

    lax.fori_loop(1, 128, told, 0)
    for j in range(4):
        e = j // 2

        @pl.when((y == 0) & (c == j))
        def _():
            @pl.when(z >= j)
            def _():
                for d in (1, 2, 3):
                    rcopy(lead.at[j, 0], lead.at[j, 0], l1s.at[d], l1r.at[0], part).wait_send()

            rcopy(cset(j), cset(j), l2s.at[0], l2r.at[e], part).wait_send()
            rcopy(cset(j), cset(j), l2s.at[1], l2r.at[e], part).wait_send()

        @pl.when((y == 0) & (k == j % 2) & (x == 3 - e))
        def _():
            rcopy(cset(j), cset(j), l2s.at[2], l2r.at[e], part).wait_send()

        @pl.when((y == 0) & (k == j % 2))
        def _():
            for d in (1, 3, 2):
                rcopy(cset(j), cset(j), l4s.at[e, d], l4r.at[e], part).wait_send()

        @pl.when(k == j % 2)
        def _():
            rcopy(cset(j), cset(j), l5s.at[e], l5r.at[e], part).wait_send()


def exchange(pattern, meta, send, front):
    vm = spec(pltpu.VMEM)
    dma = pltpu.SemaphoreType.DMA
    bf = jax.ShapeDtypeStruct((512, 512), jnp.bfloat16)

    def buf(kind, a, b, d, n):
        return kind((a, b, d, ROWS[n], T), jnp.float32)

    return pl.pallas_call(
        exchange_kernel,
        out_shape=(
            buf(jax.ShapeDtypeStruct, 4, 4, 8, 0),
            buf(jax.ShapeDtypeStruct, 8, 4, 4, 1),
            buf(jax.ShapeDtypeStruct, 4, 8, 4, 2),
            jax.ShapeDtypeStruct((8, 128), jnp.int32),
            jax.ShapeDtypeStruct((512, 512), jnp.float32),
            bf, bf, bf, bf,
        ),
        in_specs=[spec(pltpu.SMEM), vm, spec(ANY), spec(ANY)],
        out_specs=(spec(ANY), spec(ANY), spec(ANY), vm, vm, vm, vm, vm, vm),
        scratch_shapes=[
            buf(pltpu.VMEM, 8, 4, 4, 0),
            buf(pltpu.VMEM, 4, 4, 8, 1),
            buf(pltpu.VMEM, 4, 4, 8, 2),
            buf(pltpu.VMEM, 4, 8, 4, 0),
            buf(pltpu.VMEM, 4, 4, 8, 1),
            buf(pltpu.VMEM, 8, 4, 4, 2),
            pltpu.VMEM((4, 4, T, T), jnp.float32),
            pltpu.VMEM((128, 128), jnp.int32),
        ]
        + [pltpu.VMEM((T, T), jnp.float32)] * 4
        + [dma(()), dma((128,)), dma((3, 8)), dma((3, 8))]
        + [dma((3, 8, 8))] * 4
        + [dma(()), dma((4,)), dma((4,)), dma((3,)), dma((2,)), dma((2, 4)), dma((2,)), dma((2,)), dma((2,))],
        compiler_params=pltpu.CompilerParams(collective_id=0, has_side_effects=True, vmem_limit_bytes=VLIM),
        name="exchange",
    )(pattern, meta, send, front)


def panel_kernel(asm, rows, cols, lsem, ssem_sc, rsem_sc, s1s, s1r, s2s, s2r, fs, fr, rs_s, rs_r, pt_s, pt_r):
    r = lax.axis_index("prow")
    c = lax.axis_index("pcol")
    y, z, x, k = r // 4, r % 4, c // 2, c % 2
    tc = r % 8
    half = r // 8
    selfhit = (c < 4) & (tc == c)
    bar = pltpu.get_barrier_semaphore()

    def sig(rr, cc):
        pl.semaphore_signal(bar, inc=1, device_id=(rr, cc), device_id_type=MESH)

    def zn(d):
        return y * 4 + (z + d) % 4

    def yn(d):
        return ((y + d) % 4) * 4 + z

    def xn(d):
        return ((x + d) % 4) * 2 + k

    for q in range(16):
        @pl.when((c < 4) & jnp.logical_not((tc == c) & (r == q)))
        def _():
            sig(q, tc)
    for h in range(2):
        for cc in range(4):
            @pl.when(jnp.logical_not((r == c + 8 * h) & (c == cc)))
            def _():
                sig(c + 8 * h, cc)
    for d in (1, 2, 3):
        sig(zn(d), c)
        sig(yn(d), c)
    sig(r, xn(1))
    sig(r, xn(3))
    sig(r, x * 2 + 1 - k)
    n_sc = jnp.where(c < 4, 16, 0) + 8 - jnp.where(selfhit, 2, 0)
    pl.semaphore_wait(bar, n_sc + 9)

    def rcopy(src, dst, ss, rs, dev):
        return pltpu.make_async_remote_copy(
            src_ref=src, dst_ref=dst, send_sem=ss, recv_sem=rs, device_id=dev, device_id_type=MESH
        )

    def sc_dst(h, q, cc):
        return cols.at[h, pl.ds(q * 64, 64), pl.ds(cc * T, T)]

    def sc_copy(q):
        src = asm.at[q // 2, 0, pl.ds((q % 2) * 64, 64), :]
        return src, sc_dst(half, q, c), rsem_sc.at[half * 4 + c]

    own = asm.at[:, 0]

    def rowcol(cc):
        return rows.at[:, :, pl.ds(pl.multiple_of(cc * T, T), T)]

    @pl.when(c < 4)
    def _():
        for q in range(16):
            src, dst, rsem = sc_copy(q)
            hit = (tc == c) & (r == q)

            @pl.when(hit)
            def _():
                pltpu.make_async_copy(src, dst, rsem).start()

            @pl.when(jnp.logical_not(hit))
            def _():
                rcopy(src, dst, ssem_sc.at[q], rsem, (q, tc)).start()

        pltpu.make_async_copy(own, rowcol(c), lsem).start()

    for e in range(2):
        @pl.when(x == e)
        def _():
            rcopy(own, rowcol(c), rs_s.at[0], rs_r.at[e], (r, xn(1))).start()
            rcopy(own, rowcol(c), rs_s.at[1], rs_r.at[e], (r, xn(3))).start()

    def slab(h, q):
        return cols.at[h, pl.ds(q * 64, 64), :]

    for h in range(2):
        nb = zn if h == 0 else yn
        for cc in range(4):
            piece = sc_dst(h, r, cc)
            pltpu.make_async_copy(piece, piece, rsem_sc.at[h * 4 + cc]).wait()
        for d in (1, 3, 2):
            rcopy(slab(h, r), slab(h, r), s1s.at[h, d], s1r.at[h, d], (nb(d), c)).start()

    part = (r, x * 2 + 1 - k)
    for e in range(2):
        item = rowcol(2 * e + k)

        @pl.when((x == (e + 1) % 4) | (x == (e + 3) % 4))
        def _():
            rcopy(item, item, rs_s.at[2], rs_r.at[e], part).wait_recv()

        @pl.when(x == 3 - e)
        def _():
            rcopy(item, item, rs_s.at[2], rs_r.at[e], (r, (2 + e) * 2 + k)).start()

        @pl.when(x == e)
        def _():
            pltpu.make_async_copy(own, rowcol(c), lsem).wait()

        @pl.when(x != 2 + e)
        def _():
            rcopy(item, item, pt_s.at[e], pt_r.at[e], part).start()

    def line(h, p, j):
        if h == 0:
            return slab(0, ((y + p) % 4) * 4 + j)
        return slab(1, j * 4 + (z + p) % 4)

    for h in range(2):
        nb1 = zn if h == 0 else yn
        nb2 = yn if h == 0 else zn
        for d in (1, 3, 2):
            got = slab(h, nb1(-d))
            rcopy(got, got, s1s.at[h, d], s1r.at[h, d], part).wait_recv()
        for j in range(4):
            jp, jm = j, (j + 2) % 4
            for dirn, jj in ((0, jp), (1, jm)):
                sl = line(h, 0, jj)
                dev = (nb2(1 if dirn == 0 else 3), c)
                rcopy(sl, sl, s2s.at[h, dirn, jj], s2r.at[h, dirn, jj], dev).start()
    for i in range(2):
        for h in range(2):
            nb2 = yn if h == 0 else zn
            sl = line(h, 3, i)
            rcopy(sl, sl, s2s.at[h, 0, i], s2r.at[h, 0, i], part).wait_recv()
            rcopy(sl, sl, fs.at[h, 0, i], fr.at[h, 0, i], (nb2(1), c)).start()
            sl = line(h, 1, 2 + i)
            rcopy(sl, sl, s2s.at[h, 1, 2 + i], s2r.at[h, 1, 2 + i], part).wait_recv()
            rcopy(sl, sl, fs.at[h, 1, i], fr.at[h, 1, i], (nb2(3), c)).start()
    for e in range(2):
        item = rowcol(2 * e + k)

        @pl.when(x == 2 + e)
        def _():
            rcopy(item, item, rs_s.at[2], rs_r.at[e], part).wait_recv()
            rcopy(item, item, pt_s.at[e], pt_r.at[e], part).start()

    for h in range(2):
        for i in range(2):
            sl = line(h, 3, 2 + i)
            rcopy(sl, sl, s2s.at[h, 0, 2 + i], s2r.at[h, 0, 2 + i], part).wait_recv()
            sl = line(h, 1, i)
            rcopy(sl, sl, s2s.at[h, 1, i], s2r.at[h, 1, i], part).wait_recv()
            sl = line(h, 2, i)
            rcopy(sl, sl, fs.at[h, 0, i], fr.at[h, 0, i], part).wait_recv()
            sl = line(h, 2, 2 + i)
            rcopy(sl, sl, fs.at[h, 1, i], fr.at[h, 1, i], part).wait_recv()
    for e in range(2):
        item = rowcol(2 * e + 1 - k)
        rcopy(item, item, pt_s.at[e], pt_r.at[e], part).wait_recv()
    sl = slab(0, r)
    for h in range(2):
        for d in (1, 2, 3):
            rcopy(sl, sl, s1s.at[h, d], s1r.at[h, d], part).wait_send()
        for dirn in range(2):
            for j in range(4):
                rcopy(sl, sl, s2s.at[h, dirn, j], s2r.at[h, dirn, j], part).wait_send()
            for i in range(2):
                rcopy(sl, sl, fs.at[h, dirn, i], fr.at[h, dirn, i], part).wait_send()
    item = rowcol(k)
    for e in range(2):
        rcopy(item, item, pt_s.at[e], pt_r.at[e], part).wait_send()

    @pl.when(x < 2)
    def _():
        rcopy(item, item, rs_s.at[0], rs_r.at[0], part).wait_send()
        rcopy(item, item, rs_s.at[1], rs_r.at[0], part).wait_send()

    @pl.when(x >= 2)
    def _():
        rcopy(item, item, rs_s.at[2], rs_r.at[0], part).wait_send()

    @pl.when(c < 4)
    def _():
        for q in range(16):
            @pl.when(jnp.logical_not((tc == c) & (r == q)))
            def _():
                src, dst, rsem = sc_copy(q)
                rcopy(src, dst, ssem_sc.at[q], rsem, part).wait_send()


def panel(asm):
    dma = pltpu.SemaphoreType.DMA
    return pl.pallas_call(
        panel_kernel,
        out_shape=(
            jax.ShapeDtypeStruct((8, T, 512), jnp.float32),
            jax.ShapeDtypeStruct((2, 1024, 512), jnp.float32),
        ),
        in_specs=[spec(ANY)],
        out_specs=(spec(ANY), spec(ANY)),
        scratch_shapes=[
            dma(()),
            dma((16,)),
            dma((8,)),
            dma((2, 4)),
            dma((2, 4)),
            dma((2, 2, 4)),
            dma((2, 2, 4)),
            dma((2, 2, 2)),
            dma((2, 2, 2)),
            dma((3,)),
            dma((2,)),
            dma((2,)),
            dma((2,)),
        ],
        compiler_params=pltpu.CompilerParams(collective_id=1, has_side_effects=True, vmem_limit_bytes=VLIM),
        cost_estimate=pl.CostEstimate(flops=0, bytes_accessed=1 << 26, transcendentals=0),
        name="panel",
    )(asm)


def schur_kernel(pat, rows, cols, acc, phi, plo, thi, tlo, q_ref, out, yext, cext, xh, xl, qbuf):
    r = lax.axis_index("prow")
    c = lax.axis_index("pcol")
    s = pl.program_id(0)
    f32 = jnp.float32

    def masks(i):
        e0 = pat[0, i].astype(f32)
        e1 = jnp.maximum(pat[0, i], pat[1, i]).astype(f32)
        return e0, e1

    def mm(a, b):
        return jnp.dot(a, b, preferred_element_type=f32)

    def masked(x, e):
        return jnp.concatenate([x[:, :256] * e[0], x[:, 256:] * e[1]], axis=1)

    @pl.when(s == 0)
    def _():
        off = pl.multiple_of(jnp.minimum(c, 3) * T, T)
        for a in range(8):
            hi, lo = split(masked(rows[a], masks(a * 16 + r)))
            xh[a * T : (a + 1) * T, :] = hi
            xl[a * T : (a + 1) * T, :] = lo
        y = mm(xh[...], phi[...]) + mm(xl[...], phi[...]) + mm(xh[...], plo[...])
        yh, yl = split(y)
        yext[:, 0:512] = yh
        yext[:, 512:1024] = yh
        yext[:, 1024:1536] = yl

        @pl.when(c < 4)
        def _():
            th = thi[:, pl.ds(off, T)]
            qbuf[...] = mm(xh[...], th) + mm(xl[...], th) + mm(xh[...], tlo[:, pl.ds(off, T)])

        @pl.when((c < 4) & (r < 4))
        def _():
            qbuf[0:T, :] = q_ref[pl.ds(pl.multiple_of(jnp.minimum(r, 3) * T, T), T), pl.ds(off, T)]

    for h in range(2):
        hi, lo = split(masked(cols[h], masks(s * 16 + h * 8 + c)))
        cext[h * T : (h + 1) * T, 0:512] = hi
        cext[h * T : (h + 1) * T, 512:1024] = lo
        cext[h * T : (h + 1) * T, 1024:1536] = hi
    upd = lax.dot_general(yext[...], cext[...], (((1,), (1,)), ((), ())), preferred_element_type=f32)
    for a in range(8):
        for h in range(2):
            val = acc[a, 0, h, 0] - upd[a * T : (a + 1) * T, h * T : (h + 1) * T]
            if a == 0:
                val = jnp.where(r < 4, 0.0, val)
            out[a, 0, h, 0] = val

    @pl.when((s == 0) & (c < 4))
    def _():
        for a in range(8):
            out[a, 0, 0, 0] = qbuf[a * T : (a + 1) * T, :]


def schur(pattern, rows, cols, acc, phi, plo, thi, tlo, qlead):
    full = lambda *shape: pl.BlockSpec(shape, lambda s: (0,) * len(shape))
    blk = pl.BlockSpec((8, 1, 2, 1, T, T), lambda s: (0, 0, s, 0, 0, 0))
    return pl.pallas_call(
        schur_kernel,
        grid=(8,),
        out_shape=jax.ShapeDtypeStruct((8, 1, 16, 1, T, T), jnp.float32),
        in_specs=[
            spec(pltpu.SMEM),
            full(8, T, 512),
            pl.BlockSpec((2, T, 512), lambda s: (0, s, 0)),
            blk,
            full(512, 512),
            full(512, 512),
            full(512, 512),
            full(512, 512),
            full(512, 512),
        ],
        out_specs=blk,
        scratch_shapes=[
            pltpu.VMEM((1024, 1536), jnp.bfloat16),
            pltpu.VMEM((256, 1536), jnp.bfloat16),
            pltpu.VMEM((1024, 512), jnp.bfloat16),
            pltpu.VMEM((1024, 512), jnp.bfloat16),
            pltpu.VMEM((1024, T), jnp.float32),
        ],
        compiler_params=pltpu.CompilerParams(vmem_limit_bytes=VLIM),
        cost_estimate=pl.CostEstimate(flops=7 << 30, bytes_accessed=6 << 22, transcendentals=0),
        name="schur",
    )(pattern, rows, cols, acc, phi, plo, thi, tlo, qlead)


def local(front, child_blocks, owners, slots, pattern):
    send, meta = pack(owners[:, 0], slots, child_blocks)
    blocks = front.reshape(128, T, T)
    pa, pb, pc, got, qlead, thi, tlo, phi, plo = exchange(pattern, meta, send, blocks)
    asm = assemble(got, pa, pb, pc, blocks)
    rows, cols = panel(asm.reshape(8, 16, T, T))
    return schur(
        pattern, rows, cols, asm.reshape(8, 1, 16, 1, T, T), phi, plo, thi, tlo, qlead
    )


def solution(mesh):
    placed = (
        P(None, "prow", None, "pcol", None, None),
        P(("prow", "pcol"), None, None),
        P(("prow", "pcol"), None),
        P(("prow", "pcol")),
        P(),
    )
    return jax.shard_map(
        local,
        mesh=mesh,
        in_specs=placed,
        out_specs=P(None, "prow", None, "pcol", None, None),
        check_vma=False,
    )
```

```python
import jax
import jax.numpy as jnp
from jax import lax
from jax.experimental import pallas as pl
from jax.experimental.pallas import tpu as pltpu
from jax.sharding import PartitionSpec as P

T = 128
MESH = pl.DeviceIdType.MESH
ANY = pl.ANY
VLIM = 60000 * 1024
HI = lax.Precision.HIGHEST


def spec(space):
    return pl.BlockSpec(memory_space=space)


def pack_kernel(owners, owners_v, slots_v, child, send, meta, buf, cnt, isem, osem):
    for g in range(8):
        pltpu.make_async_copy(child.at[pl.ds(g * 16, 16)], buf.at[pl.ds(g * 16, 16)], isem.at[g]).start()
    meta[...] = owners_v[...] * 128 + slots_v[...]

    def zero(i, _):
        cnt[i] = 0
        return 0

    lax.fori_loop(0, 128, zero, 0)
    for g in range(8):
        pltpu.make_async_copy(child.at[pl.ds(g * 16, 16)], buf.at[pl.ds(g * 16, 16)], isem.at[g]).wait()

        def put(i, _):
            o = owners[i]
            k = cnt[o]
            cnt[o] = k + 1
            dst = send.at[o >> 5, (o >> 3) & 3, o & 7, pl.ds(pl.multiple_of(k * T, T), T)]
            pltpu.make_async_copy(buf.at[i], dst, osem.at[i]).start()
            return 0

        lax.fori_loop(g * 16, g * 16 + 16, put, 0)

    def fin(i, _):
        pltpu.make_async_copy(buf.at[i], send.at[0, 0, 0, pl.ds(0, T)], osem.at[i]).wait()
        return 0

    lax.fori_loop(0, 128, fin, 0)


def pack(owners, slots, child):
    return pl.pallas_call(
        pack_kernel,
        out_shape=(
            jax.ShapeDtypeStruct((4, 4, 8, 256, T), jnp.float32),
            jax.ShapeDtypeStruct((1, 128), jnp.int32),
        ),
        in_specs=[spec(pltpu.SMEM), spec(pltpu.VMEM), spec(pltpu.VMEM), spec(ANY)],
        out_specs=(spec(ANY), spec(pltpu.VMEM)),
        scratch_shapes=[
            pltpu.VMEM((128, T, T), jnp.float32),
            pltpu.SMEM((128,), jnp.int32),
            pltpu.SemaphoreType.DMA((8,)),
            pltpu.SemaphoreType.DMA((128,)),
        ],
        compiler_params=pltpu.CompilerParams(vmem_limit_bytes=VLIM),
        cost_estimate=pl.CostEstimate(flops=0, bytes_accessed=2 << 23, transcendentals=0),
        name="pack",
    )(owners, owners.reshape(1, 128), slots.reshape(1, 128), child)


def assemble_kernel(slots, pa, pb, pc, front, out, acc, buf, todo, where, fsem, rsem, osem):
    def copies(i, h):
        y, z, c = i >> 6, (i >> 4) & 3, (i >> 1) & 7
        a, b, d = pa.at[z, y, c], pb.at[c, z, y], pc.at[y, c, z]
        if h == 0:
            return (
                pltpu.make_async_copy(a, buf.at[i, pl.ds(0, 88)], rsem.at[i]),
                pltpu.make_async_copy(b.at[pl.ds(0, 40)], buf.at[i, pl.ds(88, 40)], rsem.at[i]),
            )
        return (
            pltpu.make_async_copy(b.at[pl.ds(40, 48)], buf.at[i, pl.ds(0, 48)], rsem.at[i]),
            pltpu.make_async_copy(d, buf.at[i, pl.ds(48, 80)], rsem.at[i]),
        )

    for g in range(8):
        pltpu.make_async_copy(front.at[pl.ds(g * 16, 16)], acc.at[pl.ds(g * 16, 16)], fsem.at[g]).start()

    def get(n, count):
        for h in range(2):
            i = 2 * n + h
            live = slots[h, n] != 0

            @pl.when(live)
            def _():
                for cp in copies(i, h):
                    cp.start()
                todo[count] = i
                where[count] = slots[h, n]

            count = count + live.astype(jnp.int32)
        return count

    count = lax.fori_loop(0, 128, get, 0)
    for g in range(8):
        pltpu.make_async_copy(front.at[pl.ds(g * 16, 16)], acc.at[pl.ds(g * 16, 16)], fsem.at[g]).wait()

    def add(m, _):
        i = todo[m]
        s = where[m]
        pltpu.make_async_copy(front.at[0], buf.at[i], rsem.at[i]).wait()
        acc[s] = acc[s] + buf[i]
        return 0

    lax.fori_loop(0, count, add, 0)
    for g in range(8):
        pltpu.make_async_copy(acc.at[pl.ds(g * 16, 16)], out.at[pl.ds(g * 16, 16)], osem.at[g]).start()
    for g in range(8):
        pltpu.make_async_copy(acc.at[pl.ds(g * 16, 16)], out.at[pl.ds(g * 16, 16)], osem.at[g]).wait()


def assemble(slots, pa, pb, pc, front):
    return pl.pallas_call(
        assemble_kernel,
        out_shape=jax.ShapeDtypeStruct((128, T, T), jnp.float32),
        in_specs=[spec(pltpu.SMEM)] + [spec(ANY)] * 4,
        out_specs=spec(ANY),
        scratch_shapes=[
            pltpu.VMEM((128, T, T), jnp.float32),
            pltpu.VMEM((256, T, T), jnp.float32),
            pltpu.SMEM((256,), jnp.int32),
            pltpu.SMEM((256,), jnp.int32),
            pltpu.SemaphoreType.DMA((8,)),
            pltpu.SemaphoreType.DMA((256,)),
            pltpu.SemaphoreType.DMA((8,)),
        ],
        compiler_params=pltpu.CompilerParams(vmem_limit_bytes=VLIM),
        cost_estimate=pl.CostEstimate(flops=0, bytes_accessed=4 << 23, transcendentals=0),
        name="assemble",
    )(slots, pa, pb, pc, front)


def dot(a, b, ta=0, tb=0):
    dims = (((0 if ta else 1,), (1 if tb else 0,)), ((), ()))
    return lax.dot_general(a, b, dims, precision=HI, preferred_element_type=jnp.float32)


def split(x):
    hi = x.astype(jnp.bfloat16)
    lo = (x - hi.astype(jnp.float32)).astype(jnp.bfloat16)
    return hi, lo


def eliminate(a_ref, b_ref, u_ref, w_ref):
    lane = lax.broadcasted_iota(jnp.int32, (T, T), 1)
    sub = lax.broadcasted_iota(jnp.int32, (T, T), 0)
    lane1 = lax.broadcasted_iota(jnp.int32, (1, T), 1)
    sub1 = lax.broadcasted_iota(jnp.int32, (T, 1), 0)
    b_ref[...] = (lane == sub).astype(jnp.float32)

    def step(k, _):
        row = a_ref[pl.ds(k, 1), :]
        brow = b_ref[pl.ds(k, 1), :]
        mat = a_ref[...]
        d = jnp.sum(jnp.where(lane1 == k, row, 0.0), axis=1, keepdims=True)
        col = jnp.sum(jnp.where(lane == k, mat, 0.0), axis=1, keepdims=True)
        rs = 1.0 / jnp.sqrt(d)
        m = jnp.where(sub1 > k, col * (1.0 / d), 0.0)
        u_ref[pl.ds(k, 1), :] = jnp.where(lane1 >= k, row * rs, 0.0)
        w_ref[pl.ds(k, 1), :] = brow * rs
        a_ref[...] = mat - m * row
        b_ref[...] = b_ref[...] - m * brow
        return 0

    lax.fori_loop(0, T, step, 0)
    return u_ref[...].T, w_ref[...]


def sym_lower(x):
    lane = lax.broadcasted_iota(jnp.int32, (T, T), 1)
    sub = lax.broadcasted_iota(jnp.int32, (T, T), 0)
    return jnp.where(sub >= lane, x, x.T)


def factor256(g00, g10, g11, a_ref, b_ref, u_ref, w_ref, hook):
    a_ref[...] = sym_lower(g00)
    l00, w00 = eliminate(a_ref, b_ref, u_ref, w_ref)
    hook()
    l10 = dot(g10, w00, tb=1)
    a_ref[...] = sym_lower(g11 - dot(l10, l10, tb=1))
    l11, w11 = eliminate(a_ref, b_ref, u_ref, w_ref)
    hook()
    w10 = -dot(w11, dot(l10, w00))
    zero = jnp.zeros((T, T), jnp.float32)
    low = jnp.concatenate([jnp.concatenate([l00, zero], 1), jnp.concatenate([l10, l11], 1)], 0)
    inv = jnp.concatenate([jnp.concatenate([w00, zero], 1), jnp.concatenate([w10, w11], 1)], 0)
    return low, inv


def lead_factor(pat, blk, q_ref, thi, tlo, phi, plo, a_ref, b_ref, u_ref, w_ref, hook):
    low0, inv0 = factor256(blk(0, 0), blk(1, 0), blk(1, 1), a_ref, b_ref, u_ref, w_ref, hook)
    rect = jnp.concatenate(
        [jnp.concatenate([blk(2, 0), blk(2, 1)], 1), jnp.concatenate([blk(3, 0), blk(3, 1)], 1)], 0
    )
    s = dot(rect, inv0, tb=1)
    e2 = pat[0, 2].astype(jnp.float32)
    e3 = pat[0, 3].astype(jnp.float32)
    s = jnp.concatenate([s[:T] * e2, s[T:] * e3], 0)
    ss = dot(s, s, tb=1)
    low1, inv1 = factor256(
        blk(2, 2) - ss[:T, :T], blk(3, 2) - ss[T:, :T], blk(3, 3) - ss[T:, T:], a_ref, b_ref, u_ref, w_ref, hook
    )
    zero = jnp.zeros((256, 256), jnp.float32)
    q_ref[0:256, 0:256] = low0
    q_ref[0:256, 256:512] = zero
    q_ref[256:512, 0:256] = s
    q_ref[256:512, 256:512] = low1
    t01 = -dot(inv0, dot(s, inv1, ta=1, tb=1), ta=1)
    t = jnp.concatenate(
        [jnp.concatenate([inv0.T, t01], 1), jnp.concatenate([zero, inv1.T], 1)], 0
    )
    p = dot(t, t, tb=1)
    hi, lo = split(t)
    thi[...] = hi
    tlo[...] = lo
    hi, lo = split(p)
    phi[...] = hi
    plo[...] = lo


PARTS = (("c", "y", "z"), ("y", "z", "c"), ("z", "c", "y"))
NEAR = {"c": (2, 3, 6, 7, 1), "y": (1, 3), "z": (1, 3)}
FAR = {"c": (4, 5), "y": (2,), "z": (2,)}
SIZE = {"c": 8, "y": 4, "z": 4}
ROWS = (88, 88, 80)


def exchange_kernel(
    pat, meta, send, front, oa, ob, oc, slots, q_ref, thi, tlo, phi, plo,
    ba1, bb1, bc1, ba2, bb2, bc2,
    lead, meta_all, a_ref, b_ref, u_ref, w_ref,
    m0, ms, mr, f1s, f1r, f2s, f2r, f3s, f3r, l0, l1s, l1r, l2s, l2r, l4s, l4r, l5s, l5r,
):
    r = lax.axis_index("prow")
    c = lax.axis_index("pcol")
    y, z, x, k = r // 4, r % 4, c // 2, c % 2
    me = r * 8 + c
    part = (r, x * 2 + 1 - k)
    b1, b2, b3 = (ba1, bb1, bc1), (ba2, bb2, bc2), (oa, ob, oc)
    own = {"y": y, "z": z, "c": c}
    bar = pltpu.get_barrier_semaphore()

    def rcopy(src, dst, s_sem, r_sem, dev):
        return pltpu.make_async_remote_copy(
            src_ref=src, dst_ref=dst, send_sem=s_sem, recv_sem=r_sem, device_id=dev, device_id_type=MESH
        )

    def plus(ax, o):
        if ax == "c":
            return ((x + o // 2) % 4) * 2 + (k + o) % 2
        return (own[ax] + o) % 4

    def minus(ax, o):
        if ax == "c":
            return ((x + 4 - o // 2) % 4) * 2 + (k + o) % 2
        return (own[ax] + 4 - o) % 4

    def dev(ax, v):
        return {"c": (r, v), "y": (v * 4 + z, c), "z": (y * 4 + v, c)}[ax]

    for ax in ("c", "y", "z"):
        for o in NEAR[ax] + FAR[ax]:
            pl.semaphore_signal(bar, inc=1, device_id=dev(ax, plus(ax, o)), device_id_type=MESH)
    pl.semaphore_wait(bar, 13)

    def src1(n, v):
        return (
            lambda: send.at[:, :, v, pl.ds(0, 88)],
            lambda: send.at[v, :, :, pl.ds(88, 88)],
            lambda: send.at[:, v, :, pl.ds(176, 80)],
        )[n]()

    def src2(n, i, v):
        return b1[n].at[i, :, v] if n == 2 else b1[n].at[i, v]

    def src3(n, j, v):
        return b2[n].at[j, :, v]

    def first(n):
        p = PARTS[n][0]
        for o in NEAR[p] + FAR[p]:
            v = plus(p, o)
            rcopy(src1(n, v), b1[n].at[own[p]], f1s.at[n, o], f1r.at[n, own[p]], dev(p, v)).start()

    def first_own(n):
        p = PARTS[n][0]
        pltpu.make_async_copy(src1(n, own[p]), b1[n].at[own[p]], f1r.at[n, own[p]]).start()

    def second(n, i):
        q = PARTS[n][1]
        piece = b1[n].at[i]
        pltpu.make_async_copy(piece, piece, f1r.at[n, i]).wait()
        for o in NEAR[q] + FAR[q]:
            v = plus(q, o)
            rcopy(src2(n, i, v), b2[n].at[own[q], i], f2s.at[n, i, o], f2r.at[n, own[q], i], dev(q, v)).start()
        pltpu.make_async_copy(src2(n, i, own[q]), b2[n].at[own[q], i], f2r.at[n, own[q], i]).start()

    def third(n, j):
        p, q, u = PARTS[n]
        for i in range(SIZE[p]):
            piece = b2[n].at[j, i]
            pltpu.make_async_copy(piece, piece, f2r.at[n, j, i]).wait()
        for o in NEAR[u] + FAR[u]:
            v = plus(u, o)
            rcopy(src3(n, j, v), b3[n].at[own[u], j], f3s.at[n, j, o], f3r.at[n, own[u], j], dev(u, v)).start()
        pltpu.make_async_copy(src3(n, j, own[u]), b3[n].at[own[u], j], f3r.at[n, own[u], j]).start()

    def go2(offsets):
        for n in range(3):
            p = PARTS[n][0]
            for o in offsets[p]:
                second(n, minus(p, o))

    def go3(offsets):
        for n in range(3):
            q = PARTS[n][1]
            for o in offsets[q]:
                third(n, minus(q, o))

    def cset(j):
        return lead.at[j, pl.ds(j, 4 - j)]

    for j in range(4):
        @pl.when((y == 0) & (c == j) & (z >= j))
        def _():
            cp = pltpu.make_async_copy(front.at[0], lead.at[j, z], l0)
            cp.start()
            cp.wait()
            for d in (1, 2, 3):
                rcopy(lead.at[j, z], lead.at[j, z], l1s.at[d], l1r.at[z], ((z + d) % 4, c)).start()

    mcopy = pltpu.make_async_copy(meta, meta_all.at[r, pl.ds(c, 1), :], m0)
    mcopy.start()
    mcopy.wait()

    def told(stage, v):
        return (
            lambda: meta_all.at[r, pl.ds(v, 1), :],
            lambda: meta_all.at[y * 4 + v],
            lambda: meta_all.at[pl.ds(v * 4, 4)],
        )[stage]()

    def tell(stage):
        ax = "czy"[stage]
        for o in NEAR[ax] + FAR[ax]:
            row = told(stage, own[ax])
            rcopy(row, row, ms.at[stage, o], mr.at[stage, own[ax]], dev(ax, plus(ax, o))).start()

    def hear(stage):
        ax = "czy"[stage]
        for o in NEAR[ax] + FAR[ax]:
            v = minus(ax, o)
            row = told(stage, v)
            rcopy(row, row, ms.at[stage, o], mr.at[stage, v], part).wait_recv()

    tell(0)
    first(2)
    first(1)

    @pl.when(y != 0)
    def _():
        first(0)

    for n in range(3):
        first_own(n)
    for j in range(4):
        e = j // 2

        @pl.when((y == 0) & (c == j))
        def _():
            for i in range(j, 4):
                @pl.when(z != i)
                def _():
                    rcopy(lead.at[j, i], lead.at[j, i], l1s.at[0], l1r.at[i], part).wait_recv()

            rcopy(cset(j), cset(j), l2s.at[0], l2r.at[e], (r, ((x + 1) % 4) * 2 + k)).start()
            rcopy(cset(j), cset(j), l2s.at[1], l2r.at[e], (r, ((x + 3) % 4) * 2 + k)).start()

    for j in range(4):
        e = j // 2

        @pl.when((y == 0) & (k == j % 2) & ((x == (e + 1) % 4) | (x == (e + 3) % 4)))
        def _():
            rcopy(cset(j), cset(j), l2s.at[2], l2r.at[e], part).wait_recv()

        @pl.when((y == 0) & (k == j % 2) & (x == 3 - e))
        def _():
            rcopy(cset(j), cset(j), l2s.at[2], l2r.at[e], (r, (2 + e) * 2 + k)).start()

    @pl.when(y == 0)
    def _():
        first(0)

    for j in range(4):
        e = j // 2

        @pl.when((y == 0) & (k == j % 2) & (x == 2 + e))
        def _():
            rcopy(cset(j), cset(j), l2s.at[2], l2r.at[e], part).wait_recv()

        @pl.when((y == 0) & (k == j % 2))
        def _():
            for d in (1, 3, 2):
                rcopy(cset(j), cset(j), l4s.at[e, d], l4r.at[e], (d * 4 + z, c)).start()

    hear(0)
    tell(1)
    for n in range(3):
        second(n, own[PARTS[n][0]])
    go2(NEAR)
    hear(1)
    tell(2)
    go2(FAR)
    go3({"c": (0,), "y": (0,), "z": (0,)})
    for j in range(4):
        e = j // 2

        @pl.when((y != 0) & (k == j % 2))
        def _():
            rcopy(cset(j), cset(j), l4s.at[e, 0], l4r.at[e], part).wait_recv()

        @pl.when(k == j % 2)
        def _():
            rcopy(cset(j), cset(j), l5s.at[e], l5r.at[e], part).start()

    hear(2)
    mt = jnp.concatenate([meta_all[i] for i in range(16)], axis=0).astype(jnp.float32).T
    whose = jnp.floor(mt * (1.0 / 128.0))
    sl = mt - whose * 128.0
    idx = lax.broadcasted_iota(jnp.int32, (128, 128), 0).astype(jnp.float32)
    mine = whose == me.astype(jnp.float32)
    low = jnp.min(jnp.where(mine, idx, 999.0), axis=0, keepdims=True)
    high = jnp.max(jnp.where(mine, idx, -1.0), axis=0, keepdims=True)
    s0 = jnp.sum(jnp.where(mine & (idx == low), sl, 0.0), axis=0, keepdims=True)
    s1 = jnp.sum(jnp.where(mine & (idx == high) & (idx > low), sl, 0.0), axis=0, keepdims=True)
    slots[0:1, :] = s0.astype(jnp.int32)
    slots[1:2, :] = s1.astype(jnp.int32)
    for j in range(4):
        e = j // 2

        @pl.when(k != j % 2)
        def _():
            rcopy(cset(j), cset(j), l5s.at[e], l5r.at[e], part).wait_recv()

    work = [lambda: (go3(NEAR), go3(FAR))]

    def hook():
        if work:
            work.pop(0)()

    lead_factor(
        pat, lambda i, j: lead[j, i], q_ref, thi, tlo, phi, plo, a_ref, b_ref, u_ref, w_ref, hook
    )
    while work:
        hook()
    for n in range(3):
        p, q, u = PARTS[n]

        def arrived(j, _):
            for v in range(SIZE[u]):
                piece = b3[n].at[v, j]
                pltpu.make_async_copy(piece, piece, f3r.at[n, v, j]).wait()
            for o in NEAR[u] + FAR[u]:
                rcopy(src3(n, 0, 0), b3[n].at[0, 0], f3s.at[n, j, o], f3r.at[n, 0, 0], part).wait_send()
            return 0

        lax.fori_loop(0, SIZE[q], arrived, 0)
        for o in NEAR[p] + FAR[p]:
            rcopy(src1(n, 0), b1[n].at[0], f1s.at[n, o], f1r.at[n, 0], part).wait_send()

        def sent(i, _):
            for o in NEAR[q] + FAR[q]:
                rcopy(src2(n, 0, 0), b2[n].at[0, 0], f2s.at[n, i, o], f2r.at[n, 0, 0], part).wait_send()
            return 0

        lax.fori_loop(0, SIZE[p], sent, 0)

    for stage in range(3):
        ax = "czy"[stage]
        for o in NEAR[ax] + FAR[ax]:
            row = told(stage, own[ax])
            rcopy(row, row, ms.at[stage, o], mr.at[stage, 0], part).wait_send()
    for j in range(4):
        e = j // 2

        @pl.when((y == 0) & (c == j))
        def _():
            @pl.when(z >= j)
            def _():
                for d in (1, 2, 3):
                    rcopy(lead.at[j, 0], lead.at[j, 0], l1s.at[d], l1r.at[0], part).wait_send()

            rcopy(cset(j), cset(j), l2s.at[0], l2r.at[e], part).wait_send()
            rcopy(cset(j), cset(j), l2s.at[1], l2r.at[e], part).wait_send()

        @pl.when((y == 0) & (k == j % 2) & (x == 3 - e))
        def _():
            rcopy(cset(j), cset(j), l2s.at[2], l2r.at[e], part).wait_send()

        @pl.when((y == 0) & (k == j % 2))
        def _():
            for d in (1, 3, 2):
                rcopy(cset(j), cset(j), l4s.at[e, d], l4r.at[e], part).wait_send()

        @pl.when(k == j % 2)
        def _():
            rcopy(cset(j), cset(j), l5s.at[e], l5r.at[e], part).wait_send()


def exchange(pattern, meta, send, front):
    vm = spec(pltpu.VMEM)
    dma = pltpu.SemaphoreType.DMA
    bf = jax.ShapeDtypeStruct((512, 512), jnp.bfloat16)

    def buf(kind, a, b, d, n):
        return kind((a, b, d, ROWS[n], T), jnp.float32)

    return pl.pallas_call(
        exchange_kernel,
        out_shape=(
            buf(jax.ShapeDtypeStruct, 4, 4, 8, 0),
            buf(jax.ShapeDtypeStruct, 8, 4, 4, 1),
            buf(jax.ShapeDtypeStruct, 4, 8, 4, 2),
            jax.ShapeDtypeStruct((8, 128), jnp.int32),
            jax.ShapeDtypeStruct((512, 512), jnp.float32),
            bf, bf, bf, bf,
        ),
        in_specs=[spec(pltpu.SMEM), vm, spec(ANY), spec(ANY)],
        out_specs=(spec(ANY), spec(ANY), spec(ANY), vm, vm, vm, vm, vm, vm),
        scratch_shapes=[
            buf(pltpu.VMEM, 8, 4, 4, 0),
            buf(pltpu.VMEM, 4, 4, 8, 1),
            buf(pltpu.VMEM, 4, 4, 8, 2),
            buf(pltpu.VMEM, 4, 8, 4, 0),
            buf(pltpu.VMEM, 4, 4, 8, 1),
            buf(pltpu.VMEM, 8, 4, 4, 2),
            pltpu.VMEM((4, 4, T, T), jnp.float32),
            pltpu.VMEM((16, 8, 128), jnp.int32),
        ]
        + [pltpu.VMEM((T, T), jnp.float32)] * 4
        + [dma(()), dma((3, 8)), dma((3, 8)), dma((3, 8)), dma((3, 8))]
        + [dma((3, 8, 8))] * 4
        + [dma(()), dma((4,)), dma((4,)), dma((3,)), dma((2,)), dma((2, 4)), dma((2,)), dma((2,)), dma((2,))],
        compiler_params=pltpu.CompilerParams(collective_id=0, has_side_effects=True, vmem_limit_bytes=VLIM),
        name="exchange",
    )(pattern, meta, send, front)


def panel_kernel(asm, rows, cols, lsem, ssem_sc, rsem_sc, s1s, s1r, s2s, s2r, fs, fr, rs_s, rs_r, pt_s, pt_r):
    r = lax.axis_index("prow")
    c = lax.axis_index("pcol")
    y, z, x, k = r // 4, r % 4, c // 2, c % 2
    tc = r % 8
    half = r // 8
    selfhit = (c < 4) & (tc == c)
    bar = pltpu.get_barrier_semaphore()

    def sig(rr, cc):
        pl.semaphore_signal(bar, inc=1, device_id=(rr, cc), device_id_type=MESH)

    def zn(d):
        return y * 4 + (z + d) % 4

    def yn(d):
        return ((y + d) % 4) * 4 + z

    def xn(d):
        return ((x + d) % 4) * 2 + k

    for q in range(16):
        @pl.when((c < 4) & jnp.logical_not((tc == c) & (r == q)))
        def _():
            sig(q, tc)
    for h in range(2):
        for cc in range(4):
            @pl.when(jnp.logical_not((r == c + 8 * h) & (c == cc)))
            def _():
                sig(c + 8 * h, cc)
    for d in (1, 2, 3):
        sig(zn(d), c)
        sig(yn(d), c)
    sig(r, xn(1))
    sig(r, xn(3))
    sig(r, x * 2 + 1 - k)
    n_sc = jnp.where(c < 4, 16, 0) + 8 - jnp.where(selfhit, 2, 0)
    pl.semaphore_wait(bar, n_sc + 9)

    def rcopy(src, dst, ss, rs, dev):
        return pltpu.make_async_remote_copy(
            src_ref=src, dst_ref=dst, send_sem=ss, recv_sem=rs, device_id=dev, device_id_type=MESH
        )

    def sc_dst(h, q, cc):
        return cols.at[h, pl.ds(q * 64, 64), pl.ds(cc * T, T)]

    def sc_copy(q):
        src = asm.at[q // 2, 0, pl.ds((q % 2) * 64, 64), :]
        return src, sc_dst(half, q, c), rsem_sc.at[half * 4 + c]

    own = asm.at[:, 0]

    def rowcol(cc):
        return rows.at[:, :, pl.ds(pl.multiple_of(cc * T, T), T)]

    @pl.when(c < 4)
    def _():
        for q in range(16):
            src, dst, rsem = sc_copy(q)
            hit = (tc == c) & (r == q)

            @pl.when(hit)
            def _():
                pltpu.make_async_copy(src, dst, rsem).start()

            @pl.when(jnp.logical_not(hit))
            def _():
                rcopy(src, dst, ssem_sc.at[q], rsem, (q, tc)).start()

        pltpu.make_async_copy(own, rowcol(c), lsem).start()

    for e in range(2):
        @pl.when(x == e)
        def _():
            rcopy(own, rowcol(c), rs_s.at[0], rs_r.at[e], (r, xn(1))).start()
            rcopy(own, rowcol(c), rs_s.at[1], rs_r.at[e], (r, xn(3))).start()

    def slab(h, q):
        return cols.at[h, pl.ds(q * 64, 64), :]

    for h in range(2):
        nb = zn if h == 0 else yn
        for cc in range(4):
            piece = sc_dst(h, r, cc)
            pltpu.make_async_copy(piece, piece, rsem_sc.at[h * 4 + cc]).wait()
        for d in (1, 3, 2):
            rcopy(slab(h, r), slab(h, r), s1s.at[h, d], s1r.at[h, d], (nb(d), c)).start()

    part = (r, x * 2 + 1 - k)
    for e in range(2):
        item = rowcol(2 * e + k)

        @pl.when((x == (e + 1) % 4) | (x == (e + 3) % 4))
        def _():
            rcopy(item, item, rs_s.at[2], rs_r.at[e], part).wait_recv()

        @pl.when(x == 3 - e)
        def _():
            rcopy(item, item, rs_s.at[2], rs_r.at[e], (r, (2 + e) * 2 + k)).start()

        @pl.when(x == e)
        def _():
            pltpu.make_async_copy(own, rowcol(c), lsem).wait()

        @pl.when(x != 2 + e)
        def _():
            rcopy(item, item, pt_s.at[e], pt_r.at[e], part).start()

    def line(h, p, j):
        if h == 0:
            return slab(0, ((y + p) % 4) * 4 + j)
        return slab(1, j * 4 + (z + p) % 4)

    for h in range(2):
        nb1 = zn if h == 0 else yn
        nb2 = yn if h == 0 else zn
        for d in (1, 3, 2):
            got = slab(h, nb1(-d))
            rcopy(got, got, s1s.at[h, d], s1r.at[h, d], part).wait_recv()
        for j in range(4):
            jp, jm = j, (j + 2) % 4
            for dirn, jj in ((0, jp), (1, jm)):
                sl = line(h, 0, jj)
                dev = (nb2(1 if dirn == 0 else 3), c)
                rcopy(sl, sl, s2s.at[h, dirn, jj], s2r.at[h, dirn, jj], dev).start()
    for i in range(2):
        for h in range(2):
            nb2 = yn if h == 0 else zn
            sl = line(h, 3, i)
            rcopy(sl, sl, s2s.at[h, 0, i], s2r.at[h, 0, i], part).wait_recv()
            rcopy(sl, sl, fs.at[h, 0, i], fr.at[h, 0, i], (nb2(1), c)).start()
            sl = line(h, 1, 2 + i)
            rcopy(sl, sl, s2s.at[h, 1, 2 + i], s2r.at[h, 1, 2 + i], part).wait_recv()
            rcopy(sl, sl, fs.at[h, 1, i], fr.at[h, 1, i], (nb2(3), c)).start()
    for e in range(2):
        item = rowcol(2 * e + k)

        @pl.when(x == 2 + e)
        def _():
            rcopy(item, item, rs_s.at[2], rs_r.at[e], part).wait_recv()
            rcopy(item, item, pt_s.at[e], pt_r.at[e], part).start()

    for h in range(2):
        for i in range(2):
            sl = line(h, 3, 2 + i)
            rcopy(sl, sl, s2s.at[h, 0, 2 + i], s2r.at[h, 0, 2 + i], part).wait_recv()
            sl = line(h, 1, i)
            rcopy(sl, sl, s2s.at[h, 1, i], s2r.at[h, 1, i], part).wait_recv()
            sl = line(h, 2, i)
            rcopy(sl, sl, fs.at[h, 0, i], fr.at[h, 0, i], part).wait_recv()
            sl = line(h, 2, 2 + i)
            rcopy(sl, sl, fs.at[h, 1, i], fr.at[h, 1, i], part).wait_recv()
    for e in range(2):
        item = rowcol(2 * e + 1 - k)
        rcopy(item, item, pt_s.at[e], pt_r.at[e], part).wait_recv()
    sl = slab(0, r)
    for h in range(2):
        for d in (1, 2, 3):
            rcopy(sl, sl, s1s.at[h, d], s1r.at[h, d], part).wait_send()
        for dirn in range(2):
            for j in range(4):
                rcopy(sl, sl, s2s.at[h, dirn, j], s2r.at[h, dirn, j], part).wait_send()
            for i in range(2):
                rcopy(sl, sl, fs.at[h, dirn, i], fr.at[h, dirn, i], part).wait_send()
    item = rowcol(k)
    for e in range(2):
        rcopy(item, item, pt_s.at[e], pt_r.at[e], part).wait_send()

    @pl.when(x < 2)
    def _():
        rcopy(item, item, rs_s.at[0], rs_r.at[0], part).wait_send()
        rcopy(item, item, rs_s.at[1], rs_r.at[0], part).wait_send()

    @pl.when(x >= 2)
    def _():
        rcopy(item, item, rs_s.at[2], rs_r.at[0], part).wait_send()

    @pl.when(c < 4)
    def _():
        for q in range(16):
            @pl.when(jnp.logical_not((tc == c) & (r == q)))
            def _():
                src, dst, rsem = sc_copy(q)
                rcopy(src, dst, ssem_sc.at[q], rsem, part).wait_send()


def panel(asm):
    dma = pltpu.SemaphoreType.DMA
    return pl.pallas_call(
        panel_kernel,
        out_shape=(
            jax.ShapeDtypeStruct((8, T, 512), jnp.float32),
            jax.ShapeDtypeStruct((2, 1024, 512), jnp.float32),
        ),
        in_specs=[spec(ANY)],
        out_specs=(spec(ANY), spec(ANY)),
        scratch_shapes=[
            dma(()),
            dma((16,)),
            dma((8,)),
            dma((2, 4)),
            dma((2, 4)),
            dma((2, 2, 4)),
            dma((2, 2, 4)),
            dma((2, 2, 2)),
            dma((2, 2, 2)),
            dma((3,)),
            dma((2,)),
            dma((2,)),
            dma((2,)),
        ],
        compiler_params=pltpu.CompilerParams(collective_id=1, has_side_effects=True, vmem_limit_bytes=VLIM),
        cost_estimate=pl.CostEstimate(flops=0, bytes_accessed=1 << 26, transcendentals=0),
        name="panel",
    )(asm)


def schur_kernel(pat, rows, cols, acc, phi, plo, thi, tlo, q_ref, out, yext, cext, xh, xl, qbuf):
    r = lax.axis_index("prow")
    c = lax.axis_index("pcol")
    s = pl.program_id(0)
    f32 = jnp.float32

    def masks(i):
        e0 = pat[0, i].astype(f32)
        e1 = jnp.maximum(pat[0, i], pat[1, i]).astype(f32)
        return e0, e1

    def mm(a, b):
        return jnp.dot(a, b, preferred_element_type=f32)

    def masked(x, e):
        return jnp.concatenate([x[:, :256] * e[0], x[:, 256:] * e[1]], axis=1)

    @pl.when(s == 0)
    def _():
        off = pl.multiple_of(jnp.minimum(c, 3) * T, T)
        for a in range(8):
            hi, lo = split(masked(rows[a], masks(a * 16 + r)))
            xh[a * T : (a + 1) * T, :] = hi
            xl[a * T : (a + 1) * T, :] = lo
        y = mm(xh[...], phi[...]) + mm(xl[...], phi[...]) + mm(xh[...], plo[...])
        yh, yl = split(y)
        yext[:, 0:512] = yh
        yext[:, 512:1024] = yh
        yext[:, 1024:1536] = yl

        @pl.when(c < 4)
        def _():
            th = thi[:, pl.ds(off, T)]
            qbuf[...] = mm(xh[...], th) + mm(xl[...], th) + mm(xh[...], tlo[:, pl.ds(off, T)])

        @pl.when((c < 4) & (r < 4))
        def _():
            qbuf[0:T, :] = q_ref[pl.ds(pl.multiple_of(jnp.minimum(r, 3) * T, T), T), pl.ds(off, T)]

    for h in range(2):
        hi, lo = split(masked(cols[h], masks(s * 16 + h * 8 + c)))
        cext[h * T : (h + 1) * T, 0:512] = hi
        cext[h * T : (h + 1) * T, 512:1024] = lo
        cext[h * T : (h + 1) * T, 1024:1536] = hi
    upd = lax.dot_general(yext[...], cext[...], (((1,), (1,)), ((), ())), preferred_element_type=f32)
    for a in range(8):
        for h in range(2):
            val = acc[a, 0, h, 0] - upd[a * T : (a + 1) * T, h * T : (h + 1) * T]
            if a == 0:
                val = jnp.where(r < 4, 0.0, val)
            out[a, 0, h, 0] = val

    @pl.when((s == 0) & (c < 4))
    def _():
        for a in range(8):
            out[a, 0, 0, 0] = qbuf[a * T : (a + 1) * T, :]


def schur(pattern, rows, cols, acc, phi, plo, thi, tlo, qlead):
    full = lambda *shape: pl.BlockSpec(shape, lambda s: (0,) * len(shape))
    blk = pl.BlockSpec((8, 1, 2, 1, T, T), lambda s: (0, 0, s, 0, 0, 0))
    return pl.pallas_call(
        schur_kernel,
        grid=(8,),
        out_shape=jax.ShapeDtypeStruct((8, 1, 16, 1, T, T), jnp.float32),
        in_specs=[
            spec(pltpu.SMEM),
            full(8, T, 512),
            pl.BlockSpec((2, T, 512), lambda s: (0, s, 0)),
            blk,
            full(512, 512),
            full(512, 512),
            full(512, 512),
            full(512, 512),
            full(512, 512),
        ],
        out_specs=blk,
        scratch_shapes=[
            pltpu.VMEM((1024, 1536), jnp.bfloat16),
            pltpu.VMEM((256, 1536), jnp.bfloat16),
            pltpu.VMEM((1024, 512), jnp.bfloat16),
            pltpu.VMEM((1024, 512), jnp.bfloat16),
            pltpu.VMEM((1024, T), jnp.float32),
        ],
        compiler_params=pltpu.CompilerParams(vmem_limit_bytes=VLIM),
        cost_estimate=pl.CostEstimate(flops=7 << 30, bytes_accessed=6 << 22, transcendentals=0),
        name="schur",
    )(pattern, rows, cols, acc, phi, plo, thi, tlo, qlead)


def local(front, child_blocks, owners, slots, pattern):
    send, meta = pack(owners[:, 0], slots, child_blocks)
    blocks = front.reshape(128, T, T)
    pa, pb, pc, got, qlead, thi, tlo, phi, plo = exchange(pattern, meta, send, blocks)
    asm = assemble(got, pa, pb, pc, blocks)
    rows, cols = panel(asm.reshape(8, 16, T, T))
    return schur(
        pattern, rows, cols, asm.reshape(8, 1, 16, 1, T, T), phi, plo, thi, tlo, qlead
    )


def solution(mesh):
    placed = (
        P(None, "prow", None, "pcol", None, None),
        P(("prow", "pcol"), None, None),
        P(("prow", "pcol"), None),
        P(("prow", "pcol")),
        P(),
    )
    return jax.shard_map(
        local,
        mesh=mesh,
        in_specs=placed,
        out_specs=P(None, "prow", None, "pcol", None, None),
        check_vma=False,
    )
```

```python
import jax
import jax.numpy as jnp
from jax import lax
from jax.experimental import pallas as pl
from jax.experimental.pallas import tpu as pltpu
from jax.sharding import PartitionSpec as P

T = 128
MESH = pl.DeviceIdType.MESH
ANY = pl.ANY
VLIM = 60000 * 1024
HI = lax.Precision.HIGHEST


def spec(space):
    return pl.BlockSpec(memory_space=space)


def pack_kernel(owners, owners_v, slots_v, child, send, meta, buf, cnt, dest, isem, osem):
    for g in range(8):
        pltpu.make_async_copy(child.at[pl.ds(g * 16, 16)], buf.at[pl.ds(g * 16, 16)], isem.at[g]).start()
    meta[...] = owners_v[...] * 128 + slots_v[...]

    def zero(i, _):
        cnt[i] = 0
        return 0

    lax.fori_loop(0, 128, zero, 0, unroll=8)

    def place(i, _):
        o = owners[i]
        k = cnt[o]
        cnt[o] = k + 1
        dest[i] = o * 2 + k
        return 0

    lax.fori_loop(0, 128, place, 0, unroll=4)
    for g in range(8):
        pltpu.make_async_copy(child.at[pl.ds(g * 16, 16)], buf.at[pl.ds(g * 16, 16)], isem.at[g]).wait()

        def put(i, _):
            d = dest[i]
            rows = pl.ds(pl.multiple_of((d & 1) * T, T), T)
            dst = send.at[d >> 6, (d >> 4) & 3, (d >> 1) & 7, rows]
            pltpu.make_async_copy(buf.at[i], dst, osem.at[i]).start()
            return 0

        lax.fori_loop(g * 16, g * 16 + 16, put, 0, unroll=4)

    def fin(i, _):
        pltpu.make_async_copy(buf.at[i], send.at[0, 0, 0, pl.ds(0, T)], osem.at[i]).wait()
        return 0

    lax.fori_loop(0, 128, fin, 0, unroll=8)


def pack(owners, slots, child):
    return pl.pallas_call(
        pack_kernel,
        out_shape=(
            jax.ShapeDtypeStruct((4, 4, 8, 256, T), jnp.float32),
            jax.ShapeDtypeStruct((1, 128), jnp.int32),
        ),
        in_specs=[spec(pltpu.SMEM), spec(pltpu.VMEM), spec(pltpu.VMEM), spec(ANY)],
        out_specs=(spec(ANY), spec(pltpu.VMEM)),
        scratch_shapes=[
            pltpu.VMEM((128, T, T), jnp.float32),
            pltpu.SMEM((128,), jnp.int32),
            pltpu.SMEM((128,), jnp.int32),
            pltpu.SemaphoreType.DMA((8,)),
            pltpu.SemaphoreType.DMA((128,)),
        ],
        compiler_params=pltpu.CompilerParams(vmem_limit_bytes=VLIM),
        cost_estimate=pl.CostEstimate(flops=0, bytes_accessed=2 << 23, transcendentals=0),
        name="pack",
    )(owners, owners.reshape(1, 128), slots.reshape(1, 128), child)


def piece_copies(pa, pb, pc, buf, rsem, i, h):
    y, z, c = i >> 6, (i >> 4) & 3, (i >> 1) & 7
    a, b, d = pa.at[z, y, c], pb.at[c, z, y], pc.at[y, c, z]
    if h == 0:
        return (
            pltpu.make_async_copy(a, buf.at[i, pl.ds(0, 88)], rsem.at[i]),
            pltpu.make_async_copy(b.at[pl.ds(0, 40)], buf.at[i, pl.ds(88, 40)], rsem.at[i]),
        )
    return (
        pltpu.make_async_copy(b.at[pl.ds(40, 48)], buf.at[i, pl.ds(0, 48)], rsem.at[i]),
        pltpu.make_async_copy(d, buf.at[i, pl.ds(48, 80)], rsem.at[i]),
    )


def fetch_children(slots, pa, pb, pc, buf, todo, where, rsem, only_panel):
    def get(n, count):
        for h in range(2):
            i = 2 * n + h
            slot = slots[h, n]
            live = slot != 0
            if only_panel:
                live = live & ((slot & 15) == 0)

            @pl.when(live)
            def _():
                for cp in piece_copies(pa, pb, pc, buf, rsem, i, h):
                    cp.start()
                todo[count] = i
                where[count] = (slot >> 4) if only_panel else slot

            count = count + live.astype(jnp.int32)
        return count

    return lax.fori_loop(0, 128, get, 0, unroll=2)


def add_children(count, front, acc, buf, todo, where, rsem):
    def add(m, _):
        i = todo[m]
        s = where[m]
        pltpu.make_async_copy(front.at[0], buf.at[i], rsem.at[i]).wait()
        acc[s] = acc[s] + buf[i]
        return 0

    lax.fori_loop(0, count, add, 0)


CHILD_SCRATCH = [
    pltpu.VMEM((256, T, T), jnp.float32),
    pltpu.SMEM((256,), jnp.int32),
    pltpu.SMEM((256,), jnp.int32),
    pltpu.SemaphoreType.DMA((8,)),
    pltpu.SemaphoreType.DMA((256,)),
]


def assemble_kernel(slots, pa, pb, pc, front, acc, buf, todo, where, fsem, rsem):
    for a in range(8):
        pltpu.make_async_copy(front.at[a * 16], acc.at[a], fsem.at[a]).start()
    count = fetch_children(slots, pa, pb, pc, buf, todo, where, rsem, True)
    for a in range(8):
        pltpu.make_async_copy(front.at[a * 16], acc.at[a], fsem.at[a]).wait()
    add_children(count, front, acc, buf, todo, where, rsem)


def assemble_panel(slots, pa, pb, pc, front):
    return pl.pallas_call(
        assemble_kernel,
        out_shape=jax.ShapeDtypeStruct((8, T, T), jnp.float32),
        in_specs=[spec(pltpu.SMEM)] + [spec(ANY)] * 4,
        out_specs=spec(pltpu.VMEM),
        scratch_shapes=CHILD_SCRATCH,
        compiler_params=pltpu.CompilerParams(vmem_limit_bytes=VLIM),
        cost_estimate=pl.CostEstimate(flops=0, bytes_accessed=1 << 20, transcendentals=0),
        name="assemble_panel",
    )(slots, pa, pb, pc, front)


def dot(a, b, ta=0, tb=0):
    dims = (((0 if ta else 1,), (1 if tb else 0,)), ((), ()))
    return lax.dot_general(a, b, dims, precision=HI, preferred_element_type=jnp.float32)


def split(x):
    hi = x.astype(jnp.bfloat16)
    lo = (x - hi.astype(jnp.float32)).astype(jnp.bfloat16)
    return hi, lo


def eliminate(a_ref, b_ref, u_ref, w_ref):
    lane = lax.broadcasted_iota(jnp.int32, (T, T), 1)
    sub = lax.broadcasted_iota(jnp.int32, (T, T), 0)
    lane1 = lax.broadcasted_iota(jnp.int32, (1, T), 1)
    sub1 = lax.broadcasted_iota(jnp.int32, (T, 1), 0)
    b_ref[...] = (lane == sub).astype(jnp.float32)

    def step(k, _):
        row = a_ref[pl.ds(k, 1), :]
        brow = b_ref[pl.ds(k, 1), :]
        mat = a_ref[...]
        d = jnp.sum(jnp.where(lane1 == k, row, 0.0), axis=1, keepdims=True)
        col = jnp.sum(jnp.where(lane == k, mat, 0.0), axis=1, keepdims=True)
        rs = 1.0 / jnp.sqrt(d)
        m = jnp.where(sub1 > k, col * (1.0 / d), 0.0)
        u_ref[pl.ds(k, 1), :] = jnp.where(lane1 >= k, row * rs, 0.0)
        w_ref[pl.ds(k, 1), :] = brow * rs
        a_ref[...] = mat - m * row
        b_ref[...] = b_ref[...] - m * brow
        return 0

    lax.fori_loop(0, T, step, 0)
    return u_ref[...].T, w_ref[...]


def sym_lower(x):
    lane = lax.broadcasted_iota(jnp.int32, (T, T), 1)
    sub = lax.broadcasted_iota(jnp.int32, (T, T), 0)
    return jnp.where(sub >= lane, x, x.T)


def factor256(g00, g10, g11, a_ref, b_ref, u_ref, w_ref, hook):
    a_ref[...] = sym_lower(g00)
    l00, w00 = eliminate(a_ref, b_ref, u_ref, w_ref)
    hook()
    l10 = dot(g10, w00, tb=1)
    a_ref[...] = sym_lower(g11 - dot(l10, l10, tb=1))
    l11, w11 = eliminate(a_ref, b_ref, u_ref, w_ref)
    hook()
    w10 = -dot(w11, dot(l10, w00))
    zero = jnp.zeros((T, T), jnp.float32)
    low = jnp.concatenate([jnp.concatenate([l00, zero], 1), jnp.concatenate([l10, l11], 1)], 0)
    inv = jnp.concatenate([jnp.concatenate([w00, zero], 1), jnp.concatenate([w10, w11], 1)], 0)
    return low, inv


def lead_factor(pat, blk, q_ref, thi, tlo, phi, plo, a_ref, b_ref, u_ref, w_ref, hook):
    low0, inv0 = factor256(blk(0, 0), blk(1, 0), blk(1, 1), a_ref, b_ref, u_ref, w_ref, hook)
    rect = jnp.concatenate(
        [jnp.concatenate([blk(2, 0), blk(2, 1)], 1), jnp.concatenate([blk(3, 0), blk(3, 1)], 1)], 0
    )
    s = dot(rect, inv0, tb=1)
    e2 = pat[0, 2].astype(jnp.float32)
    e3 = pat[0, 3].astype(jnp.float32)
    s = jnp.concatenate([s[:T] * e2, s[T:] * e3], 0)
    ss = dot(s, s, tb=1)
    low1, inv1 = factor256(
        blk(2, 2) - ss[:T, :T], blk(3, 2) - ss[T:, :T], blk(3, 3) - ss[T:, T:], a_ref, b_ref, u_ref, w_ref, hook
    )
    zero = jnp.zeros((256, 256), jnp.float32)
    q_ref[0:256, 0:256] = low0
    q_ref[0:256, 256:512] = zero
    q_ref[256:512, 0:256] = s
    q_ref[256:512, 256:512] = low1
    t01 = -dot(inv0, dot(s, inv1, ta=1, tb=1), ta=1)
    t = jnp.concatenate(
        [jnp.concatenate([inv0.T, t01], 1), jnp.concatenate([zero, inv1.T], 1)], 0
    )
    p = dot(t, t, tb=1)
    hi, lo = split(t)
    thi[...] = hi
    tlo[...] = lo
    hi, lo = split(p)
    phi[...] = hi
    plo[...] = lo


PARTS = (("c", "y", "z"), ("y", "z", "c"), ("z", "c", "y"))
NEAR = {"c": (2, 3, 6, 7, 1), "y": (1, 3), "z": (1, 3)}
FAR = {"c": (4, 5), "y": (2,), "z": (2,)}
SIZE = {"c": 8, "y": 4, "z": 4}
ROWS = (88, 88, 80)


def exchange_kernel(
    pat, meta, send, front, oa, ob, oc, slots, q_ref, thi, tlo, phi, plo,
    ba1, bb1, bc1, ba2, bb2, bc2,
    lead, meta_all, a_ref, b_ref, u_ref, w_ref,
    m0, ms, mr, f1s, f1r, f2s, f2r, f3s, f3r, l0, l1s, l1r, l2s, l2r, l4s, l4r, l5s, l5r,
):
    r = lax.axis_index("prow")
    c = lax.axis_index("pcol")
    y, z, x, k = r // 4, r % 4, c // 2, c % 2
    me = r * 8 + c
    part = (r, x * 2 + 1 - k)
    b1, b2, b3 = (ba1, bb1, bc1), (ba2, bb2, bc2), (oa, ob, oc)
    own = {"y": y, "z": z, "c": c}
    bar = pltpu.get_barrier_semaphore()

    def rcopy(src, dst, s_sem, r_sem, dev):
        return pltpu.make_async_remote_copy(
            src_ref=src, dst_ref=dst, send_sem=s_sem, recv_sem=r_sem, device_id=dev, device_id_type=MESH
        )

    def plus(ax, o):
        if ax == "c":
            return ((x + o // 2) % 4) * 2 + (k + o) % 2
        return (own[ax] + o) % 4

    def minus(ax, o):
        if ax == "c":
            return ((x + 4 - o // 2) % 4) * 2 + (k + o) % 2
        return (own[ax] + 4 - o) % 4

    def dev(ax, v):
        return {"c": (r, v), "y": (v * 4 + z, c), "z": (y * 4 + v, c)}[ax]

    for ax in ("c", "y", "z"):
        for o in NEAR[ax] + FAR[ax]:
            pl.semaphore_signal(bar, inc=1, device_id=dev(ax, plus(ax, o)), device_id_type=MESH)
    pl.semaphore_wait(bar, 13)

    def src1(n, v):
        return (
            lambda: send.at[:, :, v, pl.ds(0, 88)],
            lambda: send.at[v, :, :, pl.ds(88, 88)],
            lambda: send.at[:, v, :, pl.ds(176, 80)],
        )[n]()

    def src2(n, i, v):
        return b1[n].at[i, :, v] if n == 2 else b1[n].at[i, v]

    def src3(n, j, v):
        return b2[n].at[j, :, v]

    def first(n):
        p = PARTS[n][0]
        for o in NEAR[p] + FAR[p]:
            v = plus(p, o)
            rcopy(src1(n, v), b1[n].at[own[p]], f1s.at[n, o], f1r.at[n, own[p]], dev(p, v)).start()

    def first_own(n):
        p = PARTS[n][0]
        pltpu.make_async_copy(src1(n, own[p]), b1[n].at[own[p]], f1r.at[n, own[p]]).start()

    def second(n, i):
        q = PARTS[n][1]
        piece = b1[n].at[i]
        pltpu.make_async_copy(piece, piece, f1r.at[n, i]).wait()
        for o in NEAR[q] + FAR[q]:
            v = plus(q, o)
            rcopy(src2(n, i, v), b2[n].at[own[q], i], f2s.at[n, i, o], f2r.at[n, own[q], i], dev(q, v)).start()
        pltpu.make_async_copy(src2(n, i, own[q]), b2[n].at[own[q], i], f2r.at[n, own[q], i]).start()

    def third(n, j):
        p, q, u = PARTS[n]
        for i in range(SIZE[p]):
            piece = b2[n].at[j, i]
            pltpu.make_async_copy(piece, piece, f2r.at[n, j, i]).wait()
        for o in NEAR[u] + FAR[u]:
            v = plus(u, o)
            rcopy(src3(n, j, v), b3[n].at[own[u], j], f3s.at[n, j, o], f3r.at[n, own[u], j], dev(u, v)).start()
        pltpu.make_async_copy(src3(n, j, own[u]), b3[n].at[own[u], j], f3r.at[n, own[u], j]).start()

    def go2(offsets):
        for n in range(3):
            p = PARTS[n][0]
            for o in offsets[p]:
                second(n, minus(p, o))

    def go3(offsets):
        for n in range(3):
            q = PARTS[n][1]
            for o in offsets[q]:
                third(n, minus(q, o))

    def cset(j):
        return lead.at[j, pl.ds(j, 4 - j)]

    for j in range(4):
        @pl.when((y == 0) & (c == j) & (z >= j))
        def _():
            cp = pltpu.make_async_copy(front.at[0], lead.at[j, z], l0)
            cp.start()
            cp.wait()
            for d in (1, 2, 3):
                rcopy(lead.at[j, z], lead.at[j, z], l1s.at[d], l1r.at[z], ((z + d) % 4, c)).start()

    mcopy = pltpu.make_async_copy(meta, meta_all.at[r, pl.ds(c, 1), :], m0)
    mcopy.start()
    mcopy.wait()

    def told(stage, v):
        return (
            lambda: meta_all.at[r, pl.ds(v, 1), :],
            lambda: meta_all.at[y * 4 + v],
            lambda: meta_all.at[pl.ds(v * 4, 4)],
        )[stage]()

    def tell(stage):
        ax = "czy"[stage]
        for o in NEAR[ax] + FAR[ax]:
            row = told(stage, own[ax])
            rcopy(row, row, ms.at[stage, o], mr.at[stage, own[ax]], dev(ax, plus(ax, o))).start()

    def hear(stage):
        ax = "czy"[stage]
        for o in NEAR[ax] + FAR[ax]:
            v = minus(ax, o)
            row = told(stage, v)
            rcopy(row, row, ms.at[stage, o], mr.at[stage, v], part).wait_recv()

    tell(0)
    first(2)
    first(1)

    @pl.when(y != 0)
    def _():
        first(0)

    for n in range(3):
        first_own(n)
    for j in range(4):
        e = j // 2

        @pl.when((y == 0) & (c == j))
        def _():
            for i in range(j, 4):
                @pl.when(z != i)
                def _():
                    rcopy(lead.at[j, i], lead.at[j, i], l1s.at[0], l1r.at[i], part).wait_recv()

            rcopy(cset(j), cset(j), l2s.at[0], l2r.at[e], (r, ((x + 1) % 4) * 2 + k)).start()
            rcopy(cset(j), cset(j), l2s.at[1], l2r.at[e], (r, ((x + 3) % 4) * 2 + k)).start()

    for j in range(4):
        e = j // 2

        @pl.when((y == 0) & (k == j % 2) & ((x == (e + 1) % 4) | (x == (e + 3) % 4)))
        def _():
            rcopy(cset(j), cset(j), l2s.at[2], l2r.at[e], part).wait_recv()

        @pl.when((y == 0) & (k == j % 2) & (x == 3 - e))
        def _():
            rcopy(cset(j), cset(j), l2s.at[2], l2r.at[e], (r, (2 + e) * 2 + k)).start()

    @pl.when(y == 0)
    def _():
        first(0)

    for j in range(4):
        e = j // 2

        @pl.when((y == 0) & (k == j % 2) & (x == 2 + e))
        def _():
            rcopy(cset(j), cset(j), l2s.at[2], l2r.at[e], part).wait_recv()

        @pl.when((y == 0) & (k == j % 2))
        def _():
            for d in (1, 3, 2):
                rcopy(cset(j), cset(j), l4s.at[e, d], l4r.at[e], (d * 4 + z, c)).start()

    hear(0)
    tell(1)
    for n in range(3):
        second(n, own[PARTS[n][0]])
    go2(NEAR)
    hear(1)
    tell(2)
    go2(FAR)
    go3({"c": (0,), "y": (0,), "z": (0,)})
    for j in range(4):
        e = j // 2

        @pl.when((y != 0) & (k == j % 2))
        def _():
            rcopy(cset(j), cset(j), l4s.at[e, 0], l4r.at[e], part).wait_recv()

        @pl.when(k == j % 2)
        def _():
            rcopy(cset(j), cset(j), l5s.at[e], l5r.at[e], part).start()

    hear(2)
    mt = jnp.concatenate([meta_all[i] for i in range(16)], axis=0).astype(jnp.float32).T
    whose = jnp.floor(mt * (1.0 / 128.0))
    sl = mt - whose * 128.0
    idx = lax.broadcasted_iota(jnp.int32, (128, 128), 0).astype(jnp.float32)
    mine = whose == me.astype(jnp.float32)
    low = jnp.min(jnp.where(mine, idx, 999.0), axis=0, keepdims=True)
    high = jnp.max(jnp.where(mine, idx, -1.0), axis=0, keepdims=True)
    s0 = jnp.sum(jnp.where(mine & (idx == low), sl, 0.0), axis=0, keepdims=True)
    s1 = jnp.sum(jnp.where(mine & (idx == high) & (idx > low), sl, 0.0), axis=0, keepdims=True)
    slots[0:1, :] = s0.astype(jnp.int32)
    slots[1:2, :] = s1.astype(jnp.int32)
    for j in range(4):
        e = j // 2

        @pl.when(k != j % 2)
        def _():
            rcopy(cset(j), cset(j), l5s.at[e], l5r.at[e], part).wait_recv()

    work = [lambda: (go3(NEAR), go3(FAR))]

    def hook():
        if work:
            work.pop(0)()

    lead_factor(
        pat, lambda i, j: lead[j, i], q_ref, thi, tlo, phi, plo, a_ref, b_ref, u_ref, w_ref, hook
    )
    while work:
        hook()
    for n in range(3):
        p, q, u = PARTS[n]

        def arrived(j, _):
            for v in range(SIZE[u]):
                piece = b3[n].at[v, j]
                pltpu.make_async_copy(piece, piece, f3r.at[n, v, j]).wait()
            for o in NEAR[u] + FAR[u]:
                rcopy(src3(n, 0, 0), b3[n].at[0, 0], f3s.at[n, j, o], f3r.at[n, 0, 0], part).wait_send()
            return 0

        lax.fori_loop(0, SIZE[q], arrived, 0)
        for o in NEAR[p] + FAR[p]:
            rcopy(src1(n, 0), b1[n].at[0], f1s.at[n, o], f1r.at[n, 0], part).wait_send()

        def sent(i, _):
            for o in NEAR[q] + FAR[q]:
                rcopy(src2(n, 0, 0), b2[n].at[0, 0], f2s.at[n, i, o], f2r.at[n, 0, 0], part).wait_send()
            return 0

        lax.fori_loop(0, SIZE[p], sent, 0)

    for stage in range(3):
        ax = "czy"[stage]
        for o in NEAR[ax] + FAR[ax]:
            row = told(stage, own[ax])
            rcopy(row, row, ms.at[stage, o], mr.at[stage, 0], part).wait_send()
    for j in range(4):
        e = j // 2

        @pl.when((y == 0) & (c == j))
        def _():
            @pl.when(z >= j)
            def _():
                for d in (1, 2, 3):
                    rcopy(lead.at[j, 0], lead.at[j, 0], l1s.at[d], l1r.at[0], part).wait_send()

            rcopy(cset(j), cset(j), l2s.at[0], l2r.at[e], part).wait_send()
            rcopy(cset(j), cset(j), l2s.at[1], l2r.at[e], part).wait_send()

        @pl.when((y == 0) & (k == j % 2) & (x == 3 - e))
        def _():
            rcopy(cset(j), cset(j), l2s.at[2], l2r.at[e], part).wait_send()

        @pl.when((y == 0) & (k == j % 2))
        def _():
            for d in (1, 3, 2):
                rcopy(cset(j), cset(j), l4s.at[e, d], l4r.at[e], part).wait_send()

        @pl.when(k == j % 2)
        def _():
            rcopy(cset(j), cset(j), l5s.at[e], l5r.at[e], part).wait_send()


def exchange(pattern, meta, send, front):
    vm = spec(pltpu.VMEM)
    dma = pltpu.SemaphoreType.DMA
    bf = jax.ShapeDtypeStruct((512, 512), jnp.bfloat16)

    def buf(kind, a, b, d, n):
        return kind((a, b, d, ROWS[n], T), jnp.float32)

    return pl.pallas_call(
        exchange_kernel,
        out_shape=(
            buf(jax.ShapeDtypeStruct, 4, 4, 8, 0),
            buf(jax.ShapeDtypeStruct, 8, 4, 4, 1),
            buf(jax.ShapeDtypeStruct, 4, 8, 4, 2),
            jax.ShapeDtypeStruct((8, 128), jnp.int32),
            jax.ShapeDtypeStruct((512, 512), jnp.float32),
            bf, bf, bf, bf,
        ),
        in_specs=[spec(pltpu.SMEM), vm, spec(ANY), spec(ANY)],
        out_specs=(spec(ANY), spec(ANY), spec(ANY), vm, vm, vm, vm, vm, vm),
        scratch_shapes=[
            buf(pltpu.VMEM, 8, 4, 4, 0),
            buf(pltpu.VMEM, 4, 4, 8, 1),
            buf(pltpu.VMEM, 4, 4, 8, 2),
            buf(pltpu.VMEM, 4, 8, 4, 0),
            buf(pltpu.VMEM, 4, 4, 8, 1),
            buf(pltpu.VMEM, 8, 4, 4, 2),
            pltpu.VMEM((4, 4, T, T), jnp.float32),
            pltpu.VMEM((16, 8, 128), jnp.int32),
        ]
        + [pltpu.VMEM((T, T), jnp.float32)] * 4
        + [dma(()), dma((3, 8)), dma((3, 8)), dma((3, 8)), dma((3, 8))]
        + [dma((3, 8, 8))] * 4
        + [dma(()), dma((4,)), dma((4,)), dma((3,)), dma((2,)), dma((2, 4)), dma((2,)), dma((2,)), dma((2,))],
        compiler_params=pltpu.CompilerParams(collective_id=0, has_side_effects=True, vmem_limit_bytes=VLIM),
        name="exchange",
    )(pattern, meta, send, front)


UP, DOWN = (0, 1), (3, 2)


def panel_kernel(asm, rows, cols, lsem, ssem_sc, rsem_sc, s1s, s1r, s2s, s2r, fs, fr, rs_s, rs_r, pt_s, pt_r):
    r = lax.axis_index("prow")
    c = lax.axis_index("pcol")
    y, z, x, k = r // 4, r % 4, c // 2, c % 2
    tc = r % 8
    half = r // 8
    selfhit = (c < 4) & (tc == c)
    bar = pltpu.get_barrier_semaphore()

    def sig(rr, cc):
        pl.semaphore_signal(bar, inc=1, device_id=(rr, cc), device_id_type=MESH)

    def zn(d):
        return y * 4 + (z + d) % 4

    def yn(d):
        return ((y + d) % 4) * 4 + z

    def xn(d):
        return ((x + d) % 4) * 2 + k

    for q in range(16):
        @pl.when((c < 4) & jnp.logical_not((tc == c) & (r == q)))
        def _():
            sig(q, tc)
    for h in range(2):
        for cc in range(4):
            @pl.when(jnp.logical_not((r == c + 8 * h) & (c == cc)))
            def _():
                sig(c + 8 * h, cc)
    for d in (1, 2, 3):
        sig(zn(d), c)
        sig(yn(d), c)
    sig(r, xn(1))
    sig(r, xn(3))
    sig(r, x * 2 + 1 - k)
    n_sc = jnp.where(c < 4, 16, 0) + 8 - jnp.where(selfhit, 2, 0)
    pl.semaphore_wait(bar, n_sc + 9)

    def rcopy(src, dst, ss, rs, dev):
        return pltpu.make_async_remote_copy(
            src_ref=src, dst_ref=dst, send_sem=ss, recv_sem=rs, device_id=dev, device_id_type=MESH
        )

    def sc_dst(h, q, cc):
        return cols.at[h, pl.ds(q * 64, 64), pl.ds(cc * T, T)]

    def sc_copy(q):
        src = asm.at[q // 2, pl.ds((q % 2) * 64, 64), :]
        return src, sc_dst(half, q, c), rsem_sc.at[half * 4 + c]

    own = asm
    part = (r, x * 2 + 1 - k)

    def rowcol(cc):
        return rows.at[:, :, pl.ds(pl.multiple_of(cc * T, T), T)]

    def chunk(cc, g):
        return rows.at[pl.ds(2 * g, 2), :, pl.ds(pl.multiple_of(cc * T, T), T)]

    @pl.when(c < 4)
    def _():
        for q in range(16):
            src, dst, rsem = sc_copy(q)
            hit = (tc == c) & (r == q)

            @pl.when(hit)
            def _():
                pltpu.make_async_copy(src, dst, rsem).start()

            @pl.when(jnp.logical_not(hit))
            def _():
                rcopy(src, dst, ssem_sc.at[q], rsem, (q, tc)).start()

        pltpu.make_async_copy(own, rowcol(c), lsem).start()

    for e in range(2):
        @pl.when(x == e)
        def _():
            for g in range(4):
                src, dst = own.at[pl.ds(2 * g, 2)], chunk(c, g)
                rcopy(src, dst, rs_s.at[0, g], rs_r.at[e, g], (r, xn(1))).start()
                rcopy(src, dst, rs_s.at[1, g], rs_r.at[e, g], (r, xn(3))).start()

    def slab(h, q):
        return cols.at[h, pl.ds(q * 64, 64), :]

    for h in range(2):
        nb = zn if h == 0 else yn
        for cc in range(4):
            piece = sc_dst(h, r, cc)
            pltpu.make_async_copy(piece, piece, rsem_sc.at[h * 4 + cc]).wait()
        for d in (1, 3, 2):
            rcopy(slab(h, r), slab(h, r), s1s.at[h, d], s1r.at[h, d], (nb(d), c)).start()

    def line(h, p, o):
        if h == 0:
            return slab(0, ((y + p) % 4) * 4 + (z + 4 - o) % 4)
        return slab(1, ((y + 4 - o) % 4) * 4 + (z + p) % 4)

    def spread(h, o):
        sl = line(h, 0, o)
        if o:
            rcopy(sl, sl, s1s.at[h, o], s1r.at[h, o], part).wait_recv()
        nb2 = yn if h == 0 else zn
        for dirn in ((0, 1) if o in UP else (1, 0)):
            dev = (nb2(3 if dirn else 1), c)
            rcopy(sl, sl, s2s.at[h, dirn, o], s2r.at[h, dirn, o], dev).start()

    def near_rows(g):
        for e in range(2):
            item = chunk(2 * e + k, g)

            @pl.when((x == (e + 1) % 4) | (x == (e + 3) % 4))
            def _():
                rcopy(item, item, rs_s.at[2, g], rs_r.at[e, g], part).wait_recv()

            @pl.when(x == 3 - e)
            def _():
                rcopy(item, item, rs_s.at[2, g], rs_r.at[e, g], (r, (2 + e) * 2 + k)).start()

            @pl.when((x == (e + 1) % 4) | (x == (e + 3) % 4))
            def _():
                rcopy(item, item, pt_s.at[e, g], pt_r.at[e, g], part).start()

    def far_rows(g):
        for e in range(2):
            item = chunk(2 * e + k, g)

            @pl.when(x == 2 + e)
            def _():
                rcopy(item, item, rs_s.at[2, g], rs_r.at[e, g], part).wait_recv()
                rcopy(item, item, pt_s.at[e, g], pt_r.at[e, g], part).start()

    @pl.when(c < 4)
    def _():
        pltpu.make_async_copy(own, rowcol(c), lsem).wait()
        for g in range(4):
            item = chunk(c, g)
            for e in range(2):
                @pl.when(x == e)
                def _():
                    rcopy(item, item, pt_s.at[e, g], pt_r.at[e, g], part).start()

    for h in range(2):
        spread(h, 0)
    near_rows(0)
    near_rows(1)
    for g, o in ((2, 1), (3, 3), (None, 2)):
        for h in range(2):
            spread(h, o)
        if g is not None:
            near_rows(g)
    for i in range(2):
        for h in range(2):
            nb2 = yn if h == 0 else zn
            o = UP[i]
            sl = line(h, 3, o)
            rcopy(sl, sl, s2s.at[h, 0, o], s2r.at[h, 0, o], part).wait_recv()
            rcopy(sl, sl, fs.at[h, 0, i], fr.at[h, 0, i], (nb2(1), c)).start()
            o = DOWN[i]
            sl = line(h, 1, o)
            rcopy(sl, sl, s2s.at[h, 1, o], s2r.at[h, 1, o], part).wait_recv()
            rcopy(sl, sl, fs.at[h, 1, i], fr.at[h, 1, i], (nb2(3), c)).start()
        far_rows(2 * i)
        far_rows(2 * i + 1)
    for h in range(2):
        for i in range(2):
            sl = line(h, 3, DOWN[i])
            rcopy(sl, sl, s2s.at[h, 0, DOWN[i]], s2r.at[h, 0, DOWN[i]], part).wait_recv()
            sl = line(h, 1, UP[i])
            rcopy(sl, sl, s2s.at[h, 1, UP[i]], s2r.at[h, 1, UP[i]], part).wait_recv()
            sl = line(h, 2, UP[i])
            rcopy(sl, sl, fs.at[h, 0, i], fr.at[h, 0, i], part).wait_recv()
            sl = line(h, 2, DOWN[i])
            rcopy(sl, sl, fs.at[h, 1, i], fr.at[h, 1, i], part).wait_recv()
    for e in range(2):
        for g in range(4):
            item = chunk(2 * e + 1 - k, g)
            rcopy(item, item, pt_s.at[e, g], pt_r.at[e, g], part).wait_recv()
    sl = slab(0, r)
    for h in range(2):
        for d in (1, 2, 3):
            rcopy(sl, sl, s1s.at[h, d], s1r.at[h, d], part).wait_send()
        for dirn in range(2):
            for j in range(4):
                rcopy(sl, sl, s2s.at[h, dirn, j], s2r.at[h, dirn, j], part).wait_send()
            for i in range(2):
                rcopy(sl, sl, fs.at[h, dirn, i], fr.at[h, dirn, i], part).wait_send()
    for g in range(4):
        item = chunk(k, g)
        for e in range(2):
            rcopy(item, item, pt_s.at[e, g], pt_r.at[e, g], part).wait_send()

        @pl.when(x < 2)
        def _():
            rcopy(item, item, rs_s.at[0, g], rs_r.at[0, g], part).wait_send()
            rcopy(item, item, rs_s.at[1, g], rs_r.at[0, g], part).wait_send()

        @pl.when(x >= 2)
        def _():
            rcopy(item, item, rs_s.at[2, g], rs_r.at[0, g], part).wait_send()

    @pl.when(c < 4)
    def _():
        for q in range(16):
            @pl.when(jnp.logical_not((tc == c) & (r == q)))
            def _():
                src, dst, rsem = sc_copy(q)
                rcopy(src, dst, ssem_sc.at[q], rsem, part).wait_send()


def panel(asm):
    dma = pltpu.SemaphoreType.DMA
    return pl.pallas_call(
        panel_kernel,
        out_shape=(
            jax.ShapeDtypeStruct((8, T, 512), jnp.float32),
            jax.ShapeDtypeStruct((2, 1024, 512), jnp.float32),
        ),
        in_specs=[spec(ANY)],
        out_specs=(spec(ANY), spec(ANY)),
        scratch_shapes=[
            dma(()),
            dma((16,)),
            dma((8,)),
            dma((2, 4)),
            dma((2, 4)),
            dma((2, 2, 4)),
            dma((2, 2, 4)),
            dma((2, 2, 2)),
            dma((2, 2, 2)),
            dma((3, 4)),
            dma((2, 4)),
            dma((2, 4)),
            dma((2, 4)),
        ],
        compiler_params=pltpu.CompilerParams(collective_id=1, has_side_effects=True, vmem_limit_bytes=VLIM),
        cost_estimate=pl.CostEstimate(flops=0, bytes_accessed=1 << 26, transcendentals=0),
        name="panel",
    )(asm)


def schur_kernel(
    pat, slots, rows, cols, pa, pb, pc, front, phi, plo, thi, tlo, q_ref, out,
    yext, cext, xh, xl, qbuf, acc, buf, todo, where, fsem, rsem,
):
    r = lax.axis_index("prow")
    c = lax.axis_index("pcol")
    s = pl.program_id(0)
    f32 = jnp.float32

    def masks(i):
        e0 = pat[0, i].astype(f32)
        e1 = jnp.maximum(pat[0, i], pat[1, i]).astype(f32)
        return e0, e1

    def mm(a, b):
        return jnp.dot(a, b, preferred_element_type=f32)

    def masked(x, e):
        return jnp.concatenate([x[:, :256] * e[0], x[:, 256:] * e[1]], axis=1)

    def front_copy(g):
        at = pl.ds(g * 16, 16)
        return pltpu.make_async_copy(front.at[at], acc.at[at], fsem.at[g])

    @pl.when(s == 0)
    def _():
        for g in range(8):
            front_copy(g).start()
        count = fetch_children(slots, pa, pb, pc, buf, todo, where, rsem, False)
        off = pl.multiple_of(jnp.minimum(c, 3) * T, T)
        for a in range(8):
            hi, lo = split(masked(rows[a], masks(a * 16 + r)))
            xh[a * T : (a + 1) * T, :] = hi
            xl[a * T : (a + 1) * T, :] = lo
        y = mm(xh[...], phi[...]) + mm(xl[...], phi[...]) + mm(xh[...], plo[...])
        yh, yl = split(y)
        yext[:, 0:512] = yh
        yext[:, 512:1024] = yh
        yext[:, 1024:1536] = yl

        @pl.when(c < 4)
        def _():
            th = thi[:, pl.ds(off, T)]
            qbuf[...] = mm(xh[...], th) + mm(xl[...], th) + mm(xh[...], tlo[:, pl.ds(off, T)])

        @pl.when((c < 4) & (r < 4))
        def _():
            qbuf[0:T, :] = q_ref[pl.ds(pl.multiple_of(jnp.minimum(r, 3) * T, T), T), pl.ds(off, T)]

        for g in range(8):
            front_copy(g).wait()
        add_children(count, front, acc, buf, todo, where, rsem)

    for h in range(2):
        hi, lo = split(masked(cols[h], masks(s * 16 + h * 8 + c)))
        cext[h * T : (h + 1) * T, 0:512] = hi
        cext[h * T : (h + 1) * T, 512:1024] = lo
        cext[h * T : (h + 1) * T, 1024:1536] = hi
    upd = lax.dot_general(yext[...], cext[...], (((1,), (1,)), ((), ())), preferred_element_type=f32)
    for a in range(8):
        for h in range(2):
            val = acc[a * 16 + 2 * s + h] - upd[a * T : (a + 1) * T, h * T : (h + 1) * T]
            if a == 0:
                val = jnp.where(r < 4, 0.0, val)
            out[a, 0, h, 0] = val

    @pl.when((s == 0) & (c < 4))
    def _():
        for a in range(8):
            out[a, 0, 0, 0] = qbuf[a * T : (a + 1) * T, :]


def schur(pattern, slots, rows, cols, pa, pb, pc, front, phi, plo, thi, tlo, qlead):
    full = lambda *shape: pl.BlockSpec(shape, lambda s: (0,) * len(shape))
    blk = pl.BlockSpec((8, 1, 2, 1, T, T), lambda s: (0, 0, s, 0, 0, 0))
    return pl.pallas_call(
        schur_kernel,
        grid=(8,),
        out_shape=jax.ShapeDtypeStruct((8, 1, 16, 1, T, T), jnp.float32),
        in_specs=[
            spec(pltpu.SMEM),
            spec(pltpu.SMEM),
            full(8, T, 512),
            pl.BlockSpec((2, T, 512), lambda s: (0, s, 0)),
            spec(ANY),
            spec(ANY),
            spec(ANY),
            spec(ANY),
            full(512, 512),
            full(512, 512),
            full(512, 512),
            full(512, 512),
            full(512, 512),
        ],
        out_specs=blk,
        scratch_shapes=[
            pltpu.VMEM((1024, 1536), jnp.bfloat16),
            pltpu.VMEM((256, 1536), jnp.bfloat16),
            pltpu.VMEM((1024, 512), jnp.bfloat16),
            pltpu.VMEM((1024, 512), jnp.bfloat16),
            pltpu.VMEM((1024, T), jnp.float32),
            pltpu.VMEM((128, T, T), jnp.float32),
        ]
        + CHILD_SCRATCH,
        compiler_params=pltpu.CompilerParams(vmem_limit_bytes=VLIM),
        cost_estimate=pl.CostEstimate(flops=7 << 30, bytes_accessed=6 << 22, transcendentals=0),
        name="schur",
    )(pattern, slots, rows, cols, pa, pb, pc, front, phi, plo, thi, tlo, qlead)


def local(front, child_blocks, owners, slots, pattern):
    send, meta = pack(owners[:, 0], slots, child_blocks)
    blocks = front.reshape(128, T, T)
    pa, pb, pc, got, qlead, thi, tlo, phi, plo = exchange(pattern, meta, send, blocks)
    rows, cols = panel(assemble_panel(got, pa, pb, pc, blocks))
    return schur(pattern, got, rows, cols, pa, pb, pc, blocks, phi, plo, thi, tlo, qlead)


def solution(mesh):
    placed = (
        P(None, "prow", None, "pcol", None, None),
        P(("prow", "pcol"), None, None),
        P(("prow", "pcol"), None),
        P(("prow", "pcol")),
        P(),
    )
    return jax.shard_map(
        local,
        mesh=mesh,
        in_specs=placed,
        out_specs=P(None, "prow", None, "pcol", None, None),
        check_vma=False,
    )
```

```python
import jax
import jax.numpy as jnp
from jax import lax
from jax.experimental import pallas as pl
from jax.experimental.pallas import tpu as pltpu
from jax.sharding import PartitionSpec as P

T = 128
MESH = pl.DeviceIdType.MESH
ANY = pl.ANY
VLIM = 60000 * 1024
HI = lax.Precision.HIGHEST


def spec(space):
    return pl.BlockSpec(memory_space=space)


def pack_kernel(owners, owners_v, slots_v, child, send, meta, buf, cnt, dest, isem, osem):
    for g in range(8):
        pltpu.make_async_copy(child.at[pl.ds(g * 16, 16)], buf.at[pl.ds(g * 16, 16)], isem.at[g]).start()
    meta[...] = owners_v[...] * 128 + slots_v[...]

    def zero(i, _):
        cnt[i] = 0
        return 0

    lax.fori_loop(0, 128, zero, 0, unroll=8)

    def place(i, _):
        o = owners[i]
        k = cnt[o]
        cnt[o] = k + 1
        dest[i] = o * 2 + k
        return 0

    lax.fori_loop(0, 128, place, 0, unroll=4)
    for g in range(8):
        pltpu.make_async_copy(child.at[pl.ds(g * 16, 16)], buf.at[pl.ds(g * 16, 16)], isem.at[g]).wait()

        def put(i, _):
            d = dest[i]
            rows = pl.ds(pl.multiple_of((d & 1) * T, T), T)
            dst = send.at[d >> 6, (d >> 4) & 3, (d >> 1) & 7, rows]
            pltpu.make_async_copy(buf.at[i], dst, osem.at[i]).start()
            return 0

        lax.fori_loop(g * 16, g * 16 + 16, put, 0, unroll=4)

    def fin(i, _):
        pltpu.make_async_copy(buf.at[i], send.at[0, 0, 0, pl.ds(0, T)], osem.at[i]).wait()
        return 0

    lax.fori_loop(0, 128, fin, 0, unroll=8)


def pack(owners, slots, child):
    return pl.pallas_call(
        pack_kernel,
        out_shape=(
            jax.ShapeDtypeStruct((4, 4, 8, 256, T), jnp.float32),
            jax.ShapeDtypeStruct((1, 128), jnp.int32),
        ),
        in_specs=[spec(pltpu.SMEM), spec(pltpu.VMEM), spec(pltpu.VMEM), spec(ANY)],
        out_specs=(spec(ANY), spec(pltpu.VMEM)),
        scratch_shapes=[
            pltpu.VMEM((128, T, T), jnp.float32),
            pltpu.SMEM((128,), jnp.int32),
            pltpu.SMEM((128,), jnp.int32),
            pltpu.SemaphoreType.DMA((8,)),
            pltpu.SemaphoreType.DMA((128,)),
        ],
        compiler_params=pltpu.CompilerParams(vmem_limit_bytes=VLIM),
        cost_estimate=pl.CostEstimate(flops=0, bytes_accessed=2 << 23, transcendentals=0),
        name="pack",
    )(owners, owners.reshape(1, 128), slots.reshape(1, 128), child)


def piece_copies(pa, pb, pc, buf, rsem, i, h):
    y, z, c = i >> 6, (i >> 4) & 3, (i >> 1) & 7
    a, b, d = pa.at[z, y, c], pb.at[c, z, y], pc.at[y, c, z]
    if h == 0:
        return (
            pltpu.make_async_copy(a, buf.at[i, pl.ds(0, 88)], rsem.at[i]),
            pltpu.make_async_copy(b.at[pl.ds(0, 40)], buf.at[i, pl.ds(88, 40)], rsem.at[i]),
        )
    return (
        pltpu.make_async_copy(b.at[pl.ds(40, 48)], buf.at[i, pl.ds(0, 48)], rsem.at[i]),
        pltpu.make_async_copy(d, buf.at[i, pl.ds(48, 80)], rsem.at[i]),
    )


def fetch_children(slots, pa, pb, pc, buf, todo, where, rsem, only_panel):
    def live(slot):
        return ((slot != 0) & ((slot & 15) == 0)) if only_panel else (slot != 0)

    def get(n, count):
        pair = (slots[0, n], slots[1, n])
        counts = (count, count + live(pair[0]).astype(jnp.int32))

        def start():
            for h in range(2):
                @pl.when(live(pair[h]))
                def _():
                    i = 2 * n + h
                    for cp in piece_copies(pa, pb, pc, buf, rsem, i, h):
                        cp.start()
                    todo[counts[h]] = i
                    where[counts[h]] = (pair[h] >> 4) if only_panel else pair[h]

        if only_panel:
            pl.when(live(pair[0]) | live(pair[1]))(start)
        else:
            start()
        return counts[1] + live(pair[1]).astype(jnp.int32)

    return lax.fori_loop(0, 128, get, 0, unroll=4 if only_panel else 2)


def add_children(count, front, acc, buf, todo, where, rsem):
    def add(m, _):
        i = todo[m]
        s = where[m]
        pltpu.make_async_copy(front.at[0], buf.at[i], rsem.at[i]).wait()
        acc[s] = acc[s] + buf[i]
        return 0

    lax.fori_loop(0, count, add, 0)


CHILD_SCRATCH = [
    pltpu.VMEM((256, T, T), jnp.float32),
    pltpu.SMEM((256,), jnp.int32),
    pltpu.SMEM((256,), jnp.int32),
    pltpu.SemaphoreType.DMA((8,)),
    pltpu.SemaphoreType.DMA((256,)),
]


def assemble_kernel(slots, pa, pb, pc, front, acc, buf, todo, where, fsem, rsem):
    for a in range(8):
        pltpu.make_async_copy(front.at[a * 16], acc.at[a], fsem.at[a]).start()
    count = fetch_children(slots, pa, pb, pc, buf, todo, where, rsem, True)
    for a in range(8):
        pltpu.make_async_copy(front.at[a * 16], acc.at[a], fsem.at[a]).wait()
    add_children(count, front, acc, buf, todo, where, rsem)


def assemble_panel(slots, pa, pb, pc, front):
    return pl.pallas_call(
        assemble_kernel,
        out_shape=jax.ShapeDtypeStruct((8, T, T), jnp.float32),
        in_specs=[spec(pltpu.SMEM)] + [spec(ANY)] * 4,
        out_specs=spec(pltpu.VMEM),
        scratch_shapes=CHILD_SCRATCH,
        compiler_params=pltpu.CompilerParams(vmem_limit_bytes=VLIM),
        cost_estimate=pl.CostEstimate(flops=0, bytes_accessed=1 << 20, transcendentals=0),
        name="assemble_panel",
    )(slots, pa, pb, pc, front)


def dot(a, b, ta=0, tb=0):
    dims = (((0 if ta else 1,), (1 if tb else 0,)), ((), ()))
    return lax.dot_general(a, b, dims, precision=HI, preferred_element_type=jnp.float32)


def split(x):
    hi = x.astype(jnp.bfloat16)
    lo = (x - hi.astype(jnp.float32)).astype(jnp.bfloat16)
    return hi, lo


def eliminate(a_ref, b_ref, u_ref, w_ref):
    lane = lax.broadcasted_iota(jnp.int32, (T, T), 1)
    sub = lax.broadcasted_iota(jnp.int32, (T, T), 0)
    lane1 = lax.broadcasted_iota(jnp.int32, (1, T), 1)
    sub1 = lax.broadcasted_iota(jnp.int32, (T, 1), 0)
    b_ref[...] = (lane == sub).astype(jnp.float32)

    def step(k, _):
        row = a_ref[pl.ds(k, 1), :]
        brow = b_ref[pl.ds(k, 1), :]
        mat = a_ref[...]
        d = jnp.sum(jnp.where(lane1 == k, row, 0.0), axis=1, keepdims=True)
        col = jnp.sum(jnp.where(lane == k, mat, 0.0), axis=1, keepdims=True)
        rs = 1.0 / jnp.sqrt(d)
        m = jnp.where(sub1 > k, col * (1.0 / d), 0.0)
        u_ref[pl.ds(k, 1), :] = jnp.where(lane1 >= k, row * rs, 0.0)
        w_ref[pl.ds(k, 1), :] = brow * rs
        a_ref[...] = mat - m * row
        b_ref[...] = b_ref[...] - m * brow
        return 0

    lax.fori_loop(0, T, step, 0)
    return u_ref[...].T, w_ref[...]


def sym_lower(x):
    lane = lax.broadcasted_iota(jnp.int32, (T, T), 1)
    sub = lax.broadcasted_iota(jnp.int32, (T, T), 0)
    return jnp.where(sub >= lane, x, x.T)


def factor256(g00, g10, g11, a_ref, b_ref, u_ref, w_ref, hook):
    a_ref[...] = sym_lower(g00)
    l00, w00 = eliminate(a_ref, b_ref, u_ref, w_ref)
    hook()
    l10 = dot(g10, w00, tb=1)
    a_ref[...] = sym_lower(g11 - dot(l10, l10, tb=1))
    l11, w11 = eliminate(a_ref, b_ref, u_ref, w_ref)
    hook()
    w10 = -dot(w11, dot(l10, w00))
    zero = jnp.zeros((T, T), jnp.float32)
    low = jnp.concatenate([jnp.concatenate([l00, zero], 1), jnp.concatenate([l10, l11], 1)], 0)
    inv = jnp.concatenate([jnp.concatenate([w00, zero], 1), jnp.concatenate([w10, w11], 1)], 0)
    return low, inv


def lead_factor(pat, blk, q_ref, thi, tlo, phi, plo, a_ref, b_ref, u_ref, w_ref, hook):
    low0, inv0 = factor256(blk(0, 0), blk(1, 0), blk(1, 1), a_ref, b_ref, u_ref, w_ref, hook)
    rect = jnp.concatenate(
        [jnp.concatenate([blk(2, 0), blk(2, 1)], 1), jnp.concatenate([blk(3, 0), blk(3, 1)], 1)], 0
    )
    s = dot(rect, inv0, tb=1)
    e2 = pat[0, 2].astype(jnp.float32)
    e3 = pat[0, 3].astype(jnp.float32)
    s = jnp.concatenate([s[:T] * e2, s[T:] * e3], 0)
    ss = dot(s, s, tb=1)
    low1, inv1 = factor256(
        blk(2, 2) - ss[:T, :T], blk(3, 2) - ss[T:, :T], blk(3, 3) - ss[T:, T:], a_ref, b_ref, u_ref, w_ref, hook
    )
    zero = jnp.zeros((256, 256), jnp.float32)
    q_ref[0:256, 0:256] = low0
    q_ref[0:256, 256:512] = zero
    q_ref[256:512, 0:256] = s
    q_ref[256:512, 256:512] = low1
    t01 = -dot(inv0, dot(s, inv1, ta=1, tb=1), ta=1)
    t = jnp.concatenate(
        [jnp.concatenate([inv0.T, t01], 1), jnp.concatenate([zero, inv1.T], 1)], 0
    )
    p = dot(t, t, tb=1)
    hi, lo = split(t)
    thi[...] = hi
    tlo[...] = lo
    hi, lo = split(p)
    phi[...] = hi
    plo[...] = lo


PARTS = (("c", "y", "z"), ("y", "z", "c"), ("z", "c", "y"))
NEAR = {"c": (2, 3, 6, 7, 1), "y": (1, 3), "z": (1, 3)}
FAR = {"c": (4, 5), "y": (2,), "z": (2,)}
SIZE = {"c": 8, "y": 4, "z": 4}
ROWS = (88, 88, 80)


def exchange_kernel(
    pat, meta, send, front, oa, ob, oc, slots, q_ref, thi, tlo, phi, plo,
    ba1, bb1, bc1, ba2, bb2, bc2,
    lead, meta_all, a_ref, b_ref, u_ref, w_ref,
    m0, ms, mr, f1s, f1r, f2s, f2r, f3s, f3r, l0, l1s, l1r, l2s, l2r, l4s, l4r, l5s, l5r,
):
    r = lax.axis_index("prow")
    c = lax.axis_index("pcol")
    y, z, x, k = r // 4, r % 4, c // 2, c % 2
    me = r * 8 + c
    part = (r, x * 2 + 1 - k)
    b1, b2, b3 = (ba1, bb1, bc1), (ba2, bb2, bc2), (oa, ob, oc)
    own = {"y": y, "z": z, "c": c}
    bar = pltpu.get_barrier_semaphore()

    def rcopy(src, dst, s_sem, r_sem, dev):
        return pltpu.make_async_remote_copy(
            src_ref=src, dst_ref=dst, send_sem=s_sem, recv_sem=r_sem, device_id=dev, device_id_type=MESH
        )

    def plus(ax, o):
        if ax == "c":
            return ((x + o // 2) % 4) * 2 + (k + o) % 2
        return (own[ax] + o) % 4

    def minus(ax, o):
        if ax == "c":
            return ((x + 4 - o // 2) % 4) * 2 + (k + o) % 2
        return (own[ax] + 4 - o) % 4

    def dev(ax, v):
        return {"c": (r, v), "y": (v * 4 + z, c), "z": (y * 4 + v, c)}[ax]

    for ax in ("c", "y", "z"):
        for o in NEAR[ax] + FAR[ax]:
            pl.semaphore_signal(bar, inc=1, device_id=dev(ax, plus(ax, o)), device_id_type=MESH)
    pl.semaphore_wait(bar, 13)

    def src1(n, v):
        return (
            lambda: send.at[:, :, v, pl.ds(0, 88)],
            lambda: send.at[v, :, :, pl.ds(88, 88)],
            lambda: send.at[:, v, :, pl.ds(176, 80)],
        )[n]()

    def src2(n, i, v):
        return b1[n].at[i, :, v] if n == 2 else b1[n].at[i, v]

    def src3(n, j, v):
        return b2[n].at[j, :, v]

    def first(n):
        p = PARTS[n][0]
        for o in NEAR[p] + FAR[p]:
            v = plus(p, o)
            rcopy(src1(n, v), b1[n].at[own[p]], f1s.at[n, o], f1r.at[n, own[p]], dev(p, v)).start()

    def first_own(n):
        p = PARTS[n][0]
        pltpu.make_async_copy(src1(n, own[p]), b1[n].at[own[p]], f1r.at[n, own[p]]).start()

    def second(n, i):
        q = PARTS[n][1]
        piece = b1[n].at[i]
        pltpu.make_async_copy(piece, piece, f1r.at[n, i]).wait()
        for o in NEAR[q] + FAR[q]:
            v = plus(q, o)
            rcopy(src2(n, i, v), b2[n].at[own[q], i], f2s.at[n, i, o], f2r.at[n, own[q], i], dev(q, v)).start()
        pltpu.make_async_copy(src2(n, i, own[q]), b2[n].at[own[q], i], f2r.at[n, own[q], i]).start()

    def third(n, j):
        p, q, u = PARTS[n]
        for i in range(SIZE[p]):
            piece = b2[n].at[j, i]
            pltpu.make_async_copy(piece, piece, f2r.at[n, j, i]).wait()
        for o in NEAR[u] + FAR[u]:
            v = plus(u, o)
            rcopy(src3(n, j, v), b3[n].at[own[u], j], f3s.at[n, j, o], f3r.at[n, own[u], j], dev(u, v)).start()
        pltpu.make_async_copy(src3(n, j, own[u]), b3[n].at[own[u], j], f3r.at[n, own[u], j]).start()

    def go2(offsets):
        for n in range(3):
            p = PARTS[n][0]
            for o in offsets[p]:
                second(n, minus(p, o))

    def go3(offsets):
        for n in range(3):
            q = PARTS[n][1]
            for o in offsets[q]:
                third(n, minus(q, o))

    def cset(j):
        return lead.at[j, pl.ds(j, 4 - j)]

    for j in range(4):
        @pl.when((y == 0) & (c == j) & (z >= j))
        def _():
            cp = pltpu.make_async_copy(front.at[0], lead.at[j, z], l0)
            cp.start()
            cp.wait()
            for d in (1, 2, 3):
                rcopy(lead.at[j, z], lead.at[j, z], l1s.at[d], l1r.at[z], ((z + d) % 4, c)).start()

    mcopy = pltpu.make_async_copy(meta, meta_all.at[r, pl.ds(c, 1), :], m0)
    mcopy.start()
    mcopy.wait()

    def told(stage, v):
        return (
            lambda: meta_all.at[r, pl.ds(v, 1), :],
            lambda: meta_all.at[y * 4 + v],
            lambda: meta_all.at[pl.ds(v * 4, 4)],
        )[stage]()

    def tell(stage):
        ax = "czy"[stage]
        for o in NEAR[ax] + FAR[ax]:
            row = told(stage, own[ax])
            rcopy(row, row, ms.at[stage, o], mr.at[stage, own[ax]], dev(ax, plus(ax, o))).start()

    def hear(stage):
        ax = "czy"[stage]
        for o in NEAR[ax] + FAR[ax]:
            v = minus(ax, o)
            row = told(stage, v)
            rcopy(row, row, ms.at[stage, o], mr.at[stage, v], part).wait_recv()

    tell(0)
    first(2)
    first(1)

    @pl.when(y != 0)
    def _():
        first(0)

    for n in range(3):
        first_own(n)
    for j in range(4):
        e = j // 2

        @pl.when((y == 0) & (c == j))
        def _():
            for i in range(j, 4):
                @pl.when(z != i)
                def _():
                    rcopy(lead.at[j, i], lead.at[j, i], l1s.at[0], l1r.at[i], part).wait_recv()

            rcopy(cset(j), cset(j), l2s.at[0], l2r.at[e], (r, ((x + 1) % 4) * 2 + k)).start()
            rcopy(cset(j), cset(j), l2s.at[1], l2r.at[e], (r, ((x + 3) % 4) * 2 + k)).start()

    for j in range(4):
        e = j // 2

        @pl.when((y == 0) & (k == j % 2) & ((x == (e + 1) % 4) | (x == (e + 3) % 4)))
        def _():
            rcopy(cset(j), cset(j), l2s.at[2], l2r.at[e], part).wait_recv()

        @pl.when((y == 0) & (k == j % 2) & (x == 3 - e))
        def _():
            rcopy(cset(j), cset(j), l2s.at[2], l2r.at[e], (r, (2 + e) * 2 + k)).start()

    @pl.when(y == 0)
    def _():
        first(0)

    for j in range(4):
        e = j // 2

        @pl.when((y == 0) & (k == j % 2) & (x == 2 + e))
        def _():
            rcopy(cset(j), cset(j), l2s.at[2], l2r.at[e], part).wait_recv()

        @pl.when((y == 0) & (k == j % 2))
        def _():
            for d in (1, 3, 2):
                rcopy(cset(j), cset(j), l4s.at[e, d], l4r.at[e], (d * 4 + z, c)).start()

    hear(0)
    tell(1)
    for n in range(3):
        second(n, own[PARTS[n][0]])
    go2(NEAR)
    hear(1)
    tell(2)
    go2(FAR)
    go3({"c": (0,), "y": (0,), "z": (0,)})
    for j in range(4):
        e = j // 2

        @pl.when((y != 0) & (k == j % 2))
        def _():
            rcopy(cset(j), cset(j), l4s.at[e, 0], l4r.at[e], part).wait_recv()

        @pl.when(k == j % 2)
        def _():
            rcopy(cset(j), cset(j), l5s.at[e], l5r.at[e], part).start()

    hear(2)
    mt = jnp.concatenate([meta_all[i] for i in range(16)], axis=0).astype(jnp.float32).T
    whose = jnp.floor(mt * (1.0 / 128.0))
    sl = mt - whose * 128.0
    idx = lax.broadcasted_iota(jnp.int32, (128, 128), 0).astype(jnp.float32)
    mine = whose == me.astype(jnp.float32)
    low = jnp.min(jnp.where(mine, idx, 999.0), axis=0, keepdims=True)
    high = jnp.max(jnp.where(mine, idx, -1.0), axis=0, keepdims=True)
    s0 = jnp.sum(jnp.where(mine & (idx == low), sl, 0.0), axis=0, keepdims=True)
    s1 = jnp.sum(jnp.where(mine & (idx == high) & (idx > low), sl, 0.0), axis=0, keepdims=True)
    slots[0:1, :] = s0.astype(jnp.int32)
    slots[1:2, :] = s1.astype(jnp.int32)
    for j in range(4):
        e = j // 2

        @pl.when(k != j % 2)
        def _():
            rcopy(cset(j), cset(j), l5s.at[e], l5r.at[e], part).wait_recv()

    work = [lambda: (go3(NEAR), go3(FAR))]

    def hook():
        if work:
            work.pop(0)()

    lead_factor(
        pat, lambda i, j: lead[j, i], q_ref, thi, tlo, phi, plo, a_ref, b_ref, u_ref, w_ref, hook
    )
    while work:
        hook()
    for n in range(3):
        p, q, u = PARTS[n]

        def arrived(j, _):
            for v in range(SIZE[u]):
                piece = b3[n].at[v, j]
                pltpu.make_async_copy(piece, piece, f3r.at[n, v, j]).wait()
            for o in NEAR[u] + FAR[u]:
                rcopy(src3(n, 0, 0), b3[n].at[0, 0], f3s.at[n, j, o], f3r.at[n, 0, 0], part).wait_send()
            return 0

        lax.fori_loop(0, SIZE[q], arrived, 0)
        for o in NEAR[p] + FAR[p]:
            rcopy(src1(n, 0), b1[n].at[0], f1s.at[n, o], f1r.at[n, 0], part).wait_send()

        def sent(i, _):
            for o in NEAR[q] + FAR[q]:
                rcopy(src2(n, 0, 0), b2[n].at[0, 0], f2s.at[n, i, o], f2r.at[n, 0, 0], part).wait_send()
            return 0

        lax.fori_loop(0, SIZE[p], sent, 0)

    for stage in range(3):
        ax = "czy"[stage]
        for o in NEAR[ax] + FAR[ax]:
            row = told(stage, own[ax])
            rcopy(row, row, ms.at[stage, o], mr.at[stage, 0], part).wait_send()
    for j in range(4):
        e = j // 2

        @pl.when((y == 0) & (c == j))
        def _():
            @pl.when(z >= j)
            def _():
                for d in (1, 2, 3):
                    rcopy(lead.at[j, 0], lead.at[j, 0], l1s.at[d], l1r.at[0], part).wait_send()

            rcopy(cset(j), cset(j), l2s.at[0], l2r.at[e], part).wait_send()
            rcopy(cset(j), cset(j), l2s.at[1], l2r.at[e], part).wait_send()

        @pl.when((y == 0) & (k == j % 2) & (x == 3 - e))
        def _():
            rcopy(cset(j), cset(j), l2s.at[2], l2r.at[e], part).wait_send()

        @pl.when((y == 0) & (k == j % 2))
        def _():
            for d in (1, 3, 2):
                rcopy(cset(j), cset(j), l4s.at[e, d], l4r.at[e], part).wait_send()

        @pl.when(k == j % 2)
        def _():
            rcopy(cset(j), cset(j), l5s.at[e], l5r.at[e], part).wait_send()


def exchange(pattern, meta, send, front):
    vm = spec(pltpu.VMEM)
    dma = pltpu.SemaphoreType.DMA
    bf = jax.ShapeDtypeStruct((512, 512), jnp.bfloat16)

    def buf(kind, a, b, d, n):
        return kind((a, b, d, ROWS[n], T), jnp.float32)

    return pl.pallas_call(
        exchange_kernel,
        out_shape=(
            buf(jax.ShapeDtypeStruct, 4, 4, 8, 0),
            buf(jax.ShapeDtypeStruct, 8, 4, 4, 1),
            buf(jax.ShapeDtypeStruct, 4, 8, 4, 2),
            jax.ShapeDtypeStruct((8, 128), jnp.int32),
            jax.ShapeDtypeStruct((512, 512), jnp.float32),
            bf, bf, bf, bf,
        ),
        in_specs=[spec(pltpu.SMEM), vm, spec(ANY), spec(ANY)],
        out_specs=(spec(ANY), spec(ANY), spec(ANY), vm, vm, vm, vm, vm, vm),
        scratch_shapes=[
            buf(pltpu.VMEM, 8, 4, 4, 0),
            buf(pltpu.VMEM, 4, 4, 8, 1),
            buf(pltpu.VMEM, 4, 4, 8, 2),
            buf(pltpu.VMEM, 4, 8, 4, 0),
            buf(pltpu.VMEM, 4, 4, 8, 1),
            buf(pltpu.VMEM, 8, 4, 4, 2),
            pltpu.VMEM((4, 4, T, T), jnp.float32),
            pltpu.VMEM((16, 8, 128), jnp.int32),
        ]
        + [pltpu.VMEM((T, T), jnp.float32)] * 4
        + [dma(()), dma((3, 8)), dma((3, 8)), dma((3, 8)), dma((3, 8))]
        + [dma((3, 8, 8))] * 4
        + [dma(()), dma((4,)), dma((4,)), dma((3,)), dma((2,)), dma((2, 4)), dma((2,)), dma((2,)), dma((2,))],
        compiler_params=pltpu.CompilerParams(collective_id=0, has_side_effects=True, vmem_limit_bytes=VLIM),
        name="exchange",
    )(pattern, meta, send, front)


UP, DOWN = (0, 1), (3, 2)


def panel_kernel(asm, rows, cols, lsem, ssem_sc, rsem_sc, s1s, s1r, s2s, s2r, fs, fr, rs_s, rs_r, pt_s, pt_r):
    r = lax.axis_index("prow")
    c = lax.axis_index("pcol")
    y, z, x, k = r // 4, r % 4, c // 2, c % 2
    tc = r % 8
    half = r // 8
    selfhit = (c < 4) & (tc == c)
    bar = pltpu.get_barrier_semaphore()

    def sig(rr, cc):
        pl.semaphore_signal(bar, inc=1, device_id=(rr, cc), device_id_type=MESH)

    def zn(d):
        return y * 4 + (z + d) % 4

    def yn(d):
        return ((y + d) % 4) * 4 + z

    def xn(d):
        return ((x + d) % 4) * 2 + k

    for q in range(16):
        @pl.when((c < 4) & jnp.logical_not((tc == c) & (r == q)))
        def _():
            sig(q, tc)
    for h in range(2):
        for cc in range(4):
            @pl.when(jnp.logical_not((r == c + 8 * h) & (c == cc)))
            def _():
                sig(c + 8 * h, cc)
    for d in (1, 2, 3):
        sig(zn(d), c)
        sig(yn(d), c)
    sig(r, xn(1))
    sig(r, xn(3))
    sig(r, x * 2 + 1 - k)
    n_sc = jnp.where(c < 4, 16, 0) + 8 - jnp.where(selfhit, 2, 0)
    pl.semaphore_wait(bar, n_sc + 9)

    def rcopy(src, dst, ss, rs, dev):
        return pltpu.make_async_remote_copy(
            src_ref=src, dst_ref=dst, send_sem=ss, recv_sem=rs, device_id=dev, device_id_type=MESH
        )

    def sc_dst(h, q, cc):
        return cols.at[h, pl.ds(q * 64, 64), pl.ds(cc * T, T)]

    def sc_copy(q):
        src = asm.at[q // 2, pl.ds((q % 2) * 64, 64), :]
        return src, sc_dst(half, q, c), rsem_sc.at[half * 4 + c]

    own = asm
    part = (r, x * 2 + 1 - k)

    def rowcol(cc):
        return rows.at[:, :, pl.ds(pl.multiple_of(cc * T, T), T)]

    def chunk(cc, g):
        return rows.at[pl.ds(2 * g, 2), :, pl.ds(pl.multiple_of(cc * T, T), T)]

    @pl.when(c < 4)
    def _():
        for q in range(16):
            src, dst, rsem = sc_copy(q)
            hit = (tc == c) & (r == q)

            @pl.when(hit)
            def _():
                pltpu.make_async_copy(src, dst, rsem).start()

            @pl.when(jnp.logical_not(hit))
            def _():
                rcopy(src, dst, ssem_sc.at[q], rsem, (q, tc)).start()

        pltpu.make_async_copy(own, rowcol(c), lsem).start()

    for e in range(2):
        @pl.when(x == e)
        def _():
            for g in range(4):
                src, dst = own.at[pl.ds(2 * g, 2)], chunk(c, g)
                rcopy(src, dst, rs_s.at[0, g], rs_r.at[e, g], (r, xn(1))).start()
                rcopy(src, dst, rs_s.at[1, g], rs_r.at[e, g], (r, xn(3))).start()

    def slab(h, q):
        return cols.at[h, pl.ds(q * 64, 64), :]

    for h in range(2):
        nb = zn if h == 0 else yn
        for cc in range(4):
            piece = sc_dst(h, r, cc)
            pltpu.make_async_copy(piece, piece, rsem_sc.at[h * 4 + cc]).wait()
        for d in (1, 3, 2):
            rcopy(slab(h, r), slab(h, r), s1s.at[h, d], s1r.at[h, d], (nb(d), c)).start()

    def line(h, p, o):
        if h == 0:
            return slab(0, ((y + p) % 4) * 4 + (z + 4 - o) % 4)
        return slab(1, ((y + 4 - o) % 4) * 4 + (z + p) % 4)

    def spread(h, o):
        sl = line(h, 0, o)
        if o:
            rcopy(sl, sl, s1s.at[h, o], s1r.at[h, o], part).wait_recv()
        nb2 = yn if h == 0 else zn
        for dirn in ((0, 1) if o in UP else (1, 0)):
            dev = (nb2(3 if dirn else 1), c)
            rcopy(sl, sl, s2s.at[h, dirn, o], s2r.at[h, dirn, o], dev).start()

    def near_rows(g):
        for e in range(2):
            item = chunk(2 * e + k, g)

            @pl.when((x == (e + 1) % 4) | (x == (e + 3) % 4))
            def _():
                rcopy(item, item, rs_s.at[2, g], rs_r.at[e, g], part).wait_recv()

            @pl.when(x == 3 - e)
            def _():
                rcopy(item, item, rs_s.at[2, g], rs_r.at[e, g], (r, (2 + e) * 2 + k)).start()

            @pl.when((x == (e + 1) % 4) | (x == (e + 3) % 4))
            def _():
                rcopy(item, item, pt_s.at[e, g], pt_r.at[e, g], part).start()

    def far_rows(g):
        for e in range(2):
            item = chunk(2 * e + k, g)

            @pl.when(x == 2 + e)
            def _():
                rcopy(item, item, rs_s.at[2, g], rs_r.at[e, g], part).wait_recv()
                rcopy(item, item, pt_s.at[e, g], pt_r.at[e, g], part).start()

    @pl.when(c < 4)
    def _():
        pltpu.make_async_copy(own, rowcol(c), lsem).wait()
        for g in range(4):
            item = chunk(c, g)
            for e in range(2):
                @pl.when(x == e)
                def _():
                    rcopy(item, item, pt_s.at[e, g], pt_r.at[e, g], part).start()

    for h in range(2):
        spread(h, 0)
    near_rows(0)
    near_rows(1)
    for g, o in ((2, 1), (3, 3), (None, 2)):
        for h in range(2):
            spread(h, o)
        if g is not None:
            near_rows(g)
    for i in range(2):
        for h in range(2):
            nb2 = yn if h == 0 else zn
            o = UP[i]
            sl = line(h, 3, o)
            rcopy(sl, sl, s2s.at[h, 0, o], s2r.at[h, 0, o], part).wait_recv()
            rcopy(sl, sl, fs.at[h, 0, i], fr.at[h, 0, i], (nb2(1), c)).start()
            o = DOWN[i]
            sl = line(h, 1, o)
            rcopy(sl, sl, s2s.at[h, 1, o], s2r.at[h, 1, o], part).wait_recv()
            rcopy(sl, sl, fs.at[h, 1, i], fr.at[h, 1, i], (nb2(3), c)).start()
        far_rows(2 * i)
        far_rows(2 * i + 1)
    for h in range(2):
        for i in range(2):
            sl = line(h, 3, DOWN[i])
            rcopy(sl, sl, s2s.at[h, 0, DOWN[i]], s2r.at[h, 0, DOWN[i]], part).wait_recv()
            sl = line(h, 1, UP[i])
            rcopy(sl, sl, s2s.at[h, 1, UP[i]], s2r.at[h, 1, UP[i]], part).wait_recv()
            sl = line(h, 2, UP[i])
            rcopy(sl, sl, fs.at[h, 0, i], fr.at[h, 0, i], part).wait_recv()
            sl = line(h, 2, DOWN[i])
            rcopy(sl, sl, fs.at[h, 1, i], fr.at[h, 1, i], part).wait_recv()
    for e in range(2):
        for g in range(4):
            item = chunk(2 * e + 1 - k, g)
            rcopy(item, item, pt_s.at[e, g], pt_r.at[e, g], part).wait_recv()
    sl = slab(0, r)
    for h in range(2):
        for d in (1, 2, 3):
            rcopy(sl, sl, s1s.at[h, d], s1r.at[h, d], part).wait_send()
        for dirn in range(2):
            for j in range(4):
                rcopy(sl, sl, s2s.at[h, dirn, j], s2r.at[h, dirn, j], part).wait_send()
            for i in range(2):
                rcopy(sl, sl, fs.at[h, dirn, i], fr.at[h, dirn, i], part).wait_send()
    for g in range(4):
        item = chunk(k, g)
        for e in range(2):
            rcopy(item, item, pt_s.at[e, g], pt_r.at[e, g], part).wait_send()

        @pl.when(x < 2)
        def _():
            rcopy(item, item, rs_s.at[0, g], rs_r.at[0, g], part).wait_send()
            rcopy(item, item, rs_s.at[1, g], rs_r.at[0, g], part).wait_send()

        @pl.when(x >= 2)
        def _():
            rcopy(item, item, rs_s.at[2, g], rs_r.at[0, g], part).wait_send()

    @pl.when(c < 4)
    def _():
        for q in range(16):
            @pl.when(jnp.logical_not((tc == c) & (r == q)))
            def _():
                src, dst, rsem = sc_copy(q)
                rcopy(src, dst, ssem_sc.at[q], rsem, part).wait_send()


def panel(asm):
    dma = pltpu.SemaphoreType.DMA
    return pl.pallas_call(
        panel_kernel,
        out_shape=(
            jax.ShapeDtypeStruct((8, T, 512), jnp.float32),
            jax.ShapeDtypeStruct((2, 1024, 512), jnp.float32),
        ),
        in_specs=[spec(ANY)],
        out_specs=(spec(ANY), spec(ANY)),
        scratch_shapes=[
            dma(()),
            dma((16,)),
            dma((8,)),
            dma((2, 4)),
            dma((2, 4)),
            dma((2, 2, 4)),
            dma((2, 2, 4)),
            dma((2, 2, 2)),
            dma((2, 2, 2)),
            dma((3, 4)),
            dma((2, 4)),
            dma((2, 4)),
            dma((2, 4)),
        ],
        compiler_params=pltpu.CompilerParams(collective_id=1, has_side_effects=True, vmem_limit_bytes=VLIM),
        cost_estimate=pl.CostEstimate(flops=0, bytes_accessed=1 << 26, transcendentals=0),
        name="panel",
    )(asm)


def schur_kernel(
    pat, slots, rows, cols, pa, pb, pc, front, phi, plo, thi, tlo, q_ref, out,
    yext, cext, xh, xl, qbuf, acc, buf, todo, where, fsem, rsem,
):
    r = lax.axis_index("prow")
    c = lax.axis_index("pcol")
    s = pl.program_id(0)
    f32 = jnp.float32

    def masks(i):
        e0 = pat[0, i].astype(f32)
        e1 = jnp.maximum(pat[0, i], pat[1, i]).astype(f32)
        return e0, e1

    def mm(a, b):
        return jnp.dot(a, b, preferred_element_type=f32)

    def masked(x, e):
        return jnp.concatenate([x[:, :256] * e[0], x[:, 256:] * e[1]], axis=1)

    def front_copy(g):
        at = pl.ds(g * 16, 16)
        return pltpu.make_async_copy(front.at[at], acc.at[at], fsem.at[g])

    @pl.when(s == 0)
    def _():
        for g in range(8):
            front_copy(g).start()
        count = fetch_children(slots, pa, pb, pc, buf, todo, where, rsem, False)
        off = pl.multiple_of(jnp.minimum(c, 3) * T, T)
        for a in range(8):
            hi, lo = split(masked(rows[a], masks(a * 16 + r)))
            xh[a * T : (a + 1) * T, :] = hi
            xl[a * T : (a + 1) * T, :] = lo
        y = mm(xh[...], phi[...]) + mm(xl[...], phi[...]) + mm(xh[...], plo[...])
        yh, yl = split(y)
        yext[:, 0:512] = yh
        yext[:, 512:1024] = yh
        yext[:, 1024:1536] = yl

        @pl.when(c < 4)
        def _():
            th = thi[:, pl.ds(off, T)]
            qbuf[...] = mm(xh[...], th) + mm(xl[...], th) + mm(xh[...], tlo[:, pl.ds(off, T)])

        @pl.when((c < 4) & (r < 4))
        def _():
            qbuf[0:T, :] = q_ref[pl.ds(pl.multiple_of(jnp.minimum(r, 3) * T, T), T), pl.ds(off, T)]

        for g in range(8):
            front_copy(g).wait()
        add_children(count, front, acc, buf, todo, where, rsem)

    for h in range(2):
        hi, lo = split(masked(cols[h], masks(s * 16 + h * 8 + c)))
        cext[h * T : (h + 1) * T, 0:512] = hi
        cext[h * T : (h + 1) * T, 512:1024] = lo
        cext[h * T : (h + 1) * T, 1024:1536] = hi
    upd = lax.dot_general(yext[...], cext[...], (((1,), (1,)), ((), ())), preferred_element_type=f32)
    for a in range(8):
        for h in range(2):
            val = acc[a * 16 + 2 * s + h] - upd[a * T : (a + 1) * T, h * T : (h + 1) * T]
            if a == 0:
                val = jnp.where(r < 4, 0.0, val)
            out[a, 0, h, 0] = val

    @pl.when((s == 0) & (c < 4))
    def _():
        for a in range(8):
            out[a, 0, 0, 0] = qbuf[a * T : (a + 1) * T, :]


def schur(pattern, slots, rows, cols, pa, pb, pc, front, phi, plo, thi, tlo, qlead):
    full = lambda *shape: pl.BlockSpec(shape, lambda s: (0,) * len(shape))
    blk = pl.BlockSpec((8, 1, 2, 1, T, T), lambda s: (0, 0, s, 0, 0, 0))
    return pl.pallas_call(
        schur_kernel,
        grid=(8,),
        out_shape=jax.ShapeDtypeStruct((8, 1, 16, 1, T, T), jnp.float32),
        in_specs=[
            spec(pltpu.SMEM),
            spec(pltpu.SMEM),
            full(8, T, 512),
            pl.BlockSpec((2, T, 512), lambda s: (0, s, 0)),
            spec(ANY),
            spec(ANY),
            spec(ANY),
            spec(ANY),
            full(512, 512),
            full(512, 512),
            full(512, 512),
            full(512, 512),
            full(512, 512),
        ],
        out_specs=blk,
        scratch_shapes=[
            pltpu.VMEM((1024, 1536), jnp.bfloat16),
            pltpu.VMEM((256, 1536), jnp.bfloat16),
            pltpu.VMEM((1024, 512), jnp.bfloat16),
            pltpu.VMEM((1024, 512), jnp.bfloat16),
            pltpu.VMEM((1024, T), jnp.float32),
            pltpu.VMEM((128, T, T), jnp.float32),
        ]
        + CHILD_SCRATCH,
        compiler_params=pltpu.CompilerParams(vmem_limit_bytes=VLIM),
        cost_estimate=pl.CostEstimate(flops=7 << 30, bytes_accessed=6 << 22, transcendentals=0),
        name="schur",
    )(pattern, slots, rows, cols, pa, pb, pc, front, phi, plo, thi, tlo, qlead)


def local(front, child_blocks, owners, slots, pattern):
    send, meta = pack(owners[:, 0], slots, child_blocks)
    blocks = front.reshape(128, T, T)
    pa, pb, pc, got, qlead, thi, tlo, phi, plo = exchange(pattern, meta, send, blocks)
    rows, cols = panel(assemble_panel(got, pa, pb, pc, blocks))
    return schur(pattern, got, rows, cols, pa, pb, pc, blocks, phi, plo, thi, tlo, qlead)


def solution(mesh):
    placed = (
        P(None, "prow", None, "pcol", None, None),
        P(("prow", "pcol"), None, None),
        P(("prow", "pcol"), None),
        P(("prow", "pcol")),
        P(),
    )
    return jax.shard_map(
        local,
        mesh=mesh,
        in_specs=placed,
        out_specs=P(None, "prow", None, "pcol", None, None),
        check_vma=False,
    )
```
